32 devices in a mesh: group: 4 (over y, x), ctx: 4 (over z), shard: 2 (over core).
Axes of the slice: x: 2, y: 2, z: 4, core: 2. Of those that a mesh axis runs over, the one named last changes fastest.
Arguments:
- tokens: bfloat16 [8, 2048, 1024], P(('group', 'shard'), 'ctx'), may hold values from -6 to 6
- source: bfloat16 [8, 1024, 1024], P(('group', 'shard'), 'ctx'), may hold values from -6 to 6
- segment_ids: int32 [8, 2048], P(('group', 'shard'), 'ctx'), may hold values from 0 to 8, as said below
- positions: int32 [8, 2048], P(('group', 'shard'), 'ctx'), may hold values from 0 to 1247, as said below
- cotangent: bfloat16 [8, 2048, 1024], P(('group', 'shard'), 'ctx'), may hold values from -6 to 6
- self_gain: bfloat16 [1024], P('shard'), may hold values from 0.5 to 1.5
- self_shift: bfloat16 [1024], P('shard'), may hold values from -1.75 to 1.75
- self_weights: bfloat16 [1024, 3072], P('shard'), may hold values from -0.1875 to 0.1875
- query_bias: bfloat16 [1024], P('shard'), may hold values from -1.75 to 1.75
- value_bias: bfloat16 [1024], P('shard'), may hold values from -0.125 to 0.125
- self_output: bfloat16 [1024, 1024], P('shard'), may hold values from -3 to 3
- output_bias: bfloat16 [1024], P('shard'), may hold values from -1.75 to 1.75
- cross_gain: bfloat16 [1024], P('shard'), may hold values from 0.5 to 1.5
- cross_shift: bfloat16 [1024], P('shard'), may hold values from -1.75 to 1.75
- cross_query: bfloat16 [1024, 1024], P('shard'), may hold values from -0.1875 to 0.1875
- query_offset: bfloat16 [1024], P('shard'), may hold values from -1.75 to 1.75
- cross_memory: bfloat16 [1024, 2048], P('shard'), may hold values from -0.1875 to 0.1875
- memory_offset: bfloat16 [1024], P('shard'), may hold values from -0.125 to 0.125
- cross_output: bfloat16 [1024, 1024], P('shard'), may hold values from -3 to 3
- return_bias: bfloat16 [1024], P('shard'), may hold values from -1.75 to 1.75
- feed_gain: bfloat16 [1024], P('shard'), may hold values from 0.5 to 1.5
- feed_shift: bfloat16 [1024], P('shard'), may hold values from -1.75 to 1.75
- feed_up: bfloat16 [1024, 4096], P('shard'), may hold values from -0.1875 to 0.1875
- up_bias: bfloat16 [4096], P('shard'), may hold values from -1.75 to 1.75
- feed_down: bfloat16 [4096, 1024], P('shard'), may hold values from -0.09375 to 0.09375
- down_bias: bfloat16 [1024], P('shard'), may hold values from -1.75 to 1.75
Outputs:
- block_output: bfloat16 [8, 2048, 1024], P(('group', 'shard'), 'ctx')
- tokens_grad: float32 [8, 2048, 1024], P(('group', 'shard'), 'ctx')
- source_grad: float32 [8, 1024, 1024], P(('group', 'shard'), 'ctx')
- self_gain_grad: float32 [1024], P('shard')
- self_shift_grad: float32 [1024], P('shard')
- self_weights_grad: float32 [1024, 3072], P('shard')
- query_bias_grad: float32 [1024], P('shard')
- value_bias_grad: float32 [1024], P('shard')
- self_output_grad: float32 [1024, 1024], P('shard')
- output_bias_grad: float32 [1024], P('shard')
- cross_gain_grad: float32 [1024], P('shard')
- cross_shift_grad: float32 [1024], P('shard')
- cross_query_grad: float32 [1024, 1024], P('shard')
- query_offset_grad: float32 [1024], P('shard')
- cross_memory_grad: float32 [1024, 2048], P('shard')
- memory_offset_grad: float32 [1024], P('shard')
- cross_output_grad: float32 [1024, 1024], P('shard')
- return_bias_grad: float32 [1024], P('shard')
- feed_gain_grad: float32 [1024], P('shard')
- feed_shift_grad: float32 [1024], P('shard')
- up_grad: float32 [1024, 4096], P('shard')
- up_bias_grad: float32 [4096], P('shard')
- down_grad: float32 [4096, 1024], P('shard')
- down_bias_grad: float32 [1024], P('shard')
The draws below stay inside these ranges and needn't reach their ends.
Inputs may be any that keep to these rules, and one draw needn't show every extreme that they name: `segment_ids`: in each tree the first 1024 tokens have segment 0; continuations 1 to 8 follow in order, each a run of tokens, of lengths 1, 2, 3, 4, 4, 5, 6 and 7 times 2048 // 64 in an order drawn for each tree. A prompt token's position is its index in the tree; the tokens of a continuation have positions 1024, 1025 and so on.
All inputs are finite; a program needn't handle non-finite values.
Results may differ from the reference program's by a relative error of at most 0.025.
Values may be sent and summed in bfloat16 or wider, within the bound.
A program may use at most 320 MiB of HBM per device.

```python
import math
import jax
import jax.numpy as jnp
import numpy as np
from jax import lax

D = 1024
HEADS = 16
HEAD_DIM = 64
FF = 4096
SRC = 1024
BRANCHES = 8
TREE_TOK = 2048
PROMPT = 1024
TREES = 8


def branch_layout(key):
    order_key = jax.random.fold_in(key, 11)
    orders = jax.vmap(lambda tree_key: jax.random.permutation(tree_key, BRANCHES))(jax.random.split(order_key, TREES))
    quarters = jnp.array(np.array([1, 2, 3, 4, 4, 5, 6, 7], dtype=np.int32))
    lengths = quarters[orders] * (TREE_TOK // 64)
    branch_end = PROMPT + jnp.cumsum(lengths, axis=1)
    branch_start = branch_end - lengths
    token_index = jnp.arange(TREE_TOK, dtype=jnp.int32)
    passed = jnp.sum((token_index[None, :, None] >= branch_end[:, None, :]).astype(jnp.int32), axis=2)
    segment = jnp.where(token_index[None, :] < PROMPT, 0, passed + 1).astype(jnp.int32)
    branch_ids = jnp.arange(1, BRANCHES + 1, dtype=jnp.int32)
    start_of = jnp.sum(jnp.where(segment[:, :, None] == branch_ids[None, None, :], branch_start[:, None, :], 0), axis=2)
    position = jnp.where(segment == 0, token_index[None, :], PROMPT + token_index[None, :] - start_of).astype(jnp.int32)
    return (segment, position)


def draw_segment_ids(key, part):
    return branch_layout(key)[0]


def draw_positions(key, part):
    return branch_layout(key)[1]


def shard_levels(key, extent, shards, low, top_value):
    def one(axis_at, blocks):
        heights = jax.random.uniform(jax.random.fold_in(jax.random.fold_in(key, 6), axis_at), (blocks,), jnp.float32, low / len(shards), top_value / len(shards))
        return jnp.repeat(jnp.exp(heights), extent[axis_at] // blocks).reshape((-1,) + (1,) * (len(extent) - axis_at - 1))

    factor_of = one(*shards[0])
    for cut in shards[1:]:
        factor_of = factor_of * one(*cut)
    return factor_of


def noise(own_key, extent, deviation, most, pieces=(), kind=jnp.bfloat16):
    entries = deviation * jax.random.normal(own_key, extent, jnp.float32)
    if pieces:
        entries = entries * shard_levels(own_key, extent, pieces, -0.22, 0.18)
    return jnp.clip(entries, -most, most).astype(kind)


def setup_inputs(seed: int = 0) -> dict:
    keys = jax.random.split(jax.random.key(seed), 27)
    return {
        "tokens": noise(keys[0], (TREES, TREE_TOK, D), 1.0, 6.0, ((0, 8), (1, 4))),
        "source": noise(keys[1], (TREES, SRC, D), 1.0, 6.0, ((0, 8), (1, 4))),
        "segment_ids": draw_segment_ids(jax.random.fold_in(keys[26], 71), 0),
        "positions": draw_positions(jax.random.fold_in(keys[26], 71), 0),
        "cotangent": noise(keys[4], (TREES, TREE_TOK, D), 1.0, 6.0, ((0, 8), (1, 4))),
        "self_gain": jnp.clip(1.0 + 0.1 * jax.random.normal(keys[5], (D,), jnp.float32), 0.5, 1.5).astype(jnp.bfloat16),
        "self_shift": noise(keys[6], (D,), 0.3, 1.75, ((0, 2),)),
        "self_weights": noise(keys[7], (D, 3 * D), D ** -0.5, 0.1875, ((0, 2),)),
        "query_bias": noise(keys[8], (D,), 0.3, 1.75, ((0, 2),)),
        "value_bias": noise(keys[9], (D,), 0.02, 0.125, ((0, 2),)),
        "self_output": noise(keys[10], (D, D), 4 ** -0.5, 3.0, ((0, 2),)),
        "output_bias": noise(keys[11], (D,), 0.3, 1.75, ((0, 2),)),
        "cross_gain": jnp.clip(1.0 + 0.1 * jax.random.normal(keys[12], (D,), jnp.float32), 0.5, 1.5).astype(jnp.bfloat16),
        "cross_shift": noise(keys[13], (D,), 0.3, 1.75, ((0, 2),)),
        "cross_query": noise(keys[14], (D, D), D ** -0.5, 0.1875, ((0, 2),)),
        "query_offset": noise(keys[15], (D,), 0.3, 1.75, ((0, 2),)),
        "cross_memory": noise(keys[16], (D, 2 * D), D ** -0.5, 0.1875, ((0, 2),)),
        "memory_offset": noise(keys[17], (D,), 0.02, 0.125, ((0, 2),)),
        "cross_output": noise(keys[18], (D, D), 4 ** -0.5, 3.0, ((0, 2),)),
        "return_bias": noise(keys[19], (D,), 0.3, 1.75, ((0, 2),)),
        "feed_gain": jnp.clip(1.0 + 0.1 * jax.random.normal(keys[20], (D,), jnp.float32), 0.5, 1.5).astype(jnp.bfloat16),
        "feed_shift": noise(keys[21], (D,), 0.3, 1.75, ((0, 2),)),
        "feed_up": noise(keys[22], (D, FF), D ** -0.5, 0.1875, ((0, 2),)),
        "up_bias": noise(keys[23], (FF,), 0.3, 1.75, ((0, 2),)),
        "feed_down": noise(keys[24], (FF, D), FF ** -0.5, 0.09375, ((0, 2),)),
        "down_bias": noise(keys[25], (D,), 0.3, 1.75, ((0, 2),)),
    }


@jax.custom_vjp
def low(v):
    return lax.optimization_barrier(v.astype(jnp.bfloat16)).astype(jnp.float32)

@jax.custom_vjp
def low_back(v):
    return v

def low_keep(v):
    return (low(v), None)

def low_pass(kept, grad):
    return (grad,)

def back_keep(v):
    return (v, None)

def back_low(kept, grad):
    return (low(grad),)
low.defvjp(low_keep, low_pass)
low_back.defvjp(back_keep, back_low)
EPSILON = 1e-05
NEGATIVE = -1e+30

def norm_rows(values, gain_vec, shift_vec):
    average = lax.optimization_barrier(jnp.mean(values, axis=-1, keepdims=True))
    centred = values - average
    spread = lax.optimization_barrier(jnp.mean(centred * centred, axis=-1, keepdims=True))
    return centred * lax.rsqrt(spread + EPSILON) * gain_vec + shift_vec

def round_both(values):
    return low(low_back(values))

def highest_dot(left_side, right_side):
    return jnp.dot(left_side, right_side, precision=lax.Precision.HIGHEST, preferred_element_type=jnp.float32)

def attention(queries, keys_in, values_in, query_seg, query_pos, key_seg, key_pos, masked):
    count = queries.shape[0]
    block_rows = min(512, count)
    key_heads = keys_in.reshape(-1, HEADS, HEAD_DIM)
    value_heads = values_in.reshape(-1, HEADS, HEAD_DIM)
    query_blocks = queries.reshape(count // block_rows, block_rows, HEADS, HEAD_DIM)
    seg_blocks = query_seg.reshape(count // block_rows, block_rows)
    pos_blocks = query_pos.reshape(count // block_rows, block_rows)

    def one_block(bundle):
        query_block, seg_block, pos_block = bundle
        scores = low_back(jnp.einsum('qhd,khd->hqk', query_block, key_heads, precision=lax.Precision.HIGHEST))
        if masked:
            shared = (key_seg[None, :] == 0) | (key_seg[None, :] == seg_block[:, None])
            allowed = shared & (key_pos[None, :] <= pos_block[:, None])
            scores = jnp.where(allowed[None], scores, NEGATIVE)
        weighting = jax.nn.softmax(scores, axis=-1)
        mixed = jnp.einsum('hqk,khd->qhd', low(weighting), value_heads, precision=lax.Precision.HIGHEST)
        return mixed.reshape(block_rows, D)
    result = lax.map(jax.checkpoint(one_block), (query_blocks, seg_blocks, pos_blocks))
    return result.reshape(count, D)

def block_forward(tokens_in, source_in, seg_tree, pos_tree, params):
    self_gain, self_shift, self_weights, query_bias, value_bias, self_output, output_bias, cross_gain, cross_shift, cross_query, query_offset, cross_memory, memory_offset, cross_output, return_bias, feed_gain, feed_shift, feed_up, up_bias, feed_down, down_bias = params
    head_scale = 1.0 / math.sqrt(HEAD_DIM)
    normed_self = low(norm_rows(tokens_in, self_gain, self_shift))
    projected = highest_dot(normed_self, self_weights)
    queries = round_both((projected[:, :D] + query_bias) * head_scale)
    keys_self = round_both(projected[:, D:2 * D])
    values_self = round_both(projected[:, 2 * D:] + value_bias)
    mixed_self = round_both(attention(queries, keys_self, values_self, seg_tree, pos_tree, seg_tree, pos_tree, True))
    first_sum = tokens_in + low_back(highest_dot(mixed_self, self_output)) + output_bias
    normed_cross = low(norm_rows(first_sum, cross_gain, cross_shift))
    cross_q = round_both((highest_dot(normed_cross, cross_query) + query_offset) * head_scale)
    memory = highest_dot(source_in, cross_memory)
    cross_keys = round_both(memory[:, :D])
    cross_values = round_both(memory[:, D:] + memory_offset)
    mixed_cross = round_both(attention(cross_q, cross_keys, cross_values, seg_tree, pos_tree, seg_tree, pos_tree, False))
    second = first_sum + low_back(highest_dot(mixed_cross, cross_output)) + return_bias
    normed_feed = low(norm_rows(second, feed_gain, feed_shift))
    hidden_pre = low_back(highest_dot(normed_feed, feed_up) + up_bias)
    hidden = low(jax.nn.gelu(hidden_pre, approximate=False))
    return second + highest_dot(hidden, feed_down) + down_bias

def reference(tokens, source, segment_ids, positions, cotangent, self_gain, self_shift, self_weights, query_bias, value_bias, self_output, output_bias, cross_gain, cross_shift, cross_query, query_offset, cross_memory, memory_offset, cross_output, return_bias, feed_gain, feed_shift, feed_up, up_bias, feed_down, down_bias):
    params = tuple((weight.astype(jnp.float32) for weight in (self_gain, self_shift, self_weights, query_bias, value_bias, self_output, output_bias, cross_gain, cross_shift, cross_query, query_offset, cross_memory, memory_offset, cross_output, return_bias, feed_gain, feed_shift, feed_up, up_bias, feed_down, down_bias)))

    def per_tree(totals, bundle):
        tree_tokens, tree_source, tree_seg, tree_pos, tree_cot = bundle

        def forward(tokens_in, source_in, params_in):
            return block_forward(tokens_in, source_in, tree_seg, tree_pos, params_in)
        output, pullback = jax.vjp(forward, tree_tokens.astype(jnp.float32), tree_source.astype(jnp.float32), params)
        tokens_part, source_part, params_part = pullback(tree_cot.astype(jnp.float32))
        totals = jax.tree.map(lambda total, extra: total + extra, totals, params_part)
        return (totals, (output.astype(jnp.bfloat16), tokens_part, source_part))
    start_totals = jax.tree.map(jnp.zeros_like, params)
    totals, (outputs, tokens_grad, source_grad) = lax.scan(per_tree, start_totals, (tokens, source, segment_ids, positions, cotangent))
    return (outputs, tokens_grad, source_grad, totals[0], totals[1], totals[2], totals[3], totals[4], totals[5], totals[6], totals[7], totals[8], totals[9], totals[10], totals[11], totals[12], totals[13], totals[14], totals[15], totals[16], totals[17], totals[18], totals[19], totals[20])
```

```python
import functools
import math

import jax
import jax.numpy as jnp
from jax import lax
from jax.experimental import pallas as pl
from jax.experimental.pallas import tpu as pltpu
from jax.sharding import PartitionSpec as P

MESH = pl.DeviceIdType.MESH
BF = jnp.bfloat16
F32 = jnp.float32


def coords():
    g, z, c = lax.axis_index("group"), lax.axis_index("ctx"), lax.axis_index("shard")
    return lax.rem(g, 2), lax.div(g, 2), z, c


def device_of(x, y, z, c):
    return (y * 2 + x, z, c)


def greet(devices):
    barrier = pltpu.get_barrier_semaphore()
    for device in devices:
        pl.semaphore_signal(barrier, inc=1, device_id=device, device_id_type=MESH)
    pl.semaphore_wait(barrier, len(devices))


CH = 512
WD = 1024
SETW = 512


def reduce_kernel(pieces, n_chunks, *refs):
    n_in = len(pieces)
    grads, small = refs[:n_in], refs[n_in]
    out, small_out = refs[n_in + 1 : n_in + 3]
    (acc, r0, r1, r2, r3, r4, sv, sr, load_sem, s0s, s0r, hs, hr, gs, gr, put_sem, svs, svr) = refs[n_in + 3 :]
    x, y, z, c = coords()
    sib = device_of(x, y, z, 1 - c)
    dx, dy = device_of(1 - x, y, z, c), device_of(x, 1 - y, z, c)
    dz2, dz1 = device_of(x, y, z + 2 - 4 * lax.div(z, 2), c), device_of(x, y, z + 1 - 2 * lax.rem(z, 2), c)
    greet((sib, dx, dy, dz2, dz1))

    loads, swaps = [], []
    j = 0
    for (kind, count), ref in zip(pieces, grads):
        for i in range(count):
            if kind == "cols":
                own = ref.at[pl.ds(c * CH, CH), pl.ds(i * WD, WD)]
                other = ref.at[pl.ds((1 - c) * CH, CH), pl.ds(i * WD, WD)]
            else:
                own = ref.at[pl.ds((c * count + i) * CH, CH), :]
                other = ref.at[pl.ds(((1 - c) * count + i) * CH, CH), :]
            pltpu.make_async_copy(own, acc.at[j], load_sem.at[j]).start()
            pltpu.make_async_remote_copy(
                src_ref=other, dst_ref=r0.at[j], send_sem=s0s.at[j], recv_sem=s0r.at[j], device_id=sib, device_id_type=MESH
            ).start()
            j += 1

    partners = (sib, dx, dy, dz2, dz1)
    sv[0] = small[...]

    def small_copy(p):
        return pltpu.make_async_remote_copy(
            src_ref=sv.at[p], dst_ref=sr.at[p], send_sem=svs.at[p], recv_sem=svr.at[p], device_id=partners[p], device_id_type=MESH
        )

    z2, z1 = lax.div(z, 2), lax.rem(z, 2)
    sets = (((dx, x), (dy, y), (dz2, z2), (dz1, z1)), ((dy, y), (dx, x), (dz2, z2), (dz1, z1)))
    rbufs = (r1, r2, r3, r4)

    def start_of(s, step):
        row = 0
        for q in range(step):
            row = row + sets[s][q][1] * (CH >> (q + 1))
        return row

    def halve_copy(jj, s, q):
        size = CH >> (q + 1)
        row = start_of(s, q) + (1 - sets[s][q][1]) * size
        return pltpu.make_async_remote_copy(
            src_ref=acc.at[jj, pl.ds(pl.multiple_of(row, 32), size), pl.ds(s * SETW, SETW)],
            dst_ref=rbufs[q].at[jj, s],
            send_sem=hs.at[jj, s, q],
            recv_sem=hr.at[jj, s, q],
            device_id=sets[s][q][0],
            device_id_type=MESH,
        )

    def give_copy(jj, s, q):
        size = CH >> (q + 1)
        row = start_of(s, q + 1)
        block = out.at[jj, pl.ds(pl.multiple_of(row, 32), size), pl.ds(s * SETW, SETW)]
        return pltpu.make_async_remote_copy(
            src_ref=block, dst_ref=block, send_sem=gs.at[jj, s, q], recv_sem=gr.at[jj, s, q], device_id=sets[s][q][0], device_id_type=MESH
        )

    def put_copy(jj, s):
        size = CH >> 4
        row = start_of(s, 4)
        block = (jj, pl.ds(pl.multiple_of(row, 32), size), pl.ds(s * SETW, SETW))
        return pltpu.make_async_copy(acc.at[block], out.at[block], put_sem.at[jj, s])

    def add_rows(jj, s, q):
        size = CH >> (q + 1)
        row = pl.multiple_of(start_of(s, q + 1), 32)
        span = min(size, 64)

        def one(k, carry):
            here = pl.ds(pl.multiple_of(row + k * span, 32), span)
            there = pl.ds(pl.multiple_of(k * span, 32), span)
            cols = pl.ds(s * SETW, SETW)
            total = acc[jj, here, cols].astype(F32) + rbufs[q][jj, s, there, :].astype(F32)
            acc[jj, here, cols] = total.astype(BF)
            return carry

        lax.fori_loop(0, size // span, one, 0)

    def phase0(jj):
        pltpu.make_async_copy(acc.at[jj], acc.at[jj], load_sem.at[jj]).wait()
        pltpu.make_async_remote_copy(
            src_ref=r0.at[jj], dst_ref=r0.at[jj], send_sem=s0s.at[jj], recv_sem=s0r.at[jj], device_id=sib, device_id_type=MESH
        ).wait()

        def one(k, carry):
            here = pl.ds(pl.multiple_of(k * 32, 32), 32)
            acc[jj, here, :] = (acc[jj, here, :].astype(F32) + r0[jj, here, :].astype(F32)).astype(BF)
            return carry

        lax.fori_loop(0, CH // 32, one, 0)
        for s in range(2):
            halve_copy(jj, s, 0).start()

    def phase_halve(jj, q):
        for s in range(2):
            halve_copy(jj, s, q).wait()
            add_rows(jj, s, q)
            if q < 3:
                halve_copy(jj, s, q + 1).start()
            else:
                put_copy(jj, s).start()
        if q == 3:
            for s in range(2):
                put_copy(jj, s).wait()
                give_copy(jj, s, 3).start()

    def phase_give(jj, q):
        for s in range(2):
            give_copy(jj, s, q).wait()
            if q > 0:
                give_copy(jj, s, q - 1).start()

    def small_phase(p):
        if p > 0:
            small_copy(p - 1).wait()
            sv[p] = sv[p - 1] + sr[p - 1]
        if p < 5:
            small_copy(p).start()
        else:
            small_out[...] = sv[5]

    def step(t, carry):
        def guarded(lag, what):
            @pl.when((t >= lag) & (t < n_chunks + lag))
            def _():
                what(t - lag)

        guarded(0, phase0)
        for q in range(4):
            guarded(q + 1, functools.partial(phase_halve, q=q))
        for q in range(3, -1, -1):
            guarded(8 - q, functools.partial(phase_give, q=q))
        for p in range(6):
            pl.when(t == p)(functools.partial(small_phase, p))
        return carry

    lax.fori_loop(0, n_chunks + 8, step, 0)


def reduce_gradients(pieces, grads, small):
    n_chunks = sum(count for _, count in pieces)
    any_spec = pl.BlockSpec(memory_space=pl.ANY)
    vmem = pl.BlockSpec(memory_space=pltpu.VMEM)
    dma = pltpu.SemaphoreType.DMA
    return pl.pallas_call(
        functools.partial(reduce_kernel, pieces, n_chunks),
        out_shape=(
            jax.ShapeDtypeStruct((n_chunks, CH, WD), BF),
            jax.ShapeDtypeStruct(small.shape, F32),
        ),
        in_specs=[any_spec] * len(grads) + [vmem],
        out_specs=(any_spec, vmem),
        scratch_shapes=[
            pltpu.VMEM((n_chunks, CH, WD), BF),
            pltpu.VMEM((n_chunks, CH, WD), BF),
            pltpu.VMEM((n_chunks, 2, CH // 2, SETW), BF),
            pltpu.VMEM((n_chunks, 2, CH // 4, SETW), BF),
            pltpu.VMEM((n_chunks, 2, CH // 8, SETW), BF),
            pltpu.VMEM((n_chunks, 2, CH // 16, SETW), BF),
            pltpu.VMEM((6,) + small.shape, F32),
            pltpu.VMEM((5,) + small.shape, F32),
            dma((n_chunks,)),
            dma((n_chunks,)),
            dma((n_chunks,)),
            dma((n_chunks, 2, 4)),
            dma((n_chunks, 2, 4)),
            dma((n_chunks, 2, 4)),
            dma((n_chunks, 2, 4)),
            dma((n_chunks, 2)),
            dma((5,)),
            dma((5,)),
        ],
        compiler_params=pltpu.CompilerParams(collective_id=1, has_side_effects=True, vmem_limit_bytes=60 << 20),
        cost_estimate=pl.CostEstimate(flops=0, bytes_accessed=50 << 20, transcendentals=0),
        name="reduce_gradients",
    )(*grads, small)


VECTOR_ORDER = (0, 1, 3, 4, 6, 7, 8, 10, 12, 14, 15, 16, 18, 20)
MATRIX_PIECES = ((2, "cols"), (5, "cols"), (9, "cols"), (11, "cols"), (13, "cols"), (17, "cols"), (19, "rows"))


def share_gradients(gradients, near):
    if not near:
        halves = [
            lax.psum_scatter(g.astype(BF), "shard", scatter_dimension=0, tiled=True).astype(F32) for g in gradients
        ]
        return lax.psum(tuple(halves), ("group", "ctx"))
    c = lax.axis_index("shard")
    rows = jnp.concatenate([gradients[i].astype(F32).reshape(-1, WD) for i in VECTOR_ORDER], axis=0)
    count = rows.shape[0]
    small = jnp.pad(rows, ((0, -count % 8), (0, 0)))
    pieces, arrays = [], []
    for i, kind in MATRIX_PIECES:
        arrays.append(gradients[i].astype(BF))
        pieces.append((kind, gradients[i].shape[1] // WD if kind == "cols" else gradients[i].shape[0] // (2 * CH)))
    summed, small_sum = reduce_gradients(tuple(pieces), arrays, small)
    result = [None] * len(gradients)
    at = 0
    for (i, kind), (_, n) in zip(MATRIX_PIECES, pieces):
        parts = [summed[at + k] for k in range(n)]
        at += n
        result[i] = (parts[0] if n == 1 else jnp.concatenate(parts, axis=1 if kind == "cols" else 0)).astype(F32)
    at = 0
    for i in VECTOR_ORDER:
        size = gradients[i].shape[0]
        n = size // WD
        vector = small_sum[at : at + n].reshape(size)
        at += n
        result[i] = lax.dynamic_slice_in_dim(vector, c * (size // 2), size // 2, 0)
    return result

D = 1024
HEADS = 16
HEAD_DIM = 64


EPSILON = 1e-05
NEGATIVE = -1e30


def norm_rows(values, gain_vec, shift_vec):
    average = jnp.mean(values, axis=-1, keepdims=True)
    centred = values - average
    spread = jnp.mean(centred * centred, axis=-1, keepdims=True)
    return centred * lax.rsqrt(spread + EPSILON) * gain_vec + shift_vec


def exact_gelu(values):
    return jax.nn.gelu(values, approximate=False)


def product(left_side, right_side):
    return jnp.dot(left_side, right_side, preferred_element_type=jnp.float32)


def left_product(left_side, right_side):
    return lax.dot_general(
        left_side, right_side, (((0,), (0,)), ((), ())), preferred_element_type=jnp.float32
    )


def right_product(left_side, right_side):
    return lax.dot_general(
        left_side, right_side, (((1,), (1,)), ((), ())), preferred_element_type=jnp.float32
    )


def heads_of(matrix):
    return matrix.reshape(matrix.shape[0], HEADS, HEAD_DIM)


def allow_table(query_seg, query_pos, key_seg, key_pos):
    shared = (key_seg[None, :] == 0) | (key_seg[None, :] == query_seg[:, None])
    return shared & (key_pos[None, :] <= query_pos[:, None])


def fold_keys(folded, queries, key_block, value_block, allowed):
    run_max, run_sum, weighted = folded
    scores = jnp.einsum("qhd,khd->hqk", queries, key_block, preferred_element_type=jnp.float32)
    if allowed is not None:
        scores = jnp.where(allowed[None], scores, NEGATIVE)
    new_max = jnp.maximum(run_max, jnp.max(scores, axis=2))
    factor = jnp.exp(run_max - new_max)
    weighting = jnp.exp(scores - new_max[:, :, None])
    new_sum = run_sum * factor + jnp.sum(weighting, axis=2)
    update = jnp.einsum(
        "hqk,khd->qhd",
        weighting.astype(jnp.bfloat16),
        value_block,
        preferred_element_type=jnp.float32,
    )
    return (new_max, new_sum, weighted * jnp.transpose(factor)[:, :, None] + update)


def attend_piece(folded, queries, key_piece, value_piece, tag_bundle):
    count_rows = key_piece.shape[0]
    block_rows = math.gcd(count_rows, 512)

    def one_block(number, current):
        offset = number * block_rows
        key_block = heads_of(lax.dynamic_slice_in_dim(key_piece, offset, block_rows, 0))
        value_block = heads_of(lax.dynamic_slice_in_dim(value_piece, offset, block_rows, 0))
        allowed = None
        if tag_bundle is not None:
            query_seg, query_pos, seg_all, pos_all = tag_bundle
            key_seg = lax.dynamic_slice_in_dim(seg_all, offset, block_rows, 0)
            key_pos = lax.dynamic_slice_in_dim(pos_all, offset, block_rows, 0)
            allowed = allow_table(query_seg, query_pos, key_seg, key_pos)
        return fold_keys(current, queries, key_block, value_block, allowed)

    return lax.fori_loop(0, count_rows // block_rows, one_block, folded)


def finish(folded):
    run_max, run_sum, weighted = folded
    attended = weighted / jnp.transpose(run_sum)[:, :, None]
    return (attended, run_max + jnp.log(run_sum))


def row_deltas(out_grad, attended):
    return jnp.einsum("qhd,qhd->hq", out_grad, attended, preferred_element_type=jnp.float32)


def attend_back(queries, key_all, value_all, out_grad, row_delta, log_total, tag_bundle):
    total_rows = key_all.shape[0]
    row_count = queries.shape[0]
    block_rows = math.gcd(total_rows, 512)

    def one_block(query_acc, number):
        offset = number * block_rows
        key_block = heads_of(lax.dynamic_slice_in_dim(key_all, offset, block_rows, 0))
        value_block = heads_of(lax.dynamic_slice_in_dim(value_all, offset, block_rows, 0))
        scores = jnp.einsum("qhd,khd->hqk", queries, key_block, preferred_element_type=jnp.float32)
        if tag_bundle is not None:
            query_seg, query_pos, seg_all, pos_all = tag_bundle
            key_seg = lax.dynamic_slice_in_dim(seg_all, offset, block_rows, 0)
            key_pos = lax.dynamic_slice_in_dim(pos_all, offset, block_rows, 0)
            scores = jnp.where(
                allow_table(query_seg, query_pos, key_seg, key_pos)[None], scores, NEGATIVE
            )
        weighting = jnp.exp(scores - log_total[:, :, None])
        weight_grad = jnp.einsum(
            "qhd,khd->hqk", out_grad, value_block, preferred_element_type=jnp.float32
        )
        score_grad = (weighting * (weight_grad - row_delta[:, :, None])).astype(jnp.bfloat16)
        query_acc = query_acc + jnp.einsum(
            "hqk,khd->qhd", score_grad, key_block, preferred_element_type=jnp.float32
        )
        key_term = jnp.einsum(
            "hqk,qhd->khd", score_grad, queries, preferred_element_type=jnp.float32
        )
        value_term = jnp.einsum(
            "hqk,qhd->khd",
            weighting.astype(jnp.bfloat16),
            out_grad,
            preferred_element_type=jnp.float32,
        )
        return (query_acc, (key_term.reshape(block_rows, D), value_term.reshape(block_rows, D)))

    start_acc = jnp.zeros((row_count, HEADS, HEAD_DIM), jnp.float32)
    query_acc, terms = lax.scan(one_block, start_acc, jnp.arange(total_rows // block_rows))
    key_terms, value_terms = terms
    return (
        query_acc.reshape(row_count, D),
        key_terms.reshape(total_rows, D),
        value_terms.reshape(total_rows, D),
    )


def per_device(
    tokens,
    source,
    segment_ids,
    positions,
    cotangent,
    self_gain,
    self_shift,
    self_weights,
    query_bias,
    value_bias,
    self_output,
    output_bias,
    cross_gain,
    cross_shift,
    cross_query,
    query_offset,
    cross_memory,
    memory_offset,
    cross_output,
    return_bias,
    feed_gain,
    feed_shift,
    feed_up,
    up_bias,
    feed_down,
    down_bias,
    *,
    near,
):
    (
        self_gain,
        self_shift,
        self_weights,
        query_bias,
        value_bias,
        self_output,
        output_bias,
        cross_gain,
        cross_shift,
        cross_query,
        query_offset,
        cross_memory,
        memory_offset,
        cross_output,
        return_bias,
        feed_gain,
        feed_shift,
        feed_up,
        up_bias,
        feed_down,
        down_bias,
    ) = (
        lax.all_gather(self_gain, "shard", axis=0, tiled=True),
        lax.all_gather(self_shift, "shard", axis=0, tiled=True),
        lax.all_gather(self_weights, "shard", axis=0, tiled=True),
        lax.all_gather(query_bias, "shard", axis=0, tiled=True),
        lax.all_gather(value_bias, "shard", axis=0, tiled=True),
        lax.all_gather(self_output, "shard", axis=0, tiled=True),
        lax.all_gather(output_bias, "shard", axis=0, tiled=True),
        lax.all_gather(cross_gain, "shard", axis=0, tiled=True),
        lax.all_gather(cross_shift, "shard", axis=0, tiled=True),
        lax.all_gather(cross_query, "shard", axis=0, tiled=True),
        lax.all_gather(query_offset, "shard", axis=0, tiled=True),
        lax.all_gather(cross_memory, "shard", axis=0, tiled=True),
        lax.all_gather(memory_offset, "shard", axis=0, tiled=True),
        lax.all_gather(cross_output, "shard", axis=0, tiled=True),
        lax.all_gather(return_bias, "shard", axis=0, tiled=True),
        lax.all_gather(feed_gain, "shard", axis=0, tiled=True),
        lax.all_gather(feed_shift, "shard", axis=0, tiled=True),
        lax.all_gather(feed_up, "shard", axis=0, tiled=True),
        lax.all_gather(up_bias, "shard", axis=0, tiled=True),
        lax.all_gather(feed_down, "shard", axis=0, tiled=True),
        lax.all_gather(down_bias, "shard", axis=0, tiled=True),
    )
    head_scale = 1.0 / math.sqrt(HEAD_DIM)
    row_count = tokens.shape[1]
    tok_rows = tokens[0].astype(jnp.float32)
    source_rows = source[0]
    tag_seg, tag_pos = (
        lax.all_gather(segment_ids, "ctx", axis=1, tiled=True),
        lax.all_gather(positions, "ctx", axis=1, tiled=True),
    )
    tag_bundle = (segment_ids[0], positions[0], tag_seg[0], tag_pos[0])
    gain_self = self_gain.astype(jnp.float32)
    shift_self = self_shift.astype(jnp.float32)
    normed_self = norm_rows(tok_rows, gain_self, shift_self).astype(jnp.bfloat16)
    projected = product(normed_self, self_weights)
    queries = ((projected[:, :D] + query_bias.astype(jnp.float32)) * head_scale).astype(
        jnp.bfloat16
    )
    keys_self = projected[:, D : 2 * D].astype(jnp.bfloat16)
    values_self = (projected[:, 2 * D :] + value_bias.astype(jnp.float32)).astype(jnp.bfloat16)
    query_heads = heads_of(queries)
    start_state = (
        jnp.full((HEADS, row_count), NEGATIVE, jnp.float32),
        jnp.zeros((HEADS, row_count), jnp.float32),
        jnp.zeros((row_count, HEADS, HEAD_DIM), jnp.float32),
    )
    folded_self = attend_piece(
        start_state,
        query_heads,
        lax.all_gather(keys_self, "ctx", axis=0, tiled=True),
        lax.all_gather(values_self, "ctx", axis=0, tiled=True),
        tag_bundle,
    )
    attended_self, total_self = finish(folded_self)
    mixed_self = attended_self.reshape(row_count, D).astype(jnp.bfloat16)
    first_sum = tok_rows + product(mixed_self, self_output) + output_bias.astype(jnp.float32)
    gain_cross = cross_gain.astype(jnp.float32)
    shift_cross = cross_shift.astype(jnp.float32)
    normed_cross = norm_rows(first_sum, gain_cross, shift_cross).astype(jnp.bfloat16)
    cross_q = (
        (product(normed_cross, cross_query) + query_offset.astype(jnp.float32)) * head_scale
    ).astype(jnp.bfloat16)
    memory = product(source_rows, cross_memory)
    memory_keys = memory[:, :D].astype(jnp.bfloat16)
    memory_values = (memory[:, D:] + memory_offset.astype(jnp.float32)).astype(jnp.bfloat16)
    cross_keys, cross_values = (
        lax.all_gather(memory_keys, "ctx", axis=0, tiled=True),
        lax.all_gather(memory_values, "ctx", axis=0, tiled=True),
    )
    cross_heads = heads_of(cross_q)
    attended_cross, total_cross = finish(
        attend_piece(start_state, cross_heads, cross_keys, cross_values, None)
    )
    mixed_cross = attended_cross.reshape(row_count, D).astype(jnp.bfloat16)
    second = first_sum + product(mixed_cross, cross_output) + return_bias.astype(jnp.float32)
    gain_feed = feed_gain.astype(jnp.float32)
    shift_feed = feed_shift.astype(jnp.float32)
    normed_feed = norm_rows(second, gain_feed, shift_feed).astype(jnp.bfloat16)
    hidden_pre = product(normed_feed, feed_up) + up_bias.astype(jnp.float32)
    hidden_act, gelu_pull = jax.vjp(exact_gelu, hidden_pre)
    hidden = hidden_act.astype(jnp.bfloat16)
    block_output = (second + product(hidden, feed_down) + down_bias.astype(jnp.float32)).astype(
        jnp.bfloat16
    )
    out_grad = cotangent[0]
    down_grad = left_product(hidden, out_grad)
    down_bias_grad = jnp.sum(out_grad, axis=0, dtype=jnp.float32)
    (hidden_grad,) = gelu_pull(right_product(out_grad, feed_down))
    hidden_grad = hidden_grad.astype(jnp.bfloat16)
    up_grad = left_product(normed_feed, hidden_grad)
    up_bias_grad = jnp.sum(hidden_grad, axis=0, dtype=jnp.float32)
    norm_value, feed_pull = jax.vjp(norm_rows, second, gain_feed, shift_feed)
    second_part, feed_gain_grad, feed_shift_grad = feed_pull(right_product(hidden_grad, feed_up))
    second_grad = out_grad.astype(jnp.float32) + second_part
    branch_cross = second_grad.astype(jnp.bfloat16)
    cross_output_grad = left_product(mixed_cross, branch_cross)
    return_bias_grad = jnp.sum(second_grad, axis=0)
    mixed_cross_grad = right_product(branch_cross, cross_output).astype(jnp.bfloat16)
    cross_grad_heads = heads_of(mixed_cross_grad)
    cross_delta = row_deltas(cross_grad_heads, attended_cross)
    cross_sum, key_terms, value_terms = attend_back(
        cross_heads, cross_keys, cross_values, cross_grad_heads, cross_delta, total_cross, None
    )
    key_part, value_part = (
        lax.psum_scatter(
            key_terms.astype(jnp.bfloat16), "ctx", scatter_dimension=0, tiled=True
        ).astype(jnp.float32),
        lax.psum_scatter(
            value_terms.astype(jnp.bfloat16), "ctx", scatter_dimension=0, tiled=True
        ).astype(jnp.float32),
    )
    memory_grad = jnp.concatenate(
        [key_part.astype(jnp.bfloat16), value_part.astype(jnp.bfloat16)], axis=1
    )
    source_grad = right_product(memory_grad, cross_memory)
    cross_memory_grad = left_product(source_rows, memory_grad)
    memory_offset_grad = jnp.sum(memory_grad[:, D:], axis=0, dtype=jnp.float32)
    cross_q_grad = cross_sum.astype(jnp.bfloat16) * head_scale
    cross_query_grad = left_product(normed_cross, cross_q_grad)
    query_offset_grad = jnp.sum(cross_q_grad, axis=0, dtype=jnp.float32)
    norm_value, cross_pull = jax.vjp(norm_rows, first_sum, gain_cross, shift_cross)
    first_part, cross_gain_grad, cross_shift_grad = cross_pull(
        right_product(cross_q_grad, cross_query)
    )
    first_grad = second_grad + first_part
    branch_self = first_grad.astype(jnp.bfloat16)
    self_output_grad = left_product(mixed_self, branch_self)
    output_bias_grad = jnp.sum(first_grad, axis=0)
    mixed_self_grad = right_product(branch_self, self_output).astype(jnp.bfloat16)
    keys_back, values_back = (
        lax.all_gather(keys_self, "ctx", axis=0, tiled=True),
        lax.all_gather(values_self, "ctx", axis=0, tiled=True),
    )
    self_grad_heads = heads_of(mixed_self_grad)
    self_delta = row_deltas(self_grad_heads, attended_self)
    query_sum, key_terms_self, value_terms_self = attend_back(
        query_heads, keys_back, values_back, self_grad_heads, self_delta, total_self, tag_bundle
    )
    key_own, value_own = (
        lax.psum_scatter(
            key_terms_self.astype(jnp.bfloat16), "ctx", scatter_dimension=0, tiled=True
        ).astype(jnp.float32),
        lax.psum_scatter(
            value_terms_self.astype(jnp.bfloat16), "ctx", scatter_dimension=0, tiled=True
        ).astype(jnp.float32),
    )
    query_grad = query_sum.astype(jnp.bfloat16) * head_scale
    value_grad = value_own.astype(jnp.bfloat16)
    projected_grad = jnp.concatenate([query_grad, key_own.astype(jnp.bfloat16), value_grad], axis=1)
    self_weights_grad = left_product(normed_self, projected_grad)
    query_bias_grad = jnp.sum(query_grad, axis=0, dtype=jnp.float32)
    value_bias_grad = jnp.sum(value_grad, axis=0, dtype=jnp.float32)
    norm_value, self_pull = jax.vjp(norm_rows, tok_rows, gain_self, shift_self)
    token_part, self_gain_grad, self_shift_grad = self_pull(
        right_product(projected_grad, self_weights)
    )
    tokens_grad = first_grad + token_part
    gradients = (
        self_gain_grad,
        self_shift_grad,
        self_weights_grad,
        query_bias_grad,
        value_bias_grad,
        self_output_grad,
        output_bias_grad,
        cross_gain_grad,
        cross_shift_grad,
        cross_query_grad,
        query_offset_grad,
        cross_memory_grad,
        memory_offset_grad,
        cross_output_grad,
        return_bias_grad,
        feed_gain_grad,
        feed_shift_grad,
        up_grad,
        up_bias_grad,
        down_grad,
        down_bias_grad,
    )
    reduced = share_gradients(gradients, near)
    return (block_output[None], tokens_grad[None], source_grad[None]) + tuple(reduced)


def solution(mesh):
    near = (mesh.shape["group"], mesh.shape["ctx"], mesh.shape["shard"]) == (4, 4, 2)
    placed = (
        P(("group", "shard"), "ctx", None),
        P(("group", "shard"), "ctx", None),
        P(("group", "shard"), "ctx"),
        P(("group", "shard"), "ctx"),
        P(("group", "shard"), "ctx", None),
        P("shard"),
        P("shard"),
        P("shard", None),
        P("shard"),
        P("shard"),
        P("shard", None),
        P("shard"),
        P("shard"),
        P("shard"),
        P("shard", None),
        P("shard"),
        P("shard", None),
        P("shard"),
        P("shard", None),
        P("shard"),
        P("shard"),
        P("shard"),
        P("shard", None),
        P("shard"),
        P("shard", None),
        P("shard"),
    )
    return jax.shard_map(
        functools.partial(per_device, near=near),
        mesh=mesh,
        in_specs=placed,
        out_specs=(
            P(("group", "shard"), "ctx", None),
            P(("group", "shard"), "ctx", None),
            P(("group", "shard"), "ctx", None),
            P("shard"),
            P("shard"),
            P("shard", None),
            P("shard"),
            P("shard"),
            P("shard", None),
            P("shard"),
            P("shard"),
            P("shard"),
            P("shard", None),
            P("shard"),
            P("shard", None),
            P("shard"),
            P("shard", None),
            P("shard"),
            P("shard"),
            P("shard"),
            P("shard", None),
            P("shard"),
            P("shard", None),
            P("shard"),
        ),
        check_vma=False,
    )
```

```python
import functools
import math

import jax
import jax.numpy as jnp
from jax import lax
from jax.experimental import pallas as pl
from jax.experimental.pallas import tpu as pltpu
from jax.sharding import PartitionSpec as P

MESH = pl.DeviceIdType.MESH
BF = jnp.bfloat16
F32 = jnp.float32


def coords():
    g, z, c = lax.axis_index("group"), lax.axis_index("ctx"), lax.axis_index("shard")
    return lax.rem(g, 2), lax.div(g, 2), z, c


def device_of(x, y, z, c):
    return (y * 2 + x, z, c)


def greet(devices):
    barrier = pltpu.get_barrier_semaphore()
    for device in devices:
        pl.semaphore_signal(barrier, inc=1, device_id=device, device_id_type=MESH)
    pl.semaphore_wait(barrier, len(devices))


CH = 512
WD = 1024
SETW = 512


def reduce_kernel(pieces, n_chunks, *refs):
    n_in = len(pieces)
    grads, small = refs[:n_in], refs[n_in]
    out, small_out = refs[n_in + 1 : n_in + 3]
    (acc, r0, r1, r2, r3, r4, sv, sr, load_sem, s0s, s0r, hs, hr, gs, gr, put_sem, svs, svr) = refs[n_in + 3 :]
    x, y, z, c = coords()
    sib = device_of(x, y, z, 1 - c)
    dx, dy = device_of(1 - x, y, z, c), device_of(x, 1 - y, z, c)
    dz2, dz1 = device_of(x, y, z + 2 - 4 * lax.div(z, 2), c), device_of(x, y, z + 1 - 2 * lax.rem(z, 2), c)
    greet((sib, dx, dy, dz2, dz1))

    loads, swaps = [], []
    j = 0
    for (kind, count), ref in zip(pieces, grads):
        for i in range(count):
            if kind == "cols":
                own = ref.at[pl.ds(c * CH, CH), pl.ds(i * WD, WD)]
                other = ref.at[pl.ds((1 - c) * CH, CH), pl.ds(i * WD, WD)]
            else:
                own = ref.at[pl.ds((c * count + i) * CH, CH), :]
                other = ref.at[pl.ds(((1 - c) * count + i) * CH, CH), :]
            pltpu.make_async_copy(own, acc.at[j], load_sem.at[j]).start()
            pltpu.make_async_remote_copy(
                src_ref=other, dst_ref=r0.at[j], send_sem=s0s.at[j], recv_sem=s0r.at[j], device_id=sib, device_id_type=MESH
            ).start()
            j += 1

    partners = (sib, dx, dy, dz2, dz1)
    sv[0] = small[...]

    def small_copy(p):
        return pltpu.make_async_remote_copy(
            src_ref=sv.at[p], dst_ref=sr.at[p], send_sem=svs.at[p], recv_sem=svr.at[p], device_id=partners[p], device_id_type=MESH
        )

    z2, z1 = lax.div(z, 2), lax.rem(z, 2)
    sets = (((dx, x), (dy, y), (dz2, z2), (dz1, z1)), ((dy, y), (dx, x), (dz2, z2), (dz1, z1)))
    rbufs = (r1, r2, r3, r4)

    def start_of(s, step):
        row = 0
        for q in range(step):
            row = row + sets[s][q][1] * (CH >> (q + 1))
        return row

    def halve_copy(jj, s, q):
        size = CH >> (q + 1)
        row = start_of(s, q) + (1 - sets[s][q][1]) * size
        return pltpu.make_async_remote_copy(
            src_ref=acc.at[jj, pl.ds(pl.multiple_of(row, 32), size), pl.ds(s * SETW, SETW)],
            dst_ref=rbufs[q].at[jj, s],
            send_sem=hs.at[jj, s, q],
            recv_sem=hr.at[jj, s, q],
            device_id=sets[s][q][0],
            device_id_type=MESH,
        )

    def give_copy(jj, s, q):
        size = CH >> (q + 1)
        row = start_of(s, q + 1)
        block = out.at[jj, pl.ds(pl.multiple_of(row, 32), size), pl.ds(s * SETW, SETW)]
        return pltpu.make_async_remote_copy(
            src_ref=block, dst_ref=block, send_sem=gs.at[jj, s, q], recv_sem=gr.at[jj, s, q], device_id=sets[s][q][0], device_id_type=MESH
        )

    def put_copy(jj, s):
        size = CH >> 4
        row = start_of(s, 4)
        block = (jj, pl.ds(pl.multiple_of(row, 32), size), pl.ds(s * SETW, SETW))
        return pltpu.make_async_copy(acc.at[block], out.at[block], put_sem.at[jj, s])

    def add_rows(jj, s, q):
        size = CH >> (q + 1)
        row = pl.multiple_of(start_of(s, q + 1), 32)
        span = min(size, 64)

        def one(k, carry):
            here = pl.ds(pl.multiple_of(row + k * span, 32), span)
            there = pl.ds(pl.multiple_of(k * span, 32), span)
            cols = pl.ds(s * SETW, SETW)
            total = acc[jj, here, cols].astype(F32) + rbufs[q][jj, s, there, :].astype(F32)
            acc[jj, here, cols] = total.astype(BF)
            return carry

        lax.fori_loop(0, size // span, one, 0)

    def phase0(jj):
        pltpu.make_async_copy(acc.at[jj], acc.at[jj], load_sem.at[jj]).wait()
        pltpu.make_async_remote_copy(
            src_ref=r0.at[jj], dst_ref=r0.at[jj], send_sem=s0s.at[jj], recv_sem=s0r.at[jj], device_id=sib, device_id_type=MESH
        ).wait()

        def one(k, carry):
            here = pl.ds(pl.multiple_of(k * 32, 32), 32)
            acc[jj, here, :] = (acc[jj, here, :].astype(F32) + r0[jj, here, :].astype(F32)).astype(BF)
            return carry

        lax.fori_loop(0, CH // 32, one, 0)
        for s in range(2):
            halve_copy(jj, s, 0).start()

    def phase_halve(jj, q):
        for s in range(2):
            halve_copy(jj, s, q).wait()
            add_rows(jj, s, q)
            if q < 3:
                halve_copy(jj, s, q + 1).start()
            else:
                put_copy(jj, s).start()
        if q == 3:
            for s in range(2):
                put_copy(jj, s).wait()
                give_copy(jj, s, 3).start()

    def phase_give(jj, q):
        for s in range(2):
            give_copy(jj, s, q).wait()
            if q > 0:
                give_copy(jj, s, q - 1).start()

    def small_phase(p):
        if p > 0:
            small_copy(p - 1).wait()
            sv[p] = sv[p - 1] + sr[p - 1]
        if p < 5:
            small_copy(p).start()
        else:
            small_out[...] = sv[5]

    def step(t, carry):
        def guarded(lag, what):
            @pl.when((t >= lag) & (t < n_chunks + lag))
            def _():
                what(t - lag)

        guarded(0, phase0)
        for q in range(4):
            guarded(q + 1, functools.partial(phase_halve, q=q))
        for q in range(3, -1, -1):
            guarded(8 - q, functools.partial(phase_give, q=q))
        for p in range(6):
            pl.when(t == p)(functools.partial(small_phase, p))
        return carry

    lax.fori_loop(0, n_chunks + 8, step, 0)


def reduce_gradients(pieces, grads, small):
    n_chunks = sum(count for _, count in pieces)
    any_spec = pl.BlockSpec(memory_space=pl.ANY)
    vmem = pl.BlockSpec(memory_space=pltpu.VMEM)
    dma = pltpu.SemaphoreType.DMA
    return pl.pallas_call(
        functools.partial(reduce_kernel, pieces, n_chunks),
        out_shape=(
            jax.ShapeDtypeStruct((n_chunks, CH, WD), BF),
            jax.ShapeDtypeStruct(small.shape, F32),
        ),
        in_specs=[any_spec] * len(grads) + [vmem],
        out_specs=(any_spec, vmem),
        scratch_shapes=[
            pltpu.VMEM((n_chunks, CH, WD), BF),
            pltpu.VMEM((n_chunks, CH, WD), BF),
            pltpu.VMEM((n_chunks, 2, CH // 2, SETW), BF),
            pltpu.VMEM((n_chunks, 2, CH // 4, SETW), BF),
            pltpu.VMEM((n_chunks, 2, CH // 8, SETW), BF),
            pltpu.VMEM((n_chunks, 2, CH // 16, SETW), BF),
            pltpu.VMEM((6,) + small.shape, F32),
            pltpu.VMEM((5,) + small.shape, F32),
            dma((n_chunks,)),
            dma((n_chunks,)),
            dma((n_chunks,)),
            dma((n_chunks, 2, 4)),
            dma((n_chunks, 2, 4)),
            dma((n_chunks, 2, 4)),
            dma((n_chunks, 2, 4)),
            dma((n_chunks, 2)),
            dma((5,)),
            dma((5,)),
        ],
        compiler_params=pltpu.CompilerParams(collective_id=1, has_side_effects=True, vmem_limit_bytes=60 << 20),
        cost_estimate=pl.CostEstimate(flops=0, bytes_accessed=50 << 20, transcendentals=0),
        name="reduce_gradients",
    )(*grads, small)


VECTOR_ORDER = (0, 1, 3, 4, 6, 7, 8, 10, 12, 14, 15, 16, 18, 20)
MATRIX_PIECES = ((2, "cols"), (5, "cols"), (9, "cols"), (11, "cols"), (13, "cols"), (17, "cols"), (19, "rows"))


def share_gradients(gradients, near):
    if not near:
        halves = [
            lax.psum_scatter(g.astype(BF), "shard", scatter_dimension=0, tiled=True).astype(F32) for g in gradients
        ]
        return lax.psum(tuple(halves), ("group", "ctx"))
    c = lax.axis_index("shard")
    rows = jnp.concatenate([gradients[i].astype(F32).reshape(-1, WD) for i in VECTOR_ORDER], axis=0)
    count = rows.shape[0]
    small = jnp.pad(rows, ((0, -count % 8), (0, 0)))
    pieces, arrays = [], []
    for i, kind in MATRIX_PIECES:
        arrays.append(gradients[i].astype(BF))
        pieces.append((kind, gradients[i].shape[1] // WD if kind == "cols" else gradients[i].shape[0] // (2 * CH)))
    summed, small_sum = reduce_gradients(tuple(pieces), arrays, small)
    result = [None] * len(gradients)
    at = 0
    for (i, kind), (_, n) in zip(MATRIX_PIECES, pieces):
        parts = [summed[at + k] for k in range(n)]
        at += n
        result[i] = (parts[0] if n == 1 else jnp.concatenate(parts, axis=1 if kind == "cols" else 0)).astype(F32)
    at = 0
    for i in VECTOR_ORDER:
        size = gradients[i].shape[0]
        n = size // WD
        vector = small_sum[at : at + n].reshape(size)
        at += n
        result[i] = lax.dynamic_slice_in_dim(vector, c * (size // 2), size // 2, 0)
    return result

D = 1024
HEADS = 16
HEAD_DIM = 64


EPSILON = 1e-05
NEGATIVE = -1e30


def norm_rows(values, gain_vec, shift_vec):
    average = jnp.mean(values, axis=-1, keepdims=True)
    centred = values - average
    spread = jnp.mean(centred * centred, axis=-1, keepdims=True)
    return centred * lax.rsqrt(spread + EPSILON) * gain_vec + shift_vec


def exact_gelu(values):
    return jax.nn.gelu(values, approximate=False)


def product(left_side, right_side):
    return jnp.dot(left_side, right_side, preferred_element_type=jnp.float32)


def left_product(left_side, right_side):
    return lax.dot_general(
        left_side, right_side, (((0,), (0,)), ((), ())), preferred_element_type=jnp.float32
    )


def right_product(left_side, right_side):
    return lax.dot_general(
        left_side, right_side, (((1,), (1,)), ((), ())), preferred_element_type=jnp.float32
    )


def heads_of(matrix):
    return matrix.reshape(matrix.shape[0], HEADS, HEAD_DIM)


def allow_table(query_seg, query_pos, key_seg, key_pos):
    shared = (key_seg[None, :] == 0) | (key_seg[None, :] == query_seg[:, None])
    return shared & (key_pos[None, :] <= query_pos[:, None])


def fold_keys(folded, queries, key_block, value_block, allowed):
    run_max, run_sum, weighted = folded
    scores = jnp.einsum("qhd,khd->hqk", queries, key_block, preferred_element_type=jnp.float32)
    if allowed is not None:
        scores = jnp.where(allowed[None], scores, NEGATIVE)
    new_max = jnp.maximum(run_max, jnp.max(scores, axis=2))
    factor = jnp.exp(run_max - new_max)
    weighting = jnp.exp(scores - new_max[:, :, None])
    new_sum = run_sum * factor + jnp.sum(weighting, axis=2)
    update = jnp.einsum(
        "hqk,khd->qhd",
        weighting.astype(jnp.bfloat16),
        value_block,
        preferred_element_type=jnp.float32,
    )
    return (new_max, new_sum, weighted * jnp.transpose(factor)[:, :, None] + update)


def attend_piece(folded, queries, key_piece, value_piece, tag_bundle):
    count_rows = key_piece.shape[0]
    block_rows = math.gcd(count_rows, 512)

    def one_block(number, current):
        offset = number * block_rows
        key_block = heads_of(lax.dynamic_slice_in_dim(key_piece, offset, block_rows, 0))
        value_block = heads_of(lax.dynamic_slice_in_dim(value_piece, offset, block_rows, 0))
        allowed = None
        if tag_bundle is not None:
            query_seg, query_pos, seg_all, pos_all = tag_bundle
            key_seg = lax.dynamic_slice_in_dim(seg_all, offset, block_rows, 0)
            key_pos = lax.dynamic_slice_in_dim(pos_all, offset, block_rows, 0)
            allowed = allow_table(query_seg, query_pos, key_seg, key_pos)
        return fold_keys(current, queries, key_block, value_block, allowed)

    return lax.fori_loop(0, count_rows // block_rows, one_block, folded)


def finish(folded):
    run_max, run_sum, weighted = folded
    attended = weighted / jnp.transpose(run_sum)[:, :, None]
    return (attended, run_max + jnp.log(run_sum))


def row_deltas(out_grad, attended):
    return jnp.einsum("qhd,qhd->hq", out_grad, attended, preferred_element_type=jnp.float32)


def attend_back(queries, key_all, value_all, out_grad, row_delta, log_total, tag_bundle):
    total_rows = key_all.shape[0]
    row_count = queries.shape[0]
    block_rows = math.gcd(total_rows, 512)

    def one_block(query_acc, number):
        offset = number * block_rows
        key_block = heads_of(lax.dynamic_slice_in_dim(key_all, offset, block_rows, 0))
        value_block = heads_of(lax.dynamic_slice_in_dim(value_all, offset, block_rows, 0))
        scores = jnp.einsum("qhd,khd->hqk", queries, key_block, preferred_element_type=jnp.float32)
        if tag_bundle is not None:
            query_seg, query_pos, seg_all, pos_all = tag_bundle
            key_seg = lax.dynamic_slice_in_dim(seg_all, offset, block_rows, 0)
            key_pos = lax.dynamic_slice_in_dim(pos_all, offset, block_rows, 0)
            scores = jnp.where(
                allow_table(query_seg, query_pos, key_seg, key_pos)[None], scores, NEGATIVE
            )
        weighting = jnp.exp(scores - log_total[:, :, None])
        weight_grad = jnp.einsum(
            "qhd,khd->hqk", out_grad, value_block, preferred_element_type=jnp.float32
        )
        score_grad = (weighting * (weight_grad - row_delta[:, :, None])).astype(jnp.bfloat16)
        query_acc = query_acc + jnp.einsum(
            "hqk,khd->qhd", score_grad, key_block, preferred_element_type=jnp.float32
        )
        key_term = jnp.einsum(
            "hqk,qhd->khd", score_grad, queries, preferred_element_type=jnp.float32
        )
        value_term = jnp.einsum(
            "hqk,qhd->khd",
            weighting.astype(jnp.bfloat16),
            out_grad,
            preferred_element_type=jnp.float32,
        )
        return (query_acc, (key_term.reshape(block_rows, D), value_term.reshape(block_rows, D)))

    start_acc = jnp.zeros((row_count, HEADS, HEAD_DIM), jnp.float32)
    query_acc, terms = lax.scan(one_block, start_acc, jnp.arange(total_rows // block_rows))
    key_terms, value_terms = terms
    return (
        query_acc.reshape(row_count, D),
        key_terms.reshape(total_rows, D),
        value_terms.reshape(total_rows, D),
    )


TILE = 256
LANES = 128
NEG = -1e30


def dot_nt(a, b):
    return lax.dot_general(a, b, (((1,), (1,)), ((), ())), preferred_element_type=F32)


def dot_nn(a, b):
    return lax.dot_general(a, b, (((1,), (0,)), ((), ())), preferred_element_type=F32)


def split_heads(source, target, heads):
    rows = source.shape[0]
    step = min(rows, 256)
    even = lax.broadcasted_iota(jnp.int32, (step, LANES), 1) < LANES // 2

    def one(k, carry):
        here = pl.ds(pl.multiple_of(k * step, step), step)
        for pair in range(heads // 2):
            block = source[here, pl.ds(pair * LANES, LANES)]
            target[2 * pair, here, :] = jnp.where(even, block, jnp.zeros_like(block))
            target[2 * pair + 1, here, :] = jnp.where(even, jnp.zeros_like(block), block)
        return carry

    lax.fori_loop(0, rows // step, one, 0)


def transpose_rows(source, target):
    rows = source.shape[0]
    step = min(rows, 256)

    def one(k, carry):
        here = pl.ds(pl.multiple_of(k * step, step), step)
        target[:, here] = source[here, :].astype(F32).T.astype(target.dtype)
        return carry

    lax.fori_loop(0, rows // step, one, 0)


def tree_mask(key_tile, query_tile, key_seg, query_seg, prompt):
    key_at = key_tile * TILE + lax.broadcasted_iota(jnp.int32, (TILE, TILE), 0)
    query_at = query_tile * TILE + lax.broadcasted_iota(jnp.int32, (TILE, TILE), 1)
    return (key_at <= query_at) & ((key_at < prompt) | (key_seg == query_seg))


def forward_kernel(heads, masked, *refs):
    if masked:
        q_ref, k_ref, v_ref, seg_col, seg_row, o_ref, lse_ref, qm, vt, m_ref, l_ref, acc = refs
    else:
        q_ref, k_ref, v_ref, o_ref, lse_ref, qm, vt, m_ref, l_ref, acc = refs
    n_query, n_key = q_ref.shape[0] // TILE, k_ref.shape[0] // TILE
    prompt_tiles = n_key // 2
    split_heads(q_ref, qm, heads)
    transpose_rows(v_ref, vt)

    def query_tile(i, carry):
        rows = pl.ds(pl.multiple_of(i * TILE, TILE), TILE)
        m_ref[...] = jnp.full_like(m_ref, NEG)
        l_ref[...] = jnp.zeros_like(l_ref)
        acc[...] = jnp.zeros_like(acc)

        def tile(j, mask):
            keys = pl.ds(pl.multiple_of(j * TILE, TILE), TILE)
            for h in range(heads):
                scores = dot_nt(k_ref[keys, pl.ds(h // 2 * LANES, LANES)], qm[h, rows, :])
                if mask is not None:
                    scores = jnp.where(mask, scores, NEG)
                old = m_ref[pl.ds(h, 1), :]
                new = jnp.maximum(old, jnp.max(scores, axis=0, keepdims=True))
                weights = jnp.exp(scores - new)
                if mask is not None:
                    weights = jnp.where(mask, weights, 0.0)
                factor = jnp.exp(old - new)
                m_ref[pl.ds(h, 1), :] = new
                l_ref[pl.ds(h, 1), :] = l_ref[pl.ds(h, 1), :] * factor + jnp.sum(weights, axis=0, keepdims=True)
                part = pl.ds(h * 64, 64)
                acc[part, :] = acc[part, :] * factor + dot_nn(vt[part, keys], weights.astype(BF))

        if masked:
            lax.fori_loop(0, jnp.minimum(i, prompt_tiles), lambda j, c: (tile(j, None), c)[1], 0)

            def near(j):
                keys = pl.ds(pl.multiple_of(j * TILE, TILE), TILE)
                tile(j, tree_mask(j, i, seg_col[keys, :], seg_row[:, rows], prompt_tiles * TILE))

            first = jnp.where(i > prompt_tiles, i - 1, i)
            lax.fori_loop(first, i + 1, lambda j, c: (near(j), c)[1], 0)
        else:
            lax.fori_loop(0, n_key, lambda j, c: (tile(j, None), c)[1], 0)
        for h in range(heads):
            part = pl.ds(h * 64, 64)
            acc[part, :] = acc[part, :] / l_ref[pl.ds(h, 1), :]
        lse_ref[:, rows] = m_ref[...] + jnp.log(l_ref[...])
        o_ref[rows, :] = acc[...].T.astype(BF)
        return carry

    lax.fori_loop(0, n_query, query_tile, 0)


def attention_forward(q, k, v, seg=None):
    heads, width = 4, 256
    n, m, groups = q.shape[0], k.shape[0], q.shape[1] // 256
    masked = seg is not None
    column = lambda rows: pl.BlockSpec((rows, width), lambda p: (0, p))
    whole = lambda shape: pl.BlockSpec(shape, lambda p: (0, 0))
    extra = [seg.reshape(n, 1), seg.reshape(1, n)] if masked else []
    return pl.pallas_call(
        functools.partial(forward_kernel, heads, masked),
        grid=(groups,),
        out_shape=(jax.ShapeDtypeStruct((n, q.shape[1]), BF), jax.ShapeDtypeStruct((groups, 8, n), F32)),
        in_specs=[column(n), column(m), column(m)] + [whole(e.shape) for e in extra],
        out_specs=(column(n), pl.BlockSpec((None, 8, n), lambda p: (p, 0, 0))),
        scratch_shapes=[
            pltpu.VMEM((heads, n, LANES), BF),
            pltpu.VMEM((width, m), BF),
            pltpu.VMEM((8, TILE), F32),
            pltpu.VMEM((8, TILE), F32),
            pltpu.VMEM((width, TILE), F32),
        ],
        compiler_params=pltpu.CompilerParams(vmem_limit_bytes=40 << 20),
        cost_estimate=pl.CostEstimate(flops=4 * n * m * q.shape[1], bytes_accessed=4 * (n + m) * q.shape[1], transcendentals=n * m * heads * groups),
        name="attention_forward",
    )(q, k, v, *extra)


def backward_kernel(heads, masked, *refs):
    if masked:
        q_ref, k_ref, v_ref, g_ref, o_ref, lse_ref, seg_col, seg_row, dq_ref, dk_ref, dv_ref, qm, gm, kt, dqt, dk_acc, dv_acc, delta = refs
    else:
        q_ref, k_ref, v_ref, g_ref, o_ref, lse_ref, dq_ref, dk_ref, dv_ref, qm, gm, kt, dqt, dk_acc, dv_acc, delta = refs
    n_query, n_key = q_ref.shape[0] // TILE, k_ref.shape[0] // TILE
    prompt_tiles = n_key // 2
    split_heads(q_ref, qm, heads)
    split_heads(g_ref, gm, heads)
    transpose_rows(k_ref, kt)
    dqt[...] = jnp.zeros_like(dqt)

    def deltas(i, carry):
        rows = pl.ds(pl.multiple_of(i * TILE, TILE), TILE)
        product = (g_ref[rows, :].astype(F32) * o_ref[rows, :].astype(F32)).T
        for h in range(heads):
            delta[pl.ds(h, 1), rows] = jnp.sum(product[h * 64 : h * 64 + 64, :], axis=0, keepdims=True)
        return carry

    lax.fori_loop(0, n_query, deltas, 0)

    def key_tile(j, carry):
        keys = pl.ds(pl.multiple_of(j * TILE, TILE), TILE)
        dk_acc[...] = jnp.zeros_like(dk_acc)
        dv_acc[...] = jnp.zeros_like(dv_acc)

        def tile(i, mask):
            rows = pl.ds(pl.multiple_of(i * TILE, TILE), TILE)
            for h in range(heads):
                lanes = pl.ds(h // 2 * LANES, LANES)
                scores = dot_nt(k_ref[keys, lanes], qm[h, rows, :])
                weights = jnp.exp(scores - lse_ref[pl.ds(h, 1), rows])
                if mask is not None:
                    weights = jnp.where(mask, weights, 0.0)
                change = dot_nt(v_ref[keys, lanes], gm[h, rows, :])
                back = (weights * (change - delta[pl.ds(h, 1), rows])).astype(BF)
                dv_acc[:, lanes] += dot_nn(weights.astype(BF), gm[h, rows, :])
                dk_acc[:, lanes] += dot_nn(back, qm[h, rows, :])
                part = pl.ds(h * 64, 64)
                dqt[part, rows] += dot_nn(kt[part, keys], back)

        if masked:

            def near(i):
                rows = pl.ds(pl.multiple_of(i * TILE, TILE), TILE)
                tile(i, tree_mask(j, i, seg_col[keys, :], seg_row[:, rows], prompt_tiles * TILE))

            prompt = j < prompt_tiles
            last = jnp.where(prompt, j, jnp.minimum(j + 1, n_query - 1))
            lax.fori_loop(j, last + 1, lambda i, c: (near(i), c)[1], 0)
            lax.fori_loop(jnp.where(prompt, j + 1, n_query), n_query, lambda i, c: (tile(i, None), c)[1], 0)
        else:
            lax.fori_loop(0, n_query, lambda i, c: (tile(i, None), c)[1], 0)
        dk_ref[keys, :] = dk_acc[...].astype(BF)
        dv_ref[keys, :] = dv_acc[...].astype(BF)
        return carry

    lax.fori_loop(0, n_key, key_tile, 0)

    def finish(i, carry):
        rows = pl.ds(pl.multiple_of(i * TILE, TILE), TILE)
        dq_ref[rows, :] = dqt[:, rows].T.astype(BF)
        return carry

    lax.fori_loop(0, n_query, finish, 0)


def attention_backward(q, k, v, grad, mix, lse, seg=None):
    heads, width = 4, 256
    n, m, groups = q.shape[0], k.shape[0], q.shape[1] // 256
    masked = seg is not None
    column = lambda rows: pl.BlockSpec((rows, width), lambda p: (0, p))
    whole = lambda shape: pl.BlockSpec(shape, lambda p: (0, 0))
    extra = [seg.reshape(n, 1), seg.reshape(1, n)] if masked else []
    return pl.pallas_call(
        functools.partial(backward_kernel, heads, masked),
        grid=(groups,),
        out_shape=(
            jax.ShapeDtypeStruct((n, q.shape[1]), BF),
            jax.ShapeDtypeStruct((m, q.shape[1]), BF),
            jax.ShapeDtypeStruct((m, q.shape[1]), BF),
        ),
        in_specs=[column(n), column(m), column(m), column(n), column(n), pl.BlockSpec((None, 8, n), lambda p: (p, 0, 0))]
        + [whole(e.shape) for e in extra],
        out_specs=(column(n), column(m), column(m)),
        scratch_shapes=[
            pltpu.VMEM((heads, n, LANES), BF),
            pltpu.VMEM((heads, n, LANES), BF),
            pltpu.VMEM((width, m), BF),
            pltpu.VMEM((width, n), F32),
            pltpu.VMEM((TILE, width), F32),
            pltpu.VMEM((TILE, width), F32),
            pltpu.VMEM((8, n), F32),
        ],
        compiler_params=pltpu.CompilerParams(vmem_limit_bytes=48 << 20),
        cost_estimate=pl.CostEstimate(flops=10 * n * m * q.shape[1], bytes_accessed=8 * (n + m) * q.shape[1], transcendentals=n * m * heads * groups),
        name="attention_backward",
    )(q, k, v, grad, mix, lse, *extra)


def pair_places():
    x, y, z, c = coords()
    side = 1 - 2 * lax.rem(z, 2)
    sib, near, diag = device_of(x, y, z, 1 - c), device_of(x, y, z + side, c), device_of(x, y, z + side, 1 - c)
    far = device_of(x, y, z + 2 - 4 * lax.div(z, 2), 1 - c)
    block = 2 * c + lax.rem(z, 2)
    near_block = 2 * c + 1 - lax.rem(z, 2)
    sib_block = 2 * (1 - c) + lax.rem(z, 2)
    diag_block = 2 * (1 - c) + 1 - lax.rem(z, 2)
    home = lax.div(z, 2) == c
    return sib, near, diag, far, block, near_block, sib_block, diag_block, home


TOKEN_PARTS = 4


def spread_kernel(n_mats, *refs):
    tok, seg = refs[:2]
    mats = refs[2 : 2 + n_mats]
    tok_all, seg_all = refs[2 + n_mats : 4 + n_mats]
    fulls = refs[4 + n_mats : 4 + 2 * n_mats]
    stage = refs[4 + 2 * n_mats : 4 + 3 * n_mats]
    tok_stage, seg_stage = refs[4 + 3 * n_mats : 6 + 3 * n_mats]
    (mat_load, mat_put, mat_send, mat_recv, own_load, own_put, far_send, far_recv, sib_send, sib_recv, near_send, near_recv, pass_send, pass_recv) = refs[6 + 3 * n_mats :]
    sib, near, diag, far, block, near_block, sib_block, diag_block, home = pair_places()
    _, _, z, c = coords()
    greet((sib, near, far))
    rows = tok.shape[0]
    part = rows // TOKEN_PARTS
    n_items = TOKEN_PARTS + 1

    def source(k):
        return seg if k == TOKEN_PARTS else tok.at[pl.ds(k * part, part), :]

    def place(k, b):
        if k == TOKEN_PARTS:
            return seg_all.at[b]
        return tok_all.at[pl.ds(pl.multiple_of(b * rows + k * part, part), part), :]

    def remote(src, dst, send, recv, device):
        return pltpu.make_async_remote_copy(src_ref=src, dst_ref=dst, send_sem=send, recv_sem=recv, device_id=device, device_id_type=MESH)

    def far_copy(k):
        return remote(source(k), place(k, z), far_send.at[k], far_recv.at[k], far)

    def staged(k):
        return seg_stage if k == TOKEN_PARTS else tok_stage.at[pl.ds(k * part, part), :]

    def own_copy(k):
        return pltpu.make_async_copy(source(k), staged(k), own_load.at[k])

    def own_out(k):
        return pltpu.make_async_copy(staged(k), place(k, block), own_put.at[k])

    def sib_copy(k):
        return remote(place(k, block), place(k, block), sib_send.at[k], sib_recv.at[k], sib)

    def near_copy(k):
        return remote(place(k, block), place(k, block), near_send.at[k], near_recv.at[k], near)

    def pass_copy(k):
        return remote(place(k, near_block), place(k, near_block), pass_send.at[k], pass_recv.at[k], sib)

    @pl.when(home)
    def _():
        for k in range(n_items):
            own_copy(k).start()

    @pl.when(jnp.logical_not(home))
    def _():
        for k in range(n_items):
            far_copy(k).start()

    def mat_target(i):
        half = mats[i].shape[0]
        return fulls[i].at[pl.ds(pl.multiple_of(c * half, 8), half), :]

    def mat_in(i):
        return pltpu.make_async_copy(mats[i], stage[i], mat_load.at[i])

    def mat_out(i):
        return pltpu.make_async_copy(stage[i], mat_target(i), mat_put.at[i])

    def mat_remote(i):
        return remote(mats[i], mat_target(i), mat_send.at[i], mat_recv.at[i], sib)

    for i in range(n_mats):
        mat_in(i).start()
        mat_remote(i).start()

    for k in range(n_items + 1):
        if k < n_items:

            @pl.when(home)
            def _():
                own_copy(k).wait()
                own_out(k).start()
                own_out(k).wait()

            @pl.when(jnp.logical_not(home))
            def _():
                far_copy(k).wait()

            sib_copy(k).start()
            near_copy(k).start()
        if k > 0:
            near_copy(k - 1).wait()
            pass_copy(k - 1).start()
    for i in range(n_mats):
        mat_in(i).wait()
        mat_out(i).start()
    for k in range(n_items):
        sib_copy(k).wait()
        pass_copy(k).wait()
    for i in range(n_mats):
        mat_out(i).wait()
        mat_remote(i).wait()


def spread(tokens, seg, mats):
    n = len(mats)
    any_spec = pl.BlockSpec(memory_space=pl.ANY)
    dma = pltpu.SemaphoreType.DMA
    items = TOKEN_PARTS + 1
    return pl.pallas_call(
        functools.partial(spread_kernel, n),
        out_shape=[
            jax.ShapeDtypeStruct((4 * tokens.shape[0], tokens.shape[1]), tokens.dtype),
            jax.ShapeDtypeStruct((4,) + seg.shape, seg.dtype),
        ]
        + [jax.ShapeDtypeStruct((2 * m.shape[0], m.shape[1]), m.dtype) for m in mats],
        in_specs=[any_spec] * (2 + n),
        out_specs=[any_spec] * (2 + n),
        scratch_shapes=[pltpu.VMEM(a.shape, a.dtype) for a in (*mats, tokens, seg)] + [dma((n,))] * 4 + [dma((items,))] * 10,
        compiler_params=pltpu.CompilerParams(collective_id=2, has_side_effects=True, vmem_limit_bytes=32 << 20),
        cost_estimate=pl.CostEstimate(flops=0, bytes_accessed=64 << 20, transcendentals=0),
        name="spread",
    )(tokens, seg, *mats)


def trade_kernel(to_columns, n_in, *refs):
    srcs, out, load, send, recv = refs[:n_in], refs[n_in], refs[n_in + 1], refs[n_in + 2], refs[n_in + 3]
    sib, near, diag, far, block, near_block, sib_block, diag_block, home = pair_places()
    greet((sib, near, diag))
    if to_columns:
        rows, cols = srcs[0].shape[0] // 4, srcs[0].shape[1]
    else:
        rows, cols = srcs[0].shape[0], srcs[0].shape[1] // 4
    copies = []
    for i, src in enumerate(srcs):

        def piece(b):
            if to_columns:
                return src.at[pl.ds(pl.multiple_of(b * rows, rows), rows), :]
            return src.at[:, pl.ds(pl.multiple_of(b * cols, cols), cols)]

        if to_columns:
            target = out.at[:, pl.ds(pl.multiple_of(i * 4 * cols + block * cols, cols), cols)]
        else:
            target = out.at[pl.ds(pl.multiple_of(block * rows, rows), rows), :]
        for k, (device, b) in enumerate(((near, near_block), (diag, diag_block), (sib, sib_block))):
            copies.append(
                pltpu.make_async_remote_copy(
                    src_ref=piece(b), dst_ref=target, send_sem=send.at[i, k], recv_sem=recv.at[i, k], device_id=device, device_id_type=MESH
                )
            )
        copies.append(pltpu.make_async_copy(piece(block), target, load.at[i]))
    for copy in copies:
        copy.start()
    for copy in copies:
        copy.wait()


def trade(to_columns, srcs, collective_id):
    n = len(srcs)
    rows, cols = srcs[0].shape
    shape = (rows // 4, 4 * cols * n) if to_columns else (rows * 4, cols // 4)
    any_spec = pl.BlockSpec(memory_space=pl.ANY)
    dma = pltpu.SemaphoreType.DMA
    return pl.pallas_call(
        functools.partial(trade_kernel, to_columns, n),
        out_shape=jax.ShapeDtypeStruct(shape, srcs[0].dtype),
        in_specs=[any_spec] * n,
        out_specs=any_spec,
        scratch_shapes=[dma((n,)), dma((n, 3)), dma((n, 3))],
        compiler_params=pltpu.CompilerParams(collective_id=collective_id, has_side_effects=True),
        cost_estimate=pl.CostEstimate(flops=0, bytes_accessed=(8 << 20) * n, transcendentals=0),
        name="trade",
    )(*srcs)


SWAP = [(2 * z + c, 2 * z + c if z // 2 == c else 2 * ((z + 2) % 4) + 1 - c) for z in range(4) for c in range(2)]
NEAR = [(z, z + 1 - 2 * (z % 2)) for z in range(4)]
SIB = [(0, 1), (1, 0)]


def swap(array):
    return lax.ppermute(array, ("ctx", "shard"), SWAP)


def pair_device(
    tokens, source, segment_ids, positions, cotangent,
    self_gain, self_shift, self_weights, query_bias, value_bias, self_output, output_bias,
    cross_gain, cross_shift, cross_query, query_offset, cross_memory, memory_offset, cross_output, return_bias,
    feed_gain, feed_shift, feed_up, up_bias, feed_down, down_bias,
):
    c, z = lax.axis_index("shard"), lax.axis_index("ctx")
    block = 2 * c + lax.rem(z, 2)
    head_scale = 1.0 / math.sqrt(HEAD_DIM)
    rows = tokens.shape[1]
    vectors = (
        self_gain, self_shift, query_bias, value_bias, output_bias, cross_gain, cross_shift, query_offset, memory_offset,
        return_bias, feed_gain, feed_shift, down_bias, up_bias,
    )
    half = D // 2
    packed = jnp.concatenate([v.reshape(-1, half) for v in vectors], axis=0)
    n_packed = packed.shape[0]
    packed = jnp.pad(packed, ((0, -n_packed % 16), (0, 0)))
    mats = (self_weights, self_output, cross_memory, cross_query, cross_output, feed_up, feed_down, packed)
    spread_out = spread(tokens[0], segment_ids.reshape(4, rows // 4), mats)
    tokens_all, seg_all = spread_out[:2]
    self_weights, self_output, cross_memory, cross_query, cross_output, feed_up, feed_down, packed = spread_out[2:]
    own_source = swap(source[0])
    out_grad = swap(cotangent[0])
    near_source = lax.ppermute(own_source, "ctx", NEAR)
    chip_source = jnp.concatenate([own_source, near_source], axis=0)
    source_all = jnp.concatenate([chip_source, lax.ppermute(chip_source, "shard", SIB)], axis=0)
    packed = packed.astype(F32).reshape(2, -1, half)
    unpacked = [packed[:, i].reshape(D) for i in range(13)]
    (
        self_gain, self_shift, query_bias, value_bias, output_bias, cross_gain, cross_shift, query_offset, memory_offset,
        return_bias, feed_gain, feed_shift, down_bias,
    ) = unpacked
    up_bias = packed[:, 13:n_packed].reshape(-1)
    seg = seg_all.reshape(-1)

    width = D // 4
    own_cols = lambda a, part: lax.dynamic_slice_in_dim(a, part * D + block * width, width, a.ndim - 1)
    normed_all = norm_rows(tokens_all.astype(F32), self_gain, self_shift).astype(BF)
    q = ((product(normed_all, own_cols(self_weights, 0)) + own_cols(query_bias, 0)) * head_scale).astype(BF)
    k = product(normed_all, own_cols(self_weights, 1)).astype(BF)
    v = (product(normed_all, own_cols(self_weights, 2)) + own_cols(value_bias, 0)).astype(BF)
    mix_heads, lse_self = attention_forward(q, k, v, seg)
    mixed_self = trade(True, (mix_heads,), 3)

    tok_rows = lax.dynamic_slice_in_dim(tokens_all, block * rows, rows, 0).astype(F32)
    normed_self = lax.dynamic_slice_in_dim(normed_all, block * rows, rows, 0)
    first_sum = tok_rows + product(mixed_self, self_output) + output_bias
    normed_cross = norm_rows(first_sum, cross_gain, cross_shift).astype(BF)
    cross_q = ((product(normed_cross, cross_query) + query_offset) * head_scale).astype(BF)
    memory = product(source_all, cross_memory)
    cross_keys = memory[:, :D].astype(BF)
    cross_values = (memory[:, D:] + memory_offset).astype(BF)
    mixed_cross, lse_cross = attention_forward(cross_q, cross_keys, cross_values)
    second = first_sum + product(mixed_cross, cross_output) + return_bias
    normed_feed = norm_rows(second, feed_gain, feed_shift).astype(BF)
    hidden_pre = product(normed_feed, feed_up) + up_bias
    hidden_act, gelu_pull = jax.vjp(exact_gelu, hidden_pre)
    hidden = hidden_act.astype(BF)
    block_output = (second + product(hidden, feed_down) + down_bias).astype(BF)

    down_grad = left_product(hidden, out_grad).astype(BF)
    down_bias_grad = jnp.sum(out_grad, axis=0, dtype=F32)
    (hidden_grad,) = gelu_pull(right_product(out_grad, feed_down))
    hidden_grad = hidden_grad.astype(BF)
    up_grad = left_product(normed_feed, hidden_grad).astype(BF)
    up_bias_grad = jnp.sum(hidden_grad, axis=0, dtype=F32)
    _, feed_pull = jax.vjp(norm_rows, second, feed_gain, feed_shift)
    second_part, feed_gain_grad, feed_shift_grad = feed_pull(right_product(hidden_grad, feed_up))
    second_grad = out_grad.astype(F32) + second_part
    branch_cross = second_grad.astype(BF)
    cross_output_grad = left_product(mixed_cross, branch_cross).astype(BF)
    return_bias_grad = jnp.sum(second_grad, axis=0)
    mixed_cross_grad = right_product(branch_cross, cross_output).astype(BF)
    cross_sum, key_terms, value_terms = attention_backward(
        cross_q, cross_keys, cross_values, mixed_cross_grad, mixed_cross, lse_cross
    )

    def gather_terms(terms):
        n = terms.shape[0] // 2
        terms = (terms[:n].astype(F32) + lax.ppermute(terms[n:], "shard", SIB).astype(F32)).astype(BF)
        n = n // 2
        return (terms[:n].astype(F32) + lax.ppermute(terms[n:], "ctx", NEAR).astype(F32)).astype(BF)

    memory_grad = jnp.concatenate([gather_terms(key_terms), gather_terms(value_terms)], axis=1)
    source_grad = right_product(memory_grad, cross_memory).astype(BF)
    cross_memory_grad = left_product(own_source, memory_grad).astype(BF)
    memory_offset_grad = jnp.sum(memory_grad[:, D:], axis=0, dtype=F32)
    cross_q_grad = cross_sum * head_scale
    cross_query_grad = left_product(normed_cross, cross_q_grad).astype(BF)
    query_offset_grad = jnp.sum(cross_q_grad, axis=0, dtype=F32)
    _, cross_pull = jax.vjp(norm_rows, first_sum, cross_gain, cross_shift)
    first_part, cross_gain_grad, cross_shift_grad = cross_pull(right_product(cross_q_grad, cross_query))
    first_grad = second_grad + first_part
    branch_self = first_grad.astype(BF)
    self_output_grad = left_product(mixed_self, branch_self).astype(BF)
    output_bias_grad = jnp.sum(first_grad, axis=0)
    mixed_self_grad = right_product(branch_self, self_output).astype(BF)
    grad_heads = trade(False, (mixed_self_grad,), 4)
    dq, dk, dv = attention_backward(q, k, v, grad_heads, mix_heads, lse_self, seg)
    projected_grad = trade(True, ((dq * head_scale).astype(BF), dk, dv), 5)
    self_weights_grad = left_product(normed_self, projected_grad).astype(BF)
    query_bias_grad = jnp.sum(projected_grad[:, :D], axis=0, dtype=F32)
    value_bias_grad = jnp.sum(projected_grad[:, 2 * D :], axis=0, dtype=F32)
    _, self_pull = jax.vjp(norm_rows, tok_rows, self_gain, self_shift)
    token_part, self_gain_grad, self_shift_grad = self_pull(right_product(projected_grad, self_weights))
    tokens_grad = (first_grad + token_part).astype(BF)
    gradients = (
        self_gain_grad, self_shift_grad, self_weights_grad, query_bias_grad, value_bias_grad, self_output_grad, output_bias_grad,
        cross_gain_grad, cross_shift_grad, cross_query_grad, query_offset_grad, cross_memory_grad, memory_offset_grad,
        cross_output_grad, return_bias_grad, feed_gain_grad, feed_shift_grad, up_grad, up_bias_grad, down_grad, down_bias_grad,
    )
    reduced = share_gradients(gradients, True)
    return (
        swap(block_output)[None],
        swap(tokens_grad).astype(F32)[None],
        swap(source_grad).astype(F32)[None],
    ) + tuple(reduced)


def per_device(
    tokens,
    source,
    segment_ids,
    positions,
    cotangent,
    self_gain,
    self_shift,
    self_weights,
    query_bias,
    value_bias,
    self_output,
    output_bias,
    cross_gain,
    cross_shift,
    cross_query,
    query_offset,
    cross_memory,
    memory_offset,
    cross_output,
    return_bias,
    feed_gain,
    feed_shift,
    feed_up,
    up_bias,
    feed_down,
    down_bias,
):
    (
        self_gain,
        self_shift,
        self_weights,
        query_bias,
        value_bias,
        self_output,
        output_bias,
        cross_gain,
        cross_shift,
        cross_query,
        query_offset,
        cross_memory,
        memory_offset,
        cross_output,
        return_bias,
        feed_gain,
        feed_shift,
        feed_up,
        up_bias,
        feed_down,
        down_bias,
    ) = (
        lax.all_gather(self_gain, "shard", axis=0, tiled=True),
        lax.all_gather(self_shift, "shard", axis=0, tiled=True),
        lax.all_gather(self_weights, "shard", axis=0, tiled=True),
        lax.all_gather(query_bias, "shard", axis=0, tiled=True),
        lax.all_gather(value_bias, "shard", axis=0, tiled=True),
        lax.all_gather(self_output, "shard", axis=0, tiled=True),
        lax.all_gather(output_bias, "shard", axis=0, tiled=True),
        lax.all_gather(cross_gain, "shard", axis=0, tiled=True),
        lax.all_gather(cross_shift, "shard", axis=0, tiled=True),
        lax.all_gather(cross_query, "shard", axis=0, tiled=True),
        lax.all_gather(query_offset, "shard", axis=0, tiled=True),
        lax.all_gather(cross_memory, "shard", axis=0, tiled=True),
        lax.all_gather(memory_offset, "shard", axis=0, tiled=True),
        lax.all_gather(cross_output, "shard", axis=0, tiled=True),
        lax.all_gather(return_bias, "shard", axis=0, tiled=True),
        lax.all_gather(feed_gain, "shard", axis=0, tiled=True),
        lax.all_gather(feed_shift, "shard", axis=0, tiled=True),
        lax.all_gather(feed_up, "shard", axis=0, tiled=True),
        lax.all_gather(up_bias, "shard", axis=0, tiled=True),
        lax.all_gather(feed_down, "shard", axis=0, tiled=True),
        lax.all_gather(down_bias, "shard", axis=0, tiled=True),
    )
    head_scale = 1.0 / math.sqrt(HEAD_DIM)
    row_count = tokens.shape[1]
    tok_rows = tokens[0].astype(jnp.float32)
    source_rows = source[0]
    tag_seg, tag_pos = (
        lax.all_gather(segment_ids, "ctx", axis=1, tiled=True),
        lax.all_gather(positions, "ctx", axis=1, tiled=True),
    )
    tag_bundle = (segment_ids[0], positions[0], tag_seg[0], tag_pos[0])
    gain_self = self_gain.astype(jnp.float32)
    shift_self = self_shift.astype(jnp.float32)
    normed_self = norm_rows(tok_rows, gain_self, shift_self).astype(jnp.bfloat16)
    projected = product(normed_self, self_weights)
    queries = ((projected[:, :D] + query_bias.astype(jnp.float32)) * head_scale).astype(
        jnp.bfloat16
    )
    keys_self = projected[:, D : 2 * D].astype(jnp.bfloat16)
    values_self = (projected[:, 2 * D :] + value_bias.astype(jnp.float32)).astype(jnp.bfloat16)
    query_heads = heads_of(queries)
    start_state = (
        jnp.full((HEADS, row_count), NEGATIVE, jnp.float32),
        jnp.zeros((HEADS, row_count), jnp.float32),
        jnp.zeros((row_count, HEADS, HEAD_DIM), jnp.float32),
    )
    folded_self = attend_piece(
        start_state,
        query_heads,
        lax.all_gather(keys_self, "ctx", axis=0, tiled=True),
        lax.all_gather(values_self, "ctx", axis=0, tiled=True),
        tag_bundle,
    )
    attended_self, total_self = finish(folded_self)
    mixed_self = attended_self.reshape(row_count, D).astype(jnp.bfloat16)
    first_sum = tok_rows + product(mixed_self, self_output) + output_bias.astype(jnp.float32)
    gain_cross = cross_gain.astype(jnp.float32)
    shift_cross = cross_shift.astype(jnp.float32)
    normed_cross = norm_rows(first_sum, gain_cross, shift_cross).astype(jnp.bfloat16)
    cross_q = (
        (product(normed_cross, cross_query) + query_offset.astype(jnp.float32)) * head_scale
    ).astype(jnp.bfloat16)
    memory = product(source_rows, cross_memory)
    memory_keys = memory[:, :D].astype(jnp.bfloat16)
    memory_values = (memory[:, D:] + memory_offset.astype(jnp.float32)).astype(jnp.bfloat16)
    cross_keys, cross_values = (
        lax.all_gather(memory_keys, "ctx", axis=0, tiled=True),
        lax.all_gather(memory_values, "ctx", axis=0, tiled=True),
    )
    cross_heads = heads_of(cross_q)
    attended_cross, total_cross = finish(
        attend_piece(start_state, cross_heads, cross_keys, cross_values, None)
    )
    mixed_cross = attended_cross.reshape(row_count, D).astype(jnp.bfloat16)
    second = first_sum + product(mixed_cross, cross_output) + return_bias.astype(jnp.float32)
    gain_feed = feed_gain.astype(jnp.float32)
    shift_feed = feed_shift.astype(jnp.float32)
    normed_feed = norm_rows(second, gain_feed, shift_feed).astype(jnp.bfloat16)
    hidden_pre = product(normed_feed, feed_up) + up_bias.astype(jnp.float32)
    hidden_act, gelu_pull = jax.vjp(exact_gelu, hidden_pre)
    hidden = hidden_act.astype(jnp.bfloat16)
    block_output = (second + product(hidden, feed_down) + down_bias.astype(jnp.float32)).astype(
        jnp.bfloat16
    )
    out_grad = cotangent[0]
    down_grad = left_product(hidden, out_grad)
    down_bias_grad = jnp.sum(out_grad, axis=0, dtype=jnp.float32)
    (hidden_grad,) = gelu_pull(right_product(out_grad, feed_down))
    hidden_grad = hidden_grad.astype(jnp.bfloat16)
    up_grad = left_product(normed_feed, hidden_grad)
    up_bias_grad = jnp.sum(hidden_grad, axis=0, dtype=jnp.float32)
    norm_value, feed_pull = jax.vjp(norm_rows, second, gain_feed, shift_feed)
    second_part, feed_gain_grad, feed_shift_grad = feed_pull(right_product(hidden_grad, feed_up))
    second_grad = out_grad.astype(jnp.float32) + second_part
    branch_cross = second_grad.astype(jnp.bfloat16)
    cross_output_grad = left_product(mixed_cross, branch_cross)
    return_bias_grad = jnp.sum(second_grad, axis=0)
    mixed_cross_grad = right_product(branch_cross, cross_output).astype(jnp.bfloat16)
    cross_grad_heads = heads_of(mixed_cross_grad)
    cross_delta = row_deltas(cross_grad_heads, attended_cross)
    cross_sum, key_terms, value_terms = attend_back(
        cross_heads, cross_keys, cross_values, cross_grad_heads, cross_delta, total_cross, None
    )
    key_part, value_part = (
        lax.psum_scatter(
            key_terms.astype(jnp.bfloat16), "ctx", scatter_dimension=0, tiled=True
        ).astype(jnp.float32),
        lax.psum_scatter(
            value_terms.astype(jnp.bfloat16), "ctx", scatter_dimension=0, tiled=True
        ).astype(jnp.float32),
    )
    memory_grad = jnp.concatenate(
        [key_part.astype(jnp.bfloat16), value_part.astype(jnp.bfloat16)], axis=1
    )
    source_grad = right_product(memory_grad, cross_memory)
    cross_memory_grad = left_product(source_rows, memory_grad)
    memory_offset_grad = jnp.sum(memory_grad[:, D:], axis=0, dtype=jnp.float32)
    cross_q_grad = cross_sum.astype(jnp.bfloat16) * head_scale
    cross_query_grad = left_product(normed_cross, cross_q_grad)
    query_offset_grad = jnp.sum(cross_q_grad, axis=0, dtype=jnp.float32)
    norm_value, cross_pull = jax.vjp(norm_rows, first_sum, gain_cross, shift_cross)
    first_part, cross_gain_grad, cross_shift_grad = cross_pull(
        right_product(cross_q_grad, cross_query)
    )
    first_grad = second_grad + first_part
    branch_self = first_grad.astype(jnp.bfloat16)
    self_output_grad = left_product(mixed_self, branch_self)
    output_bias_grad = jnp.sum(first_grad, axis=0)
    mixed_self_grad = right_product(branch_self, self_output).astype(jnp.bfloat16)
    keys_back, values_back = (
        lax.all_gather(keys_self, "ctx", axis=0, tiled=True),
        lax.all_gather(values_self, "ctx", axis=0, tiled=True),
    )
    self_grad_heads = heads_of(mixed_self_grad)
    self_delta = row_deltas(self_grad_heads, attended_self)
    query_sum, key_terms_self, value_terms_self = attend_back(
        query_heads, keys_back, values_back, self_grad_heads, self_delta, total_self, tag_bundle
    )
    key_own, value_own = (
        lax.psum_scatter(
            key_terms_self.astype(jnp.bfloat16), "ctx", scatter_dimension=0, tiled=True
        ).astype(jnp.float32),
        lax.psum_scatter(
            value_terms_self.astype(jnp.bfloat16), "ctx", scatter_dimension=0, tiled=True
        ).astype(jnp.float32),
    )
    query_grad = query_sum.astype(jnp.bfloat16) * head_scale
    value_grad = value_own.astype(jnp.bfloat16)
    projected_grad = jnp.concatenate([query_grad, key_own.astype(jnp.bfloat16), value_grad], axis=1)
    self_weights_grad = left_product(normed_self, projected_grad)
    query_bias_grad = jnp.sum(query_grad, axis=0, dtype=jnp.float32)
    value_bias_grad = jnp.sum(value_grad, axis=0, dtype=jnp.float32)
    norm_value, self_pull = jax.vjp(norm_rows, tok_rows, gain_self, shift_self)
    token_part, self_gain_grad, self_shift_grad = self_pull(
        right_product(projected_grad, self_weights)
    )
    tokens_grad = first_grad + token_part
    gradients = (
        self_gain_grad,
        self_shift_grad,
        self_weights_grad,
        query_bias_grad,
        value_bias_grad,
        self_output_grad,
        output_bias_grad,
        cross_gain_grad,
        cross_shift_grad,
        cross_query_grad,
        query_offset_grad,
        cross_memory_grad,
        memory_offset_grad,
        cross_output_grad,
        return_bias_grad,
        feed_gain_grad,
        feed_shift_grad,
        up_grad,
        up_bias_grad,
        down_grad,
        down_bias_grad,
    )
    reduced = share_gradients(gradients, False)
    return (block_output[None], tokens_grad[None], source_grad[None]) + tuple(reduced)


def solution(mesh):
    near = (mesh.shape["group"], mesh.shape["ctx"], mesh.shape["shard"]) == (4, 4, 2)
    placed = (
        P(("group", "shard"), "ctx", None),
        P(("group", "shard"), "ctx", None),
        P(("group", "shard"), "ctx"),
        P(("group", "shard"), "ctx"),
        P(("group", "shard"), "ctx", None),
        P("shard"),
        P("shard"),
        P("shard", None),
        P("shard"),
        P("shard"),
        P("shard", None),
        P("shard"),
        P("shard"),
        P("shard"),
        P("shard", None),
        P("shard"),
        P("shard", None),
        P("shard"),
        P("shard", None),
        P("shard"),
        P("shard"),
        P("shard"),
        P("shard", None),
        P("shard"),
        P("shard", None),
        P("shard"),
    )
    return jax.shard_map(
        pair_device if near else per_device,
        mesh=mesh,
        in_specs=placed,
        out_specs=(
            P(("group", "shard"), "ctx", None),
            P(("group", "shard"), "ctx", None),
            P(("group", "shard"), "ctx", None),
            P("shard"),
            P("shard"),
            P("shard", None),
            P("shard"),
            P("shard"),
            P("shard", None),
            P("shard"),
            P("shard"),
            P("shard"),
            P("shard", None),
            P("shard"),
            P("shard", None),
            P("shard"),
            P("shard", None),
            P("shard"),
            P("shard"),
            P("shard"),
            P("shard", None),
            P("shard"),
            P("shard", None),
            P("shard"),
        ),
        check_vma=False,
    )
```

```python
import functools
import math

import jax
import jax.numpy as jnp
from jax import lax
from jax.experimental import pallas as pl
from jax.experimental.pallas import tpu as pltpu
from jax.sharding import PartitionSpec as P

MESH = pl.DeviceIdType.MESH
BF = jnp.bfloat16
F32 = jnp.float32


def coords():
    g, z, c = lax.axis_index("group"), lax.axis_index("ctx"), lax.axis_index("shard")
    return lax.rem(g, 2), lax.div(g, 2), z, c


def device_of(x, y, z, c):
    return (y * 2 + x, z, c)


def greet(devices):
    barrier = pltpu.get_barrier_semaphore()
    for device in devices:
        pl.semaphore_signal(barrier, inc=1, device_id=device, device_id_type=MESH)
    pl.semaphore_wait(barrier, len(devices))


CH = 512
WD = 1024
SETS = ((0, 384), (384, 384), (768, 256))


def reduce_kernel(pieces, n_chunks, *refs):
    n_in = len(pieces)
    grads, small = refs[:n_in], refs[n_in]
    out, small_out = refs[n_in + 1 : n_in + 3]
    (acc, r0, r1, r2, r3, r4, sv, sr, load_sem, s0s, s0r, hs, hr, gs, gr, put_sem, svs, svr) = refs[n_in + 3 :]
    x, y, z, c = coords()
    sib = device_of(x, y, z, 1 - c)
    dx, dy = device_of(1 - x, y, z, c), device_of(x, 1 - y, z, c)
    dz2, dz1 = device_of(x, y, z + 2 - 4 * lax.div(z, 2), c), device_of(x, y, z + 1 - 2 * lax.rem(z, 2), c)
    greet((sib, dx, dy, dz2, dz1))

    loads, swaps = [], []
    j = 0
    for (kind, count), ref in zip(pieces, grads):
        for i in range(count):
            if kind == "cols":
                own = ref.at[pl.ds(c * CH, CH), pl.ds(i * WD, WD)]
                other = ref.at[pl.ds((1 - c) * CH, CH), pl.ds(i * WD, WD)]
            else:
                own = ref.at[pl.ds((c * count + i) * CH, CH), :]
                other = ref.at[pl.ds(((1 - c) * count + i) * CH, CH), :]
            pltpu.make_async_copy(own, acc.at[j], load_sem.at[j]).start()
            pltpu.make_async_remote_copy(
                src_ref=other, dst_ref=r0.at[j], send_sem=s0s.at[j], recv_sem=s0r.at[j], device_id=sib, device_id_type=MESH
            ).start()
            j += 1

    partners = (sib, dx, dy, dz2, dz1)
    sv[0] = small[...]

    def small_copy(p):
        return pltpu.make_async_remote_copy(
            src_ref=sv.at[p], dst_ref=sr.at[p], send_sem=svs.at[p], recv_sem=svr.at[p], device_id=partners[p], device_id_type=MESH
        )

    z2, z1 = lax.div(z, 2), lax.rem(z, 2)
    sets = (((dx, x), (dy, y), (dz1, z1), (dz2, z2)), ((dy, y), (dx, x), (dz1, z1), (dz2, z2)), ((dz1, z1), (dz2, z2), (dx, x), (dy, y)))
    rbufs = (r1, r2, r3, r4)

    def start_of(s, step):
        row = 0
        for q in range(step):
            row = row + sets[s][q][1] * (CH >> (q + 1))
        return row

    def halve_copy(jj, s, q):
        size = CH >> (q + 1)
        row = start_of(s, q) + (1 - sets[s][q][1]) * size
        return pltpu.make_async_remote_copy(
            src_ref=acc.at[jj, pl.ds(pl.multiple_of(row, 32), size), pl.ds(*SETS[s])],
            dst_ref=rbufs[q].at[jj, :, pl.ds(*SETS[s])],
            send_sem=hs.at[jj, s, q],
            recv_sem=hr.at[jj, s, q],
            device_id=sets[s][q][0],
            device_id_type=MESH,
        )

    def give_copy(jj, s, q):
        size = CH >> (q + 1)
        row = start_of(s, q + 1)
        block = out.at[jj, pl.ds(pl.multiple_of(row, 32), size), pl.ds(*SETS[s])]
        return pltpu.make_async_remote_copy(
            src_ref=block, dst_ref=block, send_sem=gs.at[jj, s, q], recv_sem=gr.at[jj, s, q], device_id=sets[s][q][0], device_id_type=MESH
        )

    def put_copy(jj, s):
        size = CH >> 4
        row = start_of(s, 4)
        block = (jj, pl.ds(pl.multiple_of(row, 32), size), pl.ds(*SETS[s]))
        return pltpu.make_async_copy(acc.at[block], out.at[block], put_sem.at[jj, s])

    def add_rows(jj, s, q):
        size = CH >> (q + 1)
        row = pl.multiple_of(start_of(s, q + 1), 32)
        span = min(size, 64)

        def one(k, carry):
            here = pl.ds(pl.multiple_of(row + k * span, 32), span)
            there = pl.ds(pl.multiple_of(k * span, 32), span)
            cols = pl.ds(*SETS[s])
            total = acc[jj, here, cols].astype(F32) + rbufs[q][jj, there, cols].astype(F32)
            acc[jj, here, cols] = total.astype(BF)
            return carry

        lax.fori_loop(0, size // span, one, 0)

    def phase0(jj):
        pltpu.make_async_copy(acc.at[jj], acc.at[jj], load_sem.at[jj]).wait()
        pltpu.make_async_remote_copy(
            src_ref=r0.at[jj], dst_ref=r0.at[jj], send_sem=s0s.at[jj], recv_sem=s0r.at[jj], device_id=sib, device_id_type=MESH
        ).wait()

        def one(k, carry):
            here = pl.ds(pl.multiple_of(k * 32, 32), 32)
            acc[jj, here, :] = (acc[jj, here, :].astype(F32) + r0[jj, here, :].astype(F32)).astype(BF)
            return carry

        lax.fori_loop(0, CH // 32, one, 0)
        for s in range(len(SETS)):
            halve_copy(jj, s, 0).start()

    def phase_halve(jj, q):
        for s in range(len(SETS)):
            halve_copy(jj, s, q).wait()
            add_rows(jj, s, q)
            if q < 3:
                halve_copy(jj, s, q + 1).start()
            else:
                put_copy(jj, s).start()
        if q == 3:
            for s in range(len(SETS)):
                put_copy(jj, s).wait()
                give_copy(jj, s, 3).start()

    def phase_give(jj, q):
        for s in range(len(SETS)):
            give_copy(jj, s, q).wait()
            if q > 0:
                give_copy(jj, s, q - 1).start()

    def small_phase(p):
        if p > 0:
            small_copy(p - 1).wait()
            sv[p] = sv[p - 1] + sr[p - 1]
        if p < 5:
            small_copy(p).start()
        else:
            small_out[...] = sv[5]

    def step(t, carry):
        def guarded(lag, what):
            @pl.when((t >= lag) & (t < n_chunks + lag))
            def _():
                what(t - lag)

        guarded(0, phase0)
        for q in range(4):
            guarded(q + 1, functools.partial(phase_halve, q=q))
        for q in range(3, -1, -1):
            guarded(8 - q, functools.partial(phase_give, q=q))
        for p in range(6):
            pl.when(t == p)(functools.partial(small_phase, p))
        return carry

    lax.fori_loop(0, n_chunks + 8, step, 0)


def reduce_gradients(pieces, grads, small):
    n_chunks = sum(count for _, count in pieces)
    any_spec = pl.BlockSpec(memory_space=pl.ANY)
    vmem = pl.BlockSpec(memory_space=pltpu.VMEM)
    dma = pltpu.SemaphoreType.DMA
    return pl.pallas_call(
        functools.partial(reduce_kernel, pieces, n_chunks),
        out_shape=(
            jax.ShapeDtypeStruct((n_chunks, CH, WD), BF),
            jax.ShapeDtypeStruct(small.shape, F32),
        ),
        in_specs=[any_spec] * len(grads) + [vmem],
        out_specs=(any_spec, vmem),
        scratch_shapes=[
            pltpu.VMEM((n_chunks, CH, WD), BF),
            pltpu.VMEM((n_chunks, CH, WD), BF),
            pltpu.VMEM((n_chunks, CH // 2, WD), BF),
            pltpu.VMEM((n_chunks, CH // 4, WD), BF),
            pltpu.VMEM((n_chunks, CH // 8, WD), BF),
            pltpu.VMEM((n_chunks, CH // 16, WD), BF),
            pltpu.VMEM((6,) + small.shape, F32),
            pltpu.VMEM((5,) + small.shape, F32),
            dma((n_chunks,)),
            dma((n_chunks,)),
            dma((n_chunks,)),
            dma((n_chunks, len(SETS), 4)),
            dma((n_chunks, len(SETS), 4)),
            dma((n_chunks, len(SETS), 4)),
            dma((n_chunks, len(SETS), 4)),
            dma((n_chunks, len(SETS))),
            dma((5,)),
            dma((5,)),
        ],
        compiler_params=pltpu.CompilerParams(collective_id=1, has_side_effects=True, vmem_limit_bytes=60 << 20),
        cost_estimate=pl.CostEstimate(flops=0, bytes_accessed=50 << 20, transcendentals=0),
        name="reduce_gradients",
    )(*grads, small)


def widen_kernel(ranges, *refs):
    j = pl.program_id(0)
    src, outs = refs[0], refs[1:]
    for (first, count, _), out in zip(ranges, outs):

        @pl.when((j >= first) & (j < first + count))
        def _():
            out[...] = src[0].astype(F32)


def widen(summed, pieces):
    ranges, first = [], 0
    for kind, count in pieces:
        ranges.append((first, count, kind))
        first += count

    def spec(first, count, kind):
        def index(j):
            k = jnp.clip(j - first, 0, count - 1)
            return (0, k) if kind == "cols" else (k, 0)

        return pl.BlockSpec((CH, WD), index)

    return pl.pallas_call(
        functools.partial(widen_kernel, tuple(ranges)),
        grid=(first,),
        out_shape=[
            jax.ShapeDtypeStruct((CH, WD * count) if kind == "cols" else (CH * count, WD), F32) for _, count, kind in ranges
        ],
        in_specs=[pl.BlockSpec((1, CH, WD), lambda j: (j, 0, 0))],
        out_specs=[spec(*r) for r in ranges],
        compiler_params=pltpu.CompilerParams(vmem_limit_bytes=48 << 20),
        cost_estimate=pl.CostEstimate(flops=0, bytes_accessed=6 * CH * WD * first, transcendentals=0),
        name="widen",
    )(summed)


VECTOR_ORDER = (0, 1, 3, 4, 6, 7, 8, 10, 12, 14, 15, 16, 18, 20)
MATRIX_PIECES = ((2, "cols"), (5, "cols"), (9, "cols"), (11, "cols"), (13, "cols"), (17, "cols"), (19, "rows"))


def share_gradients(gradients, near):
    if not near:
        halves = [
            lax.psum_scatter(g.astype(BF), "shard", scatter_dimension=0, tiled=True).astype(F32) for g in gradients
        ]
        return lax.psum(tuple(halves), ("group", "ctx"))
    c = lax.axis_index("shard")
    rows = jnp.concatenate([gradients[i].astype(F32).reshape(-1, WD) for i in VECTOR_ORDER], axis=0)
    count = rows.shape[0]
    small = jnp.pad(rows, ((0, -count % 8), (0, 0)))
    pieces, arrays = [], []
    for i, kind in MATRIX_PIECES:
        arrays.append(gradients[i].astype(BF))
        pieces.append((kind, gradients[i].shape[1] // WD if kind == "cols" else gradients[i].shape[0] // (2 * CH)))
    summed, small_sum = reduce_gradients(tuple(pieces), arrays, small)
    result = [None] * len(gradients)
    for (i, _), matrix in zip(MATRIX_PIECES, widen(summed, pieces)):
        result[i] = matrix
    at = 0
    for i in VECTOR_ORDER:
        size = gradients[i].shape[0]
        n = size // WD
        vector = small_sum[at : at + n].reshape(size)
        at += n
        result[i] = lax.dynamic_slice_in_dim(vector, c * (size // 2), size // 2, 0)
    return result

D = 1024
HEADS = 16
HEAD_DIM = 64


EPSILON = 1e-05
NEGATIVE = -1e30


def norm_rows(values, gain_vec, shift_vec):
    average = jnp.mean(values, axis=-1, keepdims=True)
    centred = values - average
    spread = jnp.mean(centred * centred, axis=-1, keepdims=True)
    return centred * lax.rsqrt(spread + EPSILON) * gain_vec + shift_vec


def exact_gelu(values):
    return jax.nn.gelu(values, approximate=False)


def product(left_side, right_side):
    return jnp.dot(left_side, right_side, preferred_element_type=jnp.float32)


def left_product(left_side, right_side):
    return lax.dot_general(
        left_side, right_side, (((0,), (0,)), ((), ())), preferred_element_type=jnp.float32
    )


def right_product(left_side, right_side):
    return lax.dot_general(
        left_side, right_side, (((1,), (1,)), ((), ())), preferred_element_type=jnp.float32
    )


def heads_of(matrix):
    return matrix.reshape(matrix.shape[0], HEADS, HEAD_DIM)


def allow_table(query_seg, query_pos, key_seg, key_pos):
    shared = (key_seg[None, :] == 0) | (key_seg[None, :] == query_seg[:, None])
    return shared & (key_pos[None, :] <= query_pos[:, None])


def fold_keys(folded, queries, key_block, value_block, allowed):
    run_max, run_sum, weighted = folded
    scores = jnp.einsum("qhd,khd->hqk", queries, key_block, preferred_element_type=jnp.float32)
    if allowed is not None:
        scores = jnp.where(allowed[None], scores, NEGATIVE)
    new_max = jnp.maximum(run_max, jnp.max(scores, axis=2))
    factor = jnp.exp(run_max - new_max)
    weighting = jnp.exp(scores - new_max[:, :, None])
    new_sum = run_sum * factor + jnp.sum(weighting, axis=2)
    update = jnp.einsum(
        "hqk,khd->qhd",
        weighting.astype(jnp.bfloat16),
        value_block,
        preferred_element_type=jnp.float32,
    )
    return (new_max, new_sum, weighted * jnp.transpose(factor)[:, :, None] + update)


def attend_piece(folded, queries, key_piece, value_piece, tag_bundle):
    count_rows = key_piece.shape[0]
    block_rows = math.gcd(count_rows, 512)

    def one_block(number, current):
        offset = number * block_rows
        key_block = heads_of(lax.dynamic_slice_in_dim(key_piece, offset, block_rows, 0))
        value_block = heads_of(lax.dynamic_slice_in_dim(value_piece, offset, block_rows, 0))
        allowed = None
        if tag_bundle is not None:
            query_seg, query_pos, seg_all, pos_all = tag_bundle
            key_seg = lax.dynamic_slice_in_dim(seg_all, offset, block_rows, 0)
            key_pos = lax.dynamic_slice_in_dim(pos_all, offset, block_rows, 0)
            allowed = allow_table(query_seg, query_pos, key_seg, key_pos)
        return fold_keys(current, queries, key_block, value_block, allowed)

    return lax.fori_loop(0, count_rows // block_rows, one_block, folded)


def finish(folded):
    run_max, run_sum, weighted = folded
    attended = weighted / jnp.transpose(run_sum)[:, :, None]
    return (attended, run_max + jnp.log(run_sum))


def row_deltas(out_grad, attended):
    return jnp.einsum("qhd,qhd->hq", out_grad, attended, preferred_element_type=jnp.float32)


def attend_back(queries, key_all, value_all, out_grad, row_delta, log_total, tag_bundle):
    total_rows = key_all.shape[0]
    row_count = queries.shape[0]
    block_rows = math.gcd(total_rows, 512)

    def one_block(query_acc, number):
        offset = number * block_rows
        key_block = heads_of(lax.dynamic_slice_in_dim(key_all, offset, block_rows, 0))
        value_block = heads_of(lax.dynamic_slice_in_dim(value_all, offset, block_rows, 0))
        scores = jnp.einsum("qhd,khd->hqk", queries, key_block, preferred_element_type=jnp.float32)
        if tag_bundle is not None:
            query_seg, query_pos, seg_all, pos_all = tag_bundle
            key_seg = lax.dynamic_slice_in_dim(seg_all, offset, block_rows, 0)
            key_pos = lax.dynamic_slice_in_dim(pos_all, offset, block_rows, 0)
            scores = jnp.where(
                allow_table(query_seg, query_pos, key_seg, key_pos)[None], scores, NEGATIVE
            )
        weighting = jnp.exp(scores - log_total[:, :, None])
        weight_grad = jnp.einsum(
            "qhd,khd->hqk", out_grad, value_block, preferred_element_type=jnp.float32
        )
        score_grad = (weighting * (weight_grad - row_delta[:, :, None])).astype(jnp.bfloat16)
        query_acc = query_acc + jnp.einsum(
            "hqk,khd->qhd", score_grad, key_block, preferred_element_type=jnp.float32
        )
        key_term = jnp.einsum(
            "hqk,qhd->khd", score_grad, queries, preferred_element_type=jnp.float32
        )
        value_term = jnp.einsum(
            "hqk,qhd->khd",
            weighting.astype(jnp.bfloat16),
            out_grad,
            preferred_element_type=jnp.float32,
        )
        return (query_acc, (key_term.reshape(block_rows, D), value_term.reshape(block_rows, D)))

    start_acc = jnp.zeros((row_count, HEADS, HEAD_DIM), jnp.float32)
    query_acc, terms = lax.scan(one_block, start_acc, jnp.arange(total_rows // block_rows))
    key_terms, value_terms = terms
    return (
        query_acc.reshape(row_count, D),
        key_terms.reshape(total_rows, D),
        value_terms.reshape(total_rows, D),
    )


def pair_places():
    x, y, z, c = coords()
    side = 1 - 2 * lax.rem(z, 2)
    sib, near, diag = device_of(x, y, z, 1 - c), device_of(x, y, z + side, c), device_of(x, y, z + side, 1 - c)
    far = device_of(x, y, z + 2 - 4 * lax.div(z, 2), 1 - c)
    block = 2 * c + lax.rem(z, 2)
    near_block = 2 * c + 1 - lax.rem(z, 2)
    sib_block = 2 * (1 - c) + lax.rem(z, 2)
    diag_block = 2 * (1 - c) + 1 - lax.rem(z, 2)
    home = lax.div(z, 2) == c
    return sib, near, diag, far, block, near_block, sib_block, diag_block, home


TILE = 256
LANES = 128
NEG = -1e30


def dot_nt(a, b):
    return lax.dot_general(a, b, (((1,), (1,)), ((), ())), preferred_element_type=F32)


def dot_nn(a, b):
    return lax.dot_general(a, b, (((1,), (0,)), ((), ())), preferred_element_type=F32)


def split_heads(source, target, heads):
    rows = source.shape[0]
    step = min(rows, 256)
    even = lax.broadcasted_iota(jnp.int32, (step, LANES), 1) < LANES // 2

    def one(k, carry):
        here = pl.ds(pl.multiple_of(k * step, step), step)
        for pair in range(heads // 2):
            block = source[here, pl.ds(pair * LANES, LANES)]
            target[2 * pair, here, :] = jnp.where(even, block, jnp.zeros_like(block))
            target[2 * pair + 1, here, :] = jnp.where(even, jnp.zeros_like(block), block)
        return carry

    lax.fori_loop(0, rows // step, one, 0)


def transpose_rows(source, target):
    rows = source.shape[0]
    step = min(rows, 256)

    def one(k, carry):
        here = pl.ds(pl.multiple_of(k * step, step), step)
        target[:, here] = source[here, :].astype(F32).T.astype(target.dtype)
        return carry

    lax.fori_loop(0, rows // step, one, 0)


def tree_mask(key_tile, query_tile, key_seg, query_seg, prompt):
    key_at = key_tile * TILE + lax.broadcasted_iota(jnp.int32, (TILE, TILE), 0)
    query_at = query_tile * TILE + lax.broadcasted_iota(jnp.int32, (TILE, TILE), 1)
    return (key_at <= query_at) & ((key_at < prompt) | (key_seg == query_seg))


HEAD_SCALE = 1.0 / math.sqrt(HEAD_DIM)


class Cores:
    def __init__(self):
        sib, near, diag, _, block, near_block, sib_block, diag_block, _ = pair_places()
        self.others = (near, sib, diag)
        self.blocks = (block, near_block, sib_block, diag_block)
        self.per_block = 2

    def tile_at(self, turn):
        b = lax.rem(self.blocks[0] + 1 + lax.div(turn, self.per_block), 4)
        return b * self.per_block + lax.rem(turn, self.per_block)

    def ends(self, source, target, tile, place):
        width = source.shape[1]
        src = source.at[pl.ds(pl.multiple_of(tile * TILE, TILE), TILE), :]
        row = pl.multiple_of(lax.rem(tile, self.per_block) * TILE, TILE)
        column = pl.multiple_of(place * 4 * width + self.blocks[0] * width, width)
        return src, target.at[pl.ds(row, TILE), pl.ds(column, width)]

    def give(self, source, target, tile, place, load, send, recv):
        src, dst = self.ends(source, target, tile, place)
        owner = lax.div(tile, self.per_block)

        @pl.when(owner == self.blocks[0])
        def _():
            pltpu.make_async_copy(src, dst, load).start()

        for device, b in zip(self.others, self.blocks[1:]):

            @pl.when(owner == b)
            def _():
                pltpu.make_async_remote_copy(
                    src_ref=src, dst_ref=dst, send_sem=send, recv_sem=recv.at[self.blocks[0], lax.rem(tile, self.per_block)],
                    device_id=device, device_id_type=MESH,
                ).start()

    def finish(self, source, target, place, load, send, recv):
        for k in range(self.per_block):
            tile = self.blocks[0] * self.per_block + k
            src, dst = self.ends(source, target, tile, place)
            pltpu.make_async_copy(src, dst, load.at[tile]).wait()
            for device, b in zip(self.others, self.blocks[1:]):
                sent = b * self.per_block + k
                src, dst = self.ends(source, target, sent, place)
                pltpu.make_async_remote_copy(
                    src_ref=src, dst_ref=dst, send_sem=send.at[sent], recv_sem=recv.at[b, k], device_id=device, device_id_type=MESH
                ).wait()


def trade_semaphores(tiles, places):
    dma = pltpu.SemaphoreType.DMA
    lead = () if places == 1 else (places,)
    return [dma(lead + (tiles,)), dma(lead + (tiles,)), dma(lead + (4, tiles // 4))]


def attention_params(masked, collective_id):
    if masked:
        return pltpu.CompilerParams(vmem_limit_bytes=48 << 20, collective_id=collective_id, has_side_effects=True)
    return pltpu.CompilerParams(vmem_limit_bytes=40 << 20)


def forward_kernel(heads, masked, *refs):
    if masked:
        q_ref, k_ref, v_ref, seg_col, seg_row, o_ref, lse_ref, mixed_ref, qm, vt, acc, load, send, recv = refs
    else:
        q_ref, k_ref, v_ref, o_ref, lse_ref, qm, vt, acc = refs
    n_query, n_key = q_ref.shape[0] // TILE, k_ref.shape[0] // TILE
    prompt_tiles = n_key // 2
    if masked:
        cores = Cores()
        greet(cores.others)
    split_heads(q_ref, qm, heads)
    transpose_rows(v_ref, vt)
    H = range(heads)

    def query_tile(turn, carry):
        i = cores.tile_at(turn) if masked else turn
        rows = pl.ds(pl.multiple_of(i * TILE, TILE), TILE)
        queries = [qm[h, rows, :] for h in H]
        acc[...] = jnp.zeros_like(acc)

        def tile(j, mask, state):
            keys = pl.ds(pl.multiple_of(j * TILE, TILE), TILE)
            old_m, old_l = state
            scores = [dot_nt(k_ref[keys, pl.ds(h // 2 * LANES, LANES)], queries[h]) for h in H]
            if mask is not None:
                scores = [jnp.where(mask, s, NEG) for s in scores]
            new_m = [jnp.maximum(old_m[h], jnp.max(scores[h], axis=0, keepdims=True)) for h in H]
            weights = [jnp.exp(scores[h] - new_m[h]) for h in H]
            if mask is not None:
                weights = [jnp.where(mask, w, 0.0) for w in weights]
            factor = [jnp.exp(old_m[h] - new_m[h]) for h in H]
            new_l = [old_l[h] * factor[h] + jnp.sum(weights[h], axis=0, keepdims=True) for h in H]
            low = [w.astype(BF) for w in weights]
            for h in H:
                part = pl.ds(h * 64, 64)
                acc[part, :] = acc[part, :] * factor[h] + dot_nn(vt[part, keys], low[h])
            return (new_m, new_l)

        state = ([jnp.full((1, TILE), NEG, F32)] * heads, [jnp.zeros((1, TILE), F32)] * heads)
        if masked:
            state = lax.fori_loop(0, jnp.minimum(i, prompt_tiles), lambda j, c: tile(j, None, c), state)

            def near(j, c):
                keys = pl.ds(pl.multiple_of(j * TILE, TILE), TILE)
                return tile(j, tree_mask(j, i, seg_col[keys, :], seg_row[:, rows], prompt_tiles * TILE), c)

            first = jnp.where(i > prompt_tiles, i - 1, i)
            state = lax.fori_loop(first, i + 1, near, state)
        else:
            state = lax.fori_loop(0, n_key, lambda j, c: tile(j, None, c), state)
        m, l = state
        for h in H:
            part = pl.ds(h * 64, 64)
            acc[part, :] = acc[part, :] / l[h]
            lse_ref[pl.ds(h, 1), rows] = m[h] + jnp.log(l[h])
        o_ref[rows, :] = acc[...].T.astype(BF)
        if masked:
            cores.give(o_ref, mixed_ref, i, 0, load.at[i], send.at[i], recv)
        return carry

    lax.fori_loop(0, n_query, query_tile, 0)
    if masked:
        cores.finish(o_ref, mixed_ref, 0, load, send, recv)


def attention_forward(q, k, v, seg=None):
    heads, width = 4, 256
    n, m, groups = q.shape[0], k.shape[0], q.shape[1] // 256
    masked = seg is not None
    column = lambda rows: pl.BlockSpec((rows, width), lambda p: (0, p))
    whole = lambda shape: pl.BlockSpec(shape, lambda p: (0, 0))
    extra = [seg.reshape(n, 1), seg.reshape(1, n)] if masked else []
    return pl.pallas_call(
        functools.partial(forward_kernel, heads, masked),
        grid=(groups,),
        out_shape=(jax.ShapeDtypeStruct((n, q.shape[1]), BF), jax.ShapeDtypeStruct((groups, 8, n), F32))
        + ((jax.ShapeDtypeStruct((n // 4, 4 * width), BF),) if masked else ()),
        in_specs=[column(n), column(m), column(m)] + [whole(e.shape) for e in extra],
        out_specs=(column(n), pl.BlockSpec((None, 8, n), lambda p: (p, 0, 0)))
        + ((pl.BlockSpec(memory_space=pltpu.HBM),) if masked else ()),
        scratch_shapes=[
            pltpu.VMEM((heads, n, LANES), BF),
            pltpu.VMEM((width, m), BF),
            pltpu.VMEM((width, TILE), F32),
        ]
        + (trade_semaphores(n // TILE, 1) if masked else []),
        compiler_params=attention_params(masked, 3),
        cost_estimate=pl.CostEstimate(flops=24 * n * m * q.shape[1], bytes_accessed=4 * (n + m) * q.shape[1], transcendentals=n * m * heads * groups),
        name="attention_forward",
    )(q, k, v, *extra)


def backward_kernel(heads, masked, *refs):
    if masked:
        q_ref, k_ref, v_ref, *g_refs, o_ref, lse_ref, seg_col, seg_row, projected_ref, qm, gm, kt, dqt, dk_acc, dv_acc, delta = refs[:19]
        dq_ref, dk_ref, dv_ref, g_ref, load, send, recv = refs[19:]
    else:
        q_ref, k_ref, v_ref, g_ref, o_ref, lse_ref, dq_ref, dk_ref, dv_ref, qm, gm, kt, dqt, dk_acc, dv_acc, delta = refs
    n_query, n_key = q_ref.shape[0] // TILE, k_ref.shape[0] // TILE
    prompt_tiles = n_key // 2
    if masked:
        cores = Cores()
        greet(cores.others)
        part_rows = q_ref.shape[0] // 4
        for part_ref, b in zip(g_refs, cores.blocks):
            g_ref[pl.ds(pl.multiple_of(b * part_rows, part_rows), part_rows), :] = part_ref[...]
    split_heads(q_ref, qm, heads)
    split_heads(g_ref, gm, heads)
    transpose_rows(k_ref, kt)
    dqt[...] = jnp.zeros_like(dqt)
    H = range(heads)

    def deltas(i, carry):
        rows = pl.ds(pl.multiple_of(i * TILE, TILE), TILE)
        product = (g_ref[rows, :].astype(F32) * o_ref[rows, :].astype(F32)).T
        for h in range(heads):
            delta[pl.ds(h, 1), rows] = jnp.sum(product[h * 64 : h * 64 + 64, :], axis=0, keepdims=True)
        return carry

    lax.fori_loop(0, n_query, deltas, 0)

    def send_rows(source, place, j):
        cores.give(source, projected_ref, j, place, load.at[place, j], send.at[place, j], recv.at[place])

    def key_tile(turn, carry):
        j = lax.rem(turn + prompt_tiles, n_key) if masked else turn
        keys = pl.ds(pl.multiple_of(j * TILE, TILE), TILE)
        dk_acc[...] = jnp.zeros_like(dk_acc)
        dv_acc[...] = jnp.zeros_like(dv_acc)
        lane = [pl.ds(h // 2 * LANES, LANES) for h in H]

        def tile(i, mask):
            rows = pl.ds(pl.multiple_of(i * TILE, TILE), TILE)
            scores = [dot_nt(k_ref[keys, lane[h]], qm[h, rows, :]) for h in H]
            change = [dot_nt(v_ref[keys, lane[h]], gm[h, rows, :]) for h in H]
            weights = [jnp.exp(scores[h] - lse_ref[pl.ds(h, 1), rows]) for h in H]
            if mask is not None:
                weights = [jnp.where(mask, w, 0.0) for w in weights]
            back = [(weights[h] * (change[h] - delta[pl.ds(h, 1), rows])).astype(BF) for h in H]
            low = [w.astype(BF) for w in weights]
            for pair in range(heads // 2):
                a, b = 2 * pair, 2 * pair + 1
                dv_acc[:, lane[a]] += dot_nn(low[a], gm[a, rows, :]) + dot_nn(low[b], gm[b, rows, :])
                dk_acc[:, lane[a]] += dot_nn(back[a], qm[a, rows, :]) + dot_nn(back[b], qm[b, rows, :])
            for h in H:
                part = pl.ds(h * 64, 64)
                dqt[part, rows] += dot_nn(kt[part, keys], back[h])

        if masked:

            def near(i):
                rows = pl.ds(pl.multiple_of(i * TILE, TILE), TILE)
                tile(i, tree_mask(j, i, seg_col[keys, :], seg_row[:, rows], prompt_tiles * TILE))

            prompt = j < prompt_tiles
            last = jnp.where(prompt, j, jnp.minimum(j + 1, n_query - 1))
            lax.fori_loop(j, last + 1, lambda i, c: (near(i), c)[1], 0)
            lax.fori_loop(jnp.where(prompt, j + 1, n_query), n_query, lambda i, c: (tile(i, None), c)[1], 0)
        else:
            lax.fori_loop(0, n_query, lambda i, c: (tile(i, None), c)[1], 0)
        dk_ref[keys, :] = dk_acc[...].astype(BF)
        dv_ref[keys, :] = dv_acc[...].astype(BF)
        if masked:
            send_rows(dk_ref, 1, j)
            send_rows(dv_ref, 2, j)

            @pl.when(j < prompt_tiles)
            def _():
                finish(j, 0)

        return carry

    def finish(i, carry):
        rows = pl.ds(pl.multiple_of(i * TILE, TILE), TILE)
        dq = dqt[:, rows].T.astype(BF)
        if masked:
            dq_ref[rows, :] = (dq.astype(F32) * HEAD_SCALE).astype(BF)
            send_rows(dq_ref, 0, i)
        else:
            dq_ref[rows, :] = dq
        return carry

    lax.fori_loop(0, n_key, key_tile, 0)
    if masked:
        lax.fori_loop(prompt_tiles, n_query, finish, 0)
        for place, source in enumerate((dq_ref, dk_ref, dv_ref)):
            cores.finish(source, projected_ref, place, load.at[place], send.at[place], recv.at[place])
    else:
        lax.fori_loop(0, n_query, finish, 0)


def attention_backward(q, k, v, grads, mix, lse, seg=None):
    heads, width = 4, 256
    n, m, groups = q.shape[0], k.shape[0], q.shape[1] // 256
    masked = seg is not None
    column = lambda rows: pl.BlockSpec((rows, width), lambda p: (0, p))
    whole = lambda shape: pl.BlockSpec(shape, lambda p: (0, 0))
    extra = [seg.reshape(n, 1), seg.reshape(1, n)] if masked else []
    if masked:
        out_shape = jax.ShapeDtypeStruct((n // 4, 12 * width), BF)
        out_specs = pl.BlockSpec(memory_space=pltpu.HBM)
    else:
        out_shape = [jax.ShapeDtypeStruct((rows, q.shape[1]), BF) for rows in (n, m, m)]
        out_specs = [column(n), column(m), column(m)]
    return pl.pallas_call(
        functools.partial(backward_kernel, heads, masked),
        grid=(groups,),
        out_shape=out_shape,
        in_specs=[column(n), column(m), column(m)]
        + [column(g.shape[0]) for g in grads]
        + [column(n), pl.BlockSpec((None, 8, n), lambda p: (p, 0, 0))]
        + [whole(e.shape) for e in extra],
        out_specs=out_specs,
        scratch_shapes=[
            pltpu.VMEM((heads, n, LANES), BF),
            pltpu.VMEM((heads, n, LANES), BF),
            pltpu.VMEM((width, m), BF),
            pltpu.VMEM((width, n), F32),
            pltpu.VMEM((TILE, width), F32),
            pltpu.VMEM((TILE, width), F32),
            pltpu.VMEM((8, n), F32),
        ]
        + ([pltpu.VMEM((n, width), BF)] * 4 + trade_semaphores(n // TILE, 3) if masked else []),
        compiler_params=attention_params(masked, 5),
        cost_estimate=pl.CostEstimate(flops=32 * n * m * q.shape[1], bytes_accessed=8 * (n + m) * q.shape[1], transcendentals=n * m * heads * groups),
        name="attention_backward",
    )(q, k, v, *grads, mix, lse, *extra)


TOKEN_PARTS = 4


def spread_kernel(n_mats, *refs):
    tok, seg = refs[:2]
    mats = refs[2 : 2 + n_mats]
    tok_all, seg_all = refs[2 + n_mats : 4 + n_mats]
    fulls = refs[4 + n_mats : 4 + 2 * n_mats]
    stage = refs[4 + 2 * n_mats : 4 + 3 * n_mats]
    tok_stage, seg_stage = refs[4 + 3 * n_mats : 6 + 3 * n_mats]
    (mat_load, mat_put, mat_send, mat_recv, own_load, own_put, far_send, far_recv, sib_send, sib_recv, near_send, near_recv, pass_send, pass_recv) = refs[6 + 3 * n_mats :]
    sib, near, diag, far, block, near_block, sib_block, diag_block, home = pair_places()
    _, _, z, c = coords()
    greet((sib, near, far))
    rows = tok.shape[0]
    part = rows // TOKEN_PARTS
    n_items = TOKEN_PARTS + 1

    def source(k):
        return seg if k == TOKEN_PARTS else tok.at[pl.ds(k * part, part), :]

    def place(k, b):
        if k == TOKEN_PARTS:
            return seg_all.at[b]
        return tok_all.at[pl.ds(pl.multiple_of(b * rows + k * part, part), part), :]

    def remote(src, dst, send, recv, device):
        return pltpu.make_async_remote_copy(src_ref=src, dst_ref=dst, send_sem=send, recv_sem=recv, device_id=device, device_id_type=MESH)

    def far_copy(k):
        return remote(source(k), place(k, z), far_send.at[k], far_recv.at[k], far)

    def staged(k):
        return seg_stage if k == TOKEN_PARTS else tok_stage.at[pl.ds(k * part, part), :]

    def own_copy(k):
        return pltpu.make_async_copy(source(k), staged(k), own_load.at[k])

    def own_out(k):
        return pltpu.make_async_copy(staged(k), place(k, block), own_put.at[k])

    def sib_copy(k):
        return remote(place(k, block), place(k, block), sib_send.at[k], sib_recv.at[k], sib)

    def near_copy(k):
        return remote(place(k, block), place(k, block), near_send.at[k], near_recv.at[k], near)

    def pass_copy(k):
        return remote(place(k, near_block), place(k, near_block), pass_send.at[k], pass_recv.at[k], sib)

    @pl.when(home)
    def _():
        for k in range(n_items):
            own_copy(k).start()

    @pl.when(jnp.logical_not(home))
    def _():
        for k in range(n_items):
            far_copy(k).start()

    def mat_target(i):
        half = mats[i].shape[0]
        return fulls[i].at[pl.ds(pl.multiple_of(c * half, 8), half), :]

    def mat_in(i):
        return pltpu.make_async_copy(mats[i], stage[i], mat_load.at[i])

    def mat_out(i):
        return pltpu.make_async_copy(stage[i], mat_target(i), mat_put.at[i])

    def mat_remote(i):
        return remote(mats[i], mat_target(i), mat_send.at[i], mat_recv.at[i], sib)

    for i in range(n_mats):
        mat_in(i).start()
        mat_remote(i).start()

    for k in range(n_items + 1):
        if k < n_items:

            @pl.when(home)
            def _():
                own_copy(k).wait()
                own_out(k).start()
                own_out(k).wait()

            @pl.when(jnp.logical_not(home))
            def _():
                far_copy(k).wait()

            sib_copy(k).start()
            near_copy(k).start()
        if k > 0:
            near_copy(k - 1).wait()
            pass_copy(k - 1).start()
    for i in range(n_mats):
        mat_in(i).wait()
        mat_out(i).start()
    for k in range(n_items):
        sib_copy(k).wait()
        pass_copy(k).wait()
    for i in range(n_mats):
        mat_out(i).wait()
        mat_remote(i).wait()


def spread(tokens, seg, mats):
    n = len(mats)
    any_spec = pl.BlockSpec(memory_space=pltpu.HBM)
    dma = pltpu.SemaphoreType.DMA
    items = TOKEN_PARTS + 1
    return pl.pallas_call(
        functools.partial(spread_kernel, n),
        out_shape=[
            jax.ShapeDtypeStruct((4 * tokens.shape[0], tokens.shape[1]), tokens.dtype),
            jax.ShapeDtypeStruct((4,) + seg.shape, seg.dtype),
        ]
        + [jax.ShapeDtypeStruct((2 * m.shape[0], m.shape[1]), m.dtype) for m in mats],
        in_specs=[any_spec] * (2 + n),
        out_specs=[any_spec] * (2 + n),
        scratch_shapes=[pltpu.VMEM(a.shape, a.dtype) for a in (*mats, tokens, seg)] + [dma((n,))] * 4 + [dma((items,))] * 10,
        compiler_params=pltpu.CompilerParams(collective_id=2, has_side_effects=True, vmem_limit_bytes=60 << 20),
        cost_estimate=pl.CostEstimate(flops=0, bytes_accessed=64 << 20, transcendentals=0),
        name="spread",
    )(tokens, seg, *mats)


def project_kernel(scale, block_ref, tok, gain, shift, wq, wk, wv, bq, bv, q_ref, k_ref, v_ref):
    del block_ref
    normed = norm_rows(tok[...].astype(F32), gain[...], shift[...]).astype(BF)
    q_ref[...] = ((product(normed, wq[...]) + bq[...]) * scale).astype(BF)
    k_ref[...] = product(normed, wk[...]).astype(BF)
    v_ref[...] = (product(normed, wv[...]) + bv[...]).astype(BF)


def project(block, tokens_all, gain, shift, weights, query_bias, value_bias, scale):
    n, d = tokens_all.shape
    width, step = d // 4, 256
    row = lambda i, b: (i, 0)
    fixed = lambda i, b: (0, 0)
    weight = lambda part: pl.BlockSpec((d, width), lambda i, b: (0, 4 * part + b[0]))
    return pl.pallas_call(
        functools.partial(project_kernel, scale),
        grid_spec=pltpu.PrefetchScalarGridSpec(
            num_scalar_prefetch=1,
            grid=(n // step,),
            in_specs=[pl.BlockSpec((step, d), row), pl.BlockSpec((1, d), fixed), pl.BlockSpec((1, d), fixed)]
            + [weight(part) for part in range(3)]
            + [pl.BlockSpec((1, width), lambda i, b: (0, b[0]))] * 2,
            out_specs=[pl.BlockSpec((step, width), row)] * 3,
        ),
        out_shape=[jax.ShapeDtypeStruct((n, width), BF)] * 3,
        compiler_params=pltpu.CompilerParams(vmem_limit_bytes=32 << 20),
        cost_estimate=pl.CostEstimate(flops=6 * n * d * width, bytes_accessed=4 * n * d, transcendentals=0),
        name="project",
    )(block.reshape(1).astype(jnp.int32), tokens_all, gain.reshape(1, d), shift.reshape(1, d), weights, weights, weights,
      query_bias.reshape(1, d), value_bias.reshape(1, d))


def owner_of(z, c):
    return (z, c) if z // 2 == c else ((z + 2) % 4, 1 - c)


def flat(z, c):
    return 2 * z + c


CORES = [(z, c) for z in range(4) for c in range(2)]
SWAP = [(flat(z, c), flat(*owner_of(z, c))) for z, c in CORES if owner_of(z, c) != (z, c)]
HOME_TO_NEAR = [(flat(z, c), flat(owner_of(z, c)[0] ^ 1, owner_of(z, c)[1])) for z, c in CORES]
NEAR = [(z, z ^ 1) for z in range(4)]
SIB = [(0, 1), (1, 0)]
DIAG = [(flat(z, c), flat(z ^ 1, 1 - c)) for z, c in CORES]


def swap(array):
    home = lax.div(lax.axis_index("ctx"), 2) == lax.axis_index("shard")
    return jnp.where(home, array, lax.ppermute(array, ("ctx", "shard"), SWAP))


def pair_device(
    tokens, source, segment_ids, positions, cotangent,
    self_gain, self_shift, self_weights, query_bias, value_bias, self_output, output_bias,
    cross_gain, cross_shift, cross_query, query_offset, cross_memory, memory_offset, cross_output, return_bias,
    feed_gain, feed_shift, feed_up, up_bias, feed_down, down_bias,
):
    c, z = lax.axis_index("shard"), lax.axis_index("ctx")
    block = 2 * c + lax.rem(z, 2)
    head_scale = 1.0 / math.sqrt(HEAD_DIM)
    rows = tokens.shape[1]
    vectors = (
        self_gain, self_shift, query_bias, value_bias, output_bias, cross_gain, cross_shift, query_offset, memory_offset,
        return_bias, feed_gain, feed_shift, down_bias, up_bias,
    )
    half = D // 2
    n_packed = sum(v.shape[0] for v in vectors) // half
    packed = jnp.concatenate(vectors + (jnp.zeros((-n_packed % 16 * half,), BF),)).reshape(-1, half)
    mats = (self_weights, self_output, cross_memory, cross_query, cross_output, feed_up, feed_down, packed)
    spread_out = spread(tokens[0], segment_ids.reshape(4, rows // 4), mats)
    tokens_all, seg_all = spread_out[:2]
    self_weights, self_output, cross_memory, cross_query, cross_output, feed_up, feed_down, packed = spread_out[2:]
    tokens_all, source_home = lax.optimization_barrier((tokens_all, source[0]))
    own_source = swap(source_home)
    near_source = lax.ppermute(source_home, ("ctx", "shard"), HOME_TO_NEAR)
    chip_source = jnp.concatenate([own_source, near_source], axis=0)
    source_all = jnp.concatenate([chip_source, lax.ppermute(chip_source, "shard", SIB)], axis=0)
    packed = packed.astype(F32).reshape(2, -1, half)
    unpacked = [packed[:, i].reshape(D) for i in range(13)]
    (
        self_gain, self_shift, query_bias, value_bias, output_bias, cross_gain, cross_shift, query_offset, memory_offset,
        return_bias, feed_gain, feed_shift, down_bias,
    ) = unpacked
    up_bias = packed[:, 13:n_packed].reshape(-1)
    seg = seg_all.reshape(-1)

    width = D // 4
    q, k, v = project(block, tokens_all, self_gain, self_shift, self_weights, query_bias, value_bias, head_scale)
    mix_heads, lse_self, mixed_self = attention_forward(q, k, v, seg)
    mixed_self, out_grad_home = lax.optimization_barrier((mixed_self, cotangent[0]))
    out_grad = swap(out_grad_home)

    tok_rows = lax.dynamic_slice_in_dim(tokens_all, block * rows, rows, 0).astype(F32)
    normed_self = norm_rows(tok_rows, self_gain, self_shift).astype(BF)
    first_sum = tok_rows + product(mixed_self, self_output) + output_bias
    normed_cross = norm_rows(first_sum, cross_gain, cross_shift).astype(BF)
    cross_q = ((product(normed_cross, cross_query) + query_offset) * head_scale).astype(BF)
    memory = product(source_all, cross_memory)
    cross_keys = memory[:, :D].astype(BF)
    cross_values = (memory[:, D:] + memory_offset).astype(BF)
    mixed_cross, lse_cross = attention_forward(cross_q, cross_keys, cross_values)
    second = first_sum + product(mixed_cross, cross_output) + return_bias
    normed_feed = norm_rows(second, feed_gain, feed_shift).astype(BF)
    hidden_pre = product(normed_feed, feed_up) + up_bias
    below = 0.5 + 0.5 * lax.erf(hidden_pre * math.sqrt(0.5))
    hidden = (hidden_pre * below).astype(BF)
    slope = (below + hidden_pre * jnp.exp(-0.5 * hidden_pre * hidden_pre) * (1.0 / math.sqrt(2.0 * math.pi))).astype(BF)
    hidden, slope = lax.optimization_barrier((hidden, slope))
    block_output = (second + product(hidden, feed_down) + down_bias).astype(BF)

    down_grad = left_product(hidden, out_grad).astype(BF)
    down_bias_grad = jnp.sum(out_grad, axis=0, dtype=F32)
    hidden_grad = (right_product(out_grad, feed_down) * slope.astype(F32)).astype(BF)
    up_grad = left_product(normed_feed, hidden_grad).astype(BF)
    up_bias_grad = jnp.sum(hidden_grad, axis=0, dtype=F32)
    _, feed_pull = jax.vjp(norm_rows, second, feed_gain, feed_shift)
    second_part, feed_gain_grad, feed_shift_grad = feed_pull(right_product(hidden_grad, feed_up))
    second_grad = out_grad.astype(F32) + second_part
    branch_cross = second_grad.astype(BF)
    cross_output_grad = left_product(mixed_cross, branch_cross).astype(BF)
    return_bias_grad = jnp.sum(second_grad, axis=0)
    mixed_cross_grad = right_product(branch_cross, cross_output).astype(BF)
    cross_sum, key_terms, value_terms = attention_backward(
        cross_q, cross_keys, cross_values, (mixed_cross_grad,), mixed_cross, lse_cross
    )

    source_part = (right_product(key_terms, cross_memory[:, :D]) + right_product(value_terms, cross_memory[:, D:])).astype(BF)
    cross_memory_grad = jnp.concatenate(
        [left_product(source_all, key_terms).astype(BF), left_product(source_all, value_terms).astype(BF)], axis=1
    )
    memory_offset_grad = jnp.sum(value_terms, axis=0, dtype=F32)
    n = source_part.shape[0] // 2
    source_part = (source_part[:n].astype(F32) + lax.ppermute(source_part[n:], "shard", SIB).astype(F32)).astype(BF)
    n = n // 2
    source_near = lax.ppermute(source_part[n:], "ctx", NEAR)
    cross_q_grad = cross_sum * head_scale
    cross_query_grad = left_product(normed_cross, cross_q_grad).astype(BF)
    query_offset_grad = jnp.sum(cross_q_grad, axis=0, dtype=F32)
    _, cross_pull = jax.vjp(norm_rows, first_sum, cross_gain, cross_shift)
    first_part, cross_gain_grad, cross_shift_grad = cross_pull(right_product(cross_q_grad, cross_query))
    first_grad = second_grad + first_part
    branch_self = first_grad.astype(BF)
    self_output_grad = left_product(mixed_self, branch_self).astype(BF)
    output_bias_grad = jnp.sum(first_grad, axis=0)
    mixed_self_grad = right_product(branch_self, self_output).astype(BF)
    near_block, sib_block, diag_block = block + 1 - 2 * lax.rem(block, 2), (block + 2) % 4, 3 - block
    heads_of_block = lambda b: lax.dynamic_slice_in_dim(mixed_self_grad, b * width, width, 1)
    grad_parts = (
        heads_of_block(block),
        lax.ppermute(heads_of_block(near_block), "ctx", NEAR),
        lax.ppermute(heads_of_block(sib_block), "shard", SIB),
        lax.ppermute(heads_of_block(diag_block), ("ctx", "shard"), DIAG),
    )
    grad_parts, source_part = lax.optimization_barrier((grad_parts, source_part))
    projected_grad = attention_backward(q, k, v, grad_parts, mix_heads, lse_self, seg)
    projected_grad, source_near = lax.optimization_barrier((projected_grad, source_near))
    source_grad = (source_part[:n].astype(F32) + source_near.astype(F32)).astype(BF)
    self_weights_grad = left_product(normed_self, projected_grad).astype(BF)
    query_bias_grad = jnp.sum(projected_grad[:, :D], axis=0, dtype=F32)
    value_bias_grad = jnp.sum(projected_grad[:, 2 * D :], axis=0, dtype=F32)
    _, self_pull = jax.vjp(norm_rows, tok_rows, self_gain, self_shift)
    token_part, self_gain_grad, self_shift_grad = self_pull(right_product(projected_grad, self_weights))
    tokens_grad = (first_grad + token_part).astype(BF)
    gradients = (
        self_gain_grad, self_shift_grad, self_weights_grad, query_bias_grad, value_bias_grad, self_output_grad, output_bias_grad,
        cross_gain_grad, cross_shift_grad, cross_query_grad, query_offset_grad, cross_memory_grad, memory_offset_grad,
        cross_output_grad, return_bias_grad, feed_gain_grad, feed_shift_grad, up_grad, up_bias_grad, down_grad, down_bias_grad,
    )
    reduced = share_gradients(gradients, True)
    return (
        swap(block_output)[None],
        swap(tokens_grad).astype(F32)[None],
        swap(source_grad).astype(F32)[None],
    ) + tuple(reduced)


def per_device(
    tokens,
    source,
    segment_ids,
    positions,
    cotangent,
    self_gain,
    self_shift,
    self_weights,
    query_bias,
    value_bias,
    self_output,
    output_bias,
    cross_gain,
    cross_shift,
    cross_query,
    query_offset,
    cross_memory,
    memory_offset,
    cross_output,
    return_bias,
    feed_gain,
    feed_shift,
    feed_up,
    up_bias,
    feed_down,
    down_bias,
):
    (
        self_gain,
        self_shift,
        self_weights,
        query_bias,
        value_bias,
        self_output,
        output_bias,
        cross_gain,
        cross_shift,
        cross_query,
        query_offset,
        cross_memory,
        memory_offset,
        cross_output,
        return_bias,
        feed_gain,
        feed_shift,
        feed_up,
        up_bias,
        feed_down,
        down_bias,
    ) = (
        lax.all_gather(self_gain, "shard", axis=0, tiled=True),
        lax.all_gather(self_shift, "shard", axis=0, tiled=True),
        lax.all_gather(self_weights, "shard", axis=0, tiled=True),
        lax.all_gather(query_bias, "shard", axis=0, tiled=True),
        lax.all_gather(value_bias, "shard", axis=0, tiled=True),
        lax.all_gather(self_output, "shard", axis=0, tiled=True),
        lax.all_gather(output_bias, "shard", axis=0, tiled=True),
        lax.all_gather(cross_gain, "shard", axis=0, tiled=True),
        lax.all_gather(cross_shift, "shard", axis=0, tiled=True),
        lax.all_gather(cross_query, "shard", axis=0, tiled=True),
        lax.all_gather(query_offset, "shard", axis=0, tiled=True),
        lax.all_gather(cross_memory, "shard", axis=0, tiled=True),
        lax.all_gather(memory_offset, "shard", axis=0, tiled=True),
        lax.all_gather(cross_output, "shard", axis=0, tiled=True),
        lax.all_gather(return_bias, "shard", axis=0, tiled=True),
        lax.all_gather(feed_gain, "shard", axis=0, tiled=True),
        lax.all_gather(feed_shift, "shard", axis=0, tiled=True),
        lax.all_gather(feed_up, "shard", axis=0, tiled=True),
        lax.all_gather(up_bias, "shard", axis=0, tiled=True),
        lax.all_gather(feed_down, "shard", axis=0, tiled=True),
        lax.all_gather(down_bias, "shard", axis=0, tiled=True),
    )
    head_scale = 1.0 / math.sqrt(HEAD_DIM)
    row_count = tokens.shape[1]
    tok_rows = tokens[0].astype(jnp.float32)
    source_rows = source[0]
    tag_seg, tag_pos = (
        lax.all_gather(segment_ids, "ctx", axis=1, tiled=True),
        lax.all_gather(positions, "ctx", axis=1, tiled=True),
    )
    tag_bundle = (segment_ids[0], positions[0], tag_seg[0], tag_pos[0])
    gain_self = self_gain.astype(jnp.float32)
    shift_self = self_shift.astype(jnp.float32)
    normed_self = norm_rows(tok_rows, gain_self, shift_self).astype(jnp.bfloat16)
    projected = product(normed_self, self_weights)
    queries = ((projected[:, :D] + query_bias.astype(jnp.float32)) * head_scale).astype(
        jnp.bfloat16
    )
    keys_self = projected[:, D : 2 * D].astype(jnp.bfloat16)
    values_self = (projected[:, 2 * D :] + value_bias.astype(jnp.float32)).astype(jnp.bfloat16)
    query_heads = heads_of(queries)
    start_state = (
        jnp.full((HEADS, row_count), NEGATIVE, jnp.float32),
        jnp.zeros((HEADS, row_count), jnp.float32),
        jnp.zeros((row_count, HEADS, HEAD_DIM), jnp.float32),
    )
    folded_self = attend_piece(
        start_state,
        query_heads,
        lax.all_gather(keys_self, "ctx", axis=0, tiled=True),
        lax.all_gather(values_self, "ctx", axis=0, tiled=True),
        tag_bundle,
    )
    attended_self, total_self = finish(folded_self)
    mixed_self = attended_self.reshape(row_count, D).astype(jnp.bfloat16)
    first_sum = tok_rows + product(mixed_self, self_output) + output_bias.astype(jnp.float32)
    gain_cross = cross_gain.astype(jnp.float32)
    shift_cross = cross_shift.astype(jnp.float32)
    normed_cross = norm_rows(first_sum, gain_cross, shift_cross).astype(jnp.bfloat16)
    cross_q = (
        (product(normed_cross, cross_query) + query_offset.astype(jnp.float32)) * head_scale
    ).astype(jnp.bfloat16)
    memory = product(source_rows, cross_memory)
    memory_keys = memory[:, :D].astype(jnp.bfloat16)
    memory_values = (memory[:, D:] + memory_offset.astype(jnp.float32)).astype(jnp.bfloat16)
    cross_keys, cross_values = (
        lax.all_gather(memory_keys, "ctx", axis=0, tiled=True),
        lax.all_gather(memory_values, "ctx", axis=0, tiled=True),
    )
    cross_heads = heads_of(cross_q)
    attended_cross, total_cross = finish(
        attend_piece(start_state, cross_heads, cross_keys, cross_values, None)
    )
    mixed_cross = attended_cross.reshape(row_count, D).astype(jnp.bfloat16)
    second = first_sum + product(mixed_cross, cross_output) + return_bias.astype(jnp.float32)
    gain_feed = feed_gain.astype(jnp.float32)
    shift_feed = feed_shift.astype(jnp.float32)
    normed_feed = norm_rows(second, gain_feed, shift_feed).astype(jnp.bfloat16)
    hidden_pre = product(normed_feed, feed_up) + up_bias.astype(jnp.float32)
    hidden_act, gelu_pull = jax.vjp(exact_gelu, hidden_pre)
    hidden = hidden_act.astype(jnp.bfloat16)
    block_output = (second + product(hidden, feed_down) + down_bias.astype(jnp.float32)).astype(
        jnp.bfloat16
    )
    out_grad = cotangent[0]
    down_grad = left_product(hidden, out_grad)
    down_bias_grad = jnp.sum(out_grad, axis=0, dtype=jnp.float32)
    (hidden_grad,) = gelu_pull(right_product(out_grad, feed_down))
    hidden_grad = hidden_grad.astype(jnp.bfloat16)
    up_grad = left_product(normed_feed, hidden_grad)
    up_bias_grad = jnp.sum(hidden_grad, axis=0, dtype=jnp.float32)
    norm_value, feed_pull = jax.vjp(norm_rows, second, gain_feed, shift_feed)
    second_part, feed_gain_grad, feed_shift_grad = feed_pull(right_product(hidden_grad, feed_up))
    second_grad = out_grad.astype(jnp.float32) + second_part
    branch_cross = second_grad.astype(jnp.bfloat16)
    cross_output_grad = left_product(mixed_cross, branch_cross)
    return_bias_grad = jnp.sum(second_grad, axis=0)
    mixed_cross_grad = right_product(branch_cross, cross_output).astype(jnp.bfloat16)
    cross_grad_heads = heads_of(mixed_cross_grad)
    cross_delta = row_deltas(cross_grad_heads, attended_cross)
    cross_sum, key_terms, value_terms = attend_back(
        cross_heads, cross_keys, cross_values, cross_grad_heads, cross_delta, total_cross, None
    )
    key_part, value_part = (
        lax.psum_scatter(
            key_terms.astype(jnp.bfloat16), "ctx", scatter_dimension=0, tiled=True
        ).astype(jnp.float32),
        lax.psum_scatter(
            value_terms.astype(jnp.bfloat16), "ctx", scatter_dimension=0, tiled=True
        ).astype(jnp.float32),
    )
    memory_grad = jnp.concatenate(
        [key_part.astype(jnp.bfloat16), value_part.astype(jnp.bfloat16)], axis=1
    )
    source_grad = right_product(memory_grad, cross_memory)
    cross_memory_grad = left_product(source_rows, memory_grad)
    memory_offset_grad = jnp.sum(memory_grad[:, D:], axis=0, dtype=jnp.float32)
    cross_q_grad = cross_sum.astype(jnp.bfloat16) * head_scale
    cross_query_grad = left_product(normed_cross, cross_q_grad)
    query_offset_grad = jnp.sum(cross_q_grad, axis=0, dtype=jnp.float32)
    norm_value, cross_pull = jax.vjp(norm_rows, first_sum, gain_cross, shift_cross)
    first_part, cross_gain_grad, cross_shift_grad = cross_pull(
        right_product(cross_q_grad, cross_query)
    )
    first_grad = second_grad + first_part
    branch_self = first_grad.astype(jnp.bfloat16)
    self_output_grad = left_product(mixed_self, branch_self)
    output_bias_grad = jnp.sum(first_grad, axis=0)
    mixed_self_grad = right_product(branch_self, self_output).astype(jnp.bfloat16)
    keys_back, values_back = (
        lax.all_gather(keys_self, "ctx", axis=0, tiled=True),
        lax.all_gather(values_self, "ctx", axis=0, tiled=True),
    )
    self_grad_heads = heads_of(mixed_self_grad)
    self_delta = row_deltas(self_grad_heads, attended_self)
    query_sum, key_terms_self, value_terms_self = attend_back(
        query_heads, keys_back, values_back, self_grad_heads, self_delta, total_self, tag_bundle
    )
    key_own, value_own = (
        lax.psum_scatter(
            key_terms_self.astype(jnp.bfloat16), "ctx", scatter_dimension=0, tiled=True
        ).astype(jnp.float32),
        lax.psum_scatter(
            value_terms_self.astype(jnp.bfloat16), "ctx", scatter_dimension=0, tiled=True
        ).astype(jnp.float32),
    )
    query_grad = query_sum.astype(jnp.bfloat16) * head_scale
    value_grad = value_own.astype(jnp.bfloat16)
    projected_grad = jnp.concatenate([query_grad, key_own.astype(jnp.bfloat16), value_grad], axis=1)
    self_weights_grad = left_product(normed_self, projected_grad)
    query_bias_grad = jnp.sum(query_grad, axis=0, dtype=jnp.float32)
    value_bias_grad = jnp.sum(value_grad, axis=0, dtype=jnp.float32)
    norm_value, self_pull = jax.vjp(norm_rows, tok_rows, gain_self, shift_self)
    token_part, self_gain_grad, self_shift_grad = self_pull(
        right_product(projected_grad, self_weights)
    )
    tokens_grad = first_grad + token_part
    gradients = (
        self_gain_grad,
        self_shift_grad,
        self_weights_grad,
        query_bias_grad,
        value_bias_grad,
        self_output_grad,
        output_bias_grad,
        cross_gain_grad,
        cross_shift_grad,
        cross_query_grad,
        query_offset_grad,
        cross_memory_grad,
        memory_offset_grad,
        cross_output_grad,
        return_bias_grad,
        feed_gain_grad,
        feed_shift_grad,
        up_grad,
        up_bias_grad,
        down_grad,
        down_bias_grad,
    )
    reduced = share_gradients(gradients, False)
    return (block_output[None], tokens_grad[None], source_grad[None]) + tuple(reduced)


def solution(mesh):
    near = (mesh.shape["group"], mesh.shape["ctx"], mesh.shape["shard"]) == (4, 4, 2)
    placed = (
        P(("group", "shard"), "ctx", None),
        P(("group", "shard"), "ctx", None),
        P(("group", "shard"), "ctx"),
        P(("group", "shard"), "ctx"),
        P(("group", "shard"), "ctx", None),
        P("shard"),
        P("shard"),
        P("shard", None),
        P("shard"),
        P("shard"),
        P("shard", None),
        P("shard"),
        P("shard"),
        P("shard"),
        P("shard", None),
        P("shard"),
        P("shard", None),
        P("shard"),
        P("shard", None),
        P("shard"),
        P("shard"),
        P("shard"),
        P("shard", None),
        P("shard"),
        P("shard", None),
        P("shard"),
    )
    return jax.shard_map(
        pair_device if near else per_device,
        mesh=mesh,
        in_specs=placed,
        out_specs=(
            P(("group", "shard"), "ctx", None),
            P(("group", "shard"), "ctx", None),
            P(("group", "shard"), "ctx", None),
            P("shard"),
            P("shard"),
            P("shard", None),
            P("shard"),
            P("shard"),
            P("shard", None),
            P("shard"),
            P("shard"),
            P("shard"),
            P("shard", None),
            P("shard"),
            P("shard", None),
            P("shard"),
            P("shard", None),
            P("shard"),
            P("shard"),
            P("shard"),
            P("shard", None),
            P("shard"),
            P("shard", None),
            P("shard"),
        ),
        check_vma=False,
    )
```

```python
import functools
import math

import jax
import jax.numpy as jnp
from jax import lax
from jax.experimental import pallas as pl
from jax.experimental.pallas import tpu as pltpu
from jax.sharding import PartitionSpec as P

MESH = pl.DeviceIdType.MESH
BF = jnp.bfloat16
F32 = jnp.float32


def coords():
    g, z, c = lax.axis_index("group"), lax.axis_index("ctx"), lax.axis_index("shard")
    return lax.rem(g, 2), lax.div(g, 2), z, c


def device_of(x, y, z, c):
    return (y * 2 + x, z, c)


def greet(devices):
    barrier = pltpu.get_barrier_semaphore()
    for device in devices:
        pl.semaphore_signal(barrier, inc=1, device_id=device, device_id_type=MESH)
    pl.semaphore_wait(barrier, len(devices))


D = 1024
HEADS = 16
HEAD_DIM = 64


EPSILON = 1e-05
NEGATIVE = -1e30


def norm_rows(values, gain_vec, shift_vec):
    average = jnp.mean(values, axis=-1, keepdims=True)
    centred = values - average
    spread = jnp.mean(centred * centred, axis=-1, keepdims=True)
    return centred * lax.rsqrt(spread + EPSILON) * gain_vec + shift_vec


def exact_gelu(values):
    return jax.nn.gelu(values, approximate=False)


def product(left_side, right_side):
    return jnp.dot(left_side, right_side, preferred_element_type=jnp.float32)


def left_product(left_side, right_side):
    return lax.dot_general(
        left_side, right_side, (((0,), (0,)), ((), ())), preferred_element_type=jnp.float32
    )


def right_product(left_side, right_side):
    return lax.dot_general(
        left_side, right_side, (((1,), (1,)), ((), ())), preferred_element_type=jnp.float32
    )


def heads_of(matrix):
    return matrix.reshape(matrix.shape[0], HEADS, HEAD_DIM)


def allow_table(query_seg, query_pos, key_seg, key_pos):
    shared = (key_seg[None, :] == 0) | (key_seg[None, :] == query_seg[:, None])
    return shared & (key_pos[None, :] <= query_pos[:, None])


def fold_keys(folded, queries, key_block, value_block, allowed):
    run_max, run_sum, weighted = folded
    scores = jnp.einsum("qhd,khd->hqk", queries, key_block, preferred_element_type=jnp.float32)
    if allowed is not None:
        scores = jnp.where(allowed[None], scores, NEGATIVE)
    new_max = jnp.maximum(run_max, jnp.max(scores, axis=2))
    factor = jnp.exp(run_max - new_max)
    weighting = jnp.exp(scores - new_max[:, :, None])
    new_sum = run_sum * factor + jnp.sum(weighting, axis=2)
    update = jnp.einsum(
        "hqk,khd->qhd",
        weighting.astype(jnp.bfloat16),
        value_block,
        preferred_element_type=jnp.float32,
    )
    return (new_max, new_sum, weighted * jnp.transpose(factor)[:, :, None] + update)


def attend_piece(folded, queries, key_piece, value_piece, tag_bundle):
    count_rows = key_piece.shape[0]
    block_rows = math.gcd(count_rows, 512)

    def one_block(number, current):
        offset = number * block_rows
        key_block = heads_of(lax.dynamic_slice_in_dim(key_piece, offset, block_rows, 0))
        value_block = heads_of(lax.dynamic_slice_in_dim(value_piece, offset, block_rows, 0))
        allowed = None
        if tag_bundle is not None:
            query_seg, query_pos, seg_all, pos_all = tag_bundle
            key_seg = lax.dynamic_slice_in_dim(seg_all, offset, block_rows, 0)
            key_pos = lax.dynamic_slice_in_dim(pos_all, offset, block_rows, 0)
            allowed = allow_table(query_seg, query_pos, key_seg, key_pos)
        return fold_keys(current, queries, key_block, value_block, allowed)

    return lax.fori_loop(0, count_rows // block_rows, one_block, folded)


def finish(folded):
    run_max, run_sum, weighted = folded
    attended = weighted / jnp.transpose(run_sum)[:, :, None]
    return (attended, run_max + jnp.log(run_sum))


def row_deltas(out_grad, attended):
    return jnp.einsum("qhd,qhd->hq", out_grad, attended, preferred_element_type=jnp.float32)


def attend_back(queries, key_all, value_all, out_grad, row_delta, log_total, tag_bundle):
    total_rows = key_all.shape[0]
    row_count = queries.shape[0]
    block_rows = math.gcd(total_rows, 512)

    def one_block(query_acc, number):
        offset = number * block_rows
        key_block = heads_of(lax.dynamic_slice_in_dim(key_all, offset, block_rows, 0))
        value_block = heads_of(lax.dynamic_slice_in_dim(value_all, offset, block_rows, 0))
        scores = jnp.einsum("qhd,khd->hqk", queries, key_block, preferred_element_type=jnp.float32)
        if tag_bundle is not None:
            query_seg, query_pos, seg_all, pos_all = tag_bundle
            key_seg = lax.dynamic_slice_in_dim(seg_all, offset, block_rows, 0)
            key_pos = lax.dynamic_slice_in_dim(pos_all, offset, block_rows, 0)
            scores = jnp.where(
                allow_table(query_seg, query_pos, key_seg, key_pos)[None], scores, NEGATIVE
            )
        weighting = jnp.exp(scores - log_total[:, :, None])
        weight_grad = jnp.einsum(
            "qhd,khd->hqk", out_grad, value_block, preferred_element_type=jnp.float32
        )
        score_grad = (weighting * (weight_grad - row_delta[:, :, None])).astype(jnp.bfloat16)
        query_acc = query_acc + jnp.einsum(
            "hqk,khd->qhd", score_grad, key_block, preferred_element_type=jnp.float32
        )
        key_term = jnp.einsum(
            "hqk,qhd->khd", score_grad, queries, preferred_element_type=jnp.float32
        )
        value_term = jnp.einsum(
            "hqk,qhd->khd",
            weighting.astype(jnp.bfloat16),
            out_grad,
            preferred_element_type=jnp.float32,
        )
        return (query_acc, (key_term.reshape(block_rows, D), value_term.reshape(block_rows, D)))

    start_acc = jnp.zeros((row_count, HEADS, HEAD_DIM), jnp.float32)
    query_acc, terms = lax.scan(one_block, start_acc, jnp.arange(total_rows // block_rows))
    key_terms, value_terms = terms
    return (
        query_acc.reshape(row_count, D),
        key_terms.reshape(total_rows, D),
        value_terms.reshape(total_rows, D),
    )


def pair_places():
    x, y, z, c = coords()
    side = 1 - 2 * lax.rem(z, 2)
    sib, near, diag = device_of(x, y, z, 1 - c), device_of(x, y, z + side, c), device_of(x, y, z + side, 1 - c)
    far = device_of(x, y, z + 2 - 4 * lax.div(z, 2), 1 - c)
    block = 2 * c + lax.rem(z, 2)
    near_block = 2 * c + 1 - lax.rem(z, 2)
    sib_block = 2 * (1 - c) + lax.rem(z, 2)
    diag_block = 2 * (1 - c) + 1 - lax.rem(z, 2)
    home = lax.div(z, 2) == c
    return sib, near, diag, far, block, near_block, sib_block, diag_block, home


TILE = 256
LANES = 128
NEG = -1e30


def dot_nt(a, b):
    return lax.dot_general(a, b, (((1,), (1,)), ((), ())), preferred_element_type=F32)


def dot_nn(a, b):
    return lax.dot_general(a, b, (((1,), (0,)), ((), ())), preferred_element_type=F32)


def split_heads(source, target, heads):
    rows = source.shape[0]
    step = min(rows, 256)
    even = lax.broadcasted_iota(jnp.int32, (step, LANES), 1) < LANES // 2

    def one(k, carry):
        here = pl.ds(pl.multiple_of(k * step, step), step)
        for pair in range(heads // 2):
            block = source[here, pl.ds(pair * LANES, LANES)]
            target[2 * pair, here, :] = jnp.where(even, block, jnp.zeros_like(block))
            target[2 * pair + 1, here, :] = jnp.where(even, jnp.zeros_like(block), block)
        return carry

    lax.fori_loop(0, rows // step, one, 0)


def transpose_rows(source, target):
    rows = source.shape[0]
    step = min(rows, 256)

    def one(k, carry):
        here = pl.ds(pl.multiple_of(k * step, step), step)
        target[:, here] = source[here, :].astype(F32).T.astype(target.dtype)
        return carry

    lax.fori_loop(0, rows // step, one, 0)


def tree_mask(key_tile, query_tile, key_seg, query_seg, prompt):
    key_at = key_tile * TILE + lax.broadcasted_iota(jnp.int32, (TILE, TILE), 0)
    query_at = query_tile * TILE + lax.broadcasted_iota(jnp.int32, (TILE, TILE), 1)
    return (key_at <= query_at) & ((key_at < prompt) | (key_seg == query_seg))


HEAD_SCALE = 1.0 / math.sqrt(HEAD_DIM)


class Cores:
    def __init__(self):
        sib, near, diag, _, block, near_block, sib_block, diag_block, _ = pair_places()
        self.others = (near, sib, diag)
        self.blocks = (block, near_block, sib_block, diag_block)
        self.per_block = 2

    def tile_at(self, turn):
        b = lax.rem(self.blocks[0] + 1 + lax.div(turn, self.per_block), 4)
        return b * self.per_block + lax.rem(turn, self.per_block)

    def ends(self, source, target, tile, place):
        width = source.shape[1]
        src = source.at[pl.ds(pl.multiple_of(tile * TILE, TILE), TILE), :]
        row = pl.multiple_of(lax.rem(tile, self.per_block) * TILE, TILE)
        column = pl.multiple_of(place * 4 * width + self.blocks[0] * width, width)
        return src, target.at[pl.ds(row, TILE), pl.ds(column, width)]

    def give(self, source, target, tile, place, load, send, recv):
        src, dst = self.ends(source, target, tile, place)
        owner = lax.div(tile, self.per_block)

        @pl.when(owner == self.blocks[0])
        def _():
            pltpu.make_async_copy(src, dst, load).start()

        for device, b in zip(self.others, self.blocks[1:]):

            @pl.when(owner == b)
            def _():
                pltpu.make_async_remote_copy(
                    src_ref=src, dst_ref=dst, send_sem=send, recv_sem=recv.at[self.blocks[0], lax.rem(tile, self.per_block)],
                    device_id=device, device_id_type=MESH,
                ).start()

    def finish(self, source, target, place, load, send, recv):
        for k in range(self.per_block):
            tile = self.blocks[0] * self.per_block + k
            src, dst = self.ends(source, target, tile, place)
            pltpu.make_async_copy(src, dst, load.at[tile]).wait()
            for device, b in zip(self.others, self.blocks[1:]):
                sent = b * self.per_block + k
                src, dst = self.ends(source, target, sent, place)
                pltpu.make_async_remote_copy(
                    src_ref=src, dst_ref=dst, send_sem=send.at[sent], recv_sem=recv.at[b, k], device_id=device, device_id_type=MESH
                ).wait()


def trade_semaphores(tiles, places):
    dma = pltpu.SemaphoreType.DMA
    lead = () if places == 1 else (places,)
    return [dma(lead + (tiles,)), dma(lead + (tiles,)), dma(lead + (4, tiles // 4))]


def attention_params(masked, collective_id):
    if masked:
        return pltpu.CompilerParams(vmem_limit_bytes=60 << 20, collective_id=collective_id, has_side_effects=True)
    return pltpu.CompilerParams(vmem_limit_bytes=40 << 20)


def forward_kernel(heads, masked, *refs):
    if masked:
        q_ref, k_ref, v_ref, seg_col, seg_row, o_ref, lse_ref, mixed_ref, qm, vt, acc, load, send, recv = refs
    else:
        q_ref, k_ref, v_ref, o_ref, lse_ref, qm, vt, acc = refs
    n_query, n_key = q_ref.shape[0] // TILE, k_ref.shape[0] // TILE
    prompt_tiles = n_key // 2
    if masked:
        cores = Cores()
        greet(cores.others)
    split_heads(q_ref, qm, heads)
    transpose_rows(v_ref, vt)
    H = range(heads)

    def query_tile(turn, carry):
        i = cores.tile_at(turn) if masked else turn
        rows = pl.ds(pl.multiple_of(i * TILE, TILE), TILE)
        queries = [qm[h, rows, :] for h in H]
        acc[...] = jnp.zeros_like(acc)

        def tile(j, mask, state, span=1):
            keys = pl.ds(pl.multiple_of(j * TILE, TILE), span * TILE)
            old_m, old_l = state
            scores = [dot_nt(k_ref[keys, pl.ds(h // 2 * LANES, LANES)], queries[h]) for h in H]
            if mask is not None:
                scores = [jnp.where(mask, s, NEG) for s in scores]
            new_m = [jnp.maximum(old_m[h], jnp.max(scores[h], axis=0, keepdims=True)) for h in H]
            weights = [jnp.exp(scores[h] - new_m[h]) for h in H]
            if mask is not None:
                weights = [jnp.where(mask, w, 0.0) for w in weights]
            factor = [jnp.exp(old_m[h] - new_m[h]) for h in H]
            new_l = [old_l[h] * factor[h] + jnp.sum(weights[h], axis=0, keepdims=True) for h in H]
            low = [w.astype(BF) for w in weights]
            for h in H:
                part = pl.ds(h * 64, 64)
                acc[part, :] = acc[part, :] * factor[h] + dot_nn(vt[part, keys], low[h])
            return (new_m, new_l)

        state = ([jnp.full((1, TILE), NEG, F32)] * heads, [jnp.zeros((1, TILE), F32)] * heads)
        if masked:
            later = i >= prompt_tiles
            state = lax.fori_loop(0, jnp.where(later, 0, i), lambda j, c: tile(j, None, c), state)
            state = lax.fori_loop(0, jnp.where(later, 1, 0), lambda j, c: tile(0, None, c, prompt_tiles), state)

            def near(j, c):
                keys = pl.ds(pl.multiple_of(j * TILE, TILE), TILE)
                return tile(j, tree_mask(j, i, seg_col[keys, :], seg_row[:, rows], prompt_tiles * TILE), c)

            first = jnp.where(i > prompt_tiles, i - 1, i)
            state = lax.fori_loop(first, i + 1, near, state)
        else:
            state = tile(0, None, state, n_key)
        m, l = state
        for h in H:
            part = pl.ds(h * 64, 64)
            acc[part, :] = acc[part, :] / l[h]
            lse_ref[pl.ds(h, 1), rows] = m[h] + jnp.log(l[h])
        o_ref[rows, :] = acc[...].T.astype(BF)
        if masked:
            cores.give(o_ref, mixed_ref, i, 0, load.at[i], send.at[i], recv)
        return carry

    lax.fori_loop(0, n_query, query_tile, 0)
    if masked:
        cores.finish(o_ref, mixed_ref, 0, load, send, recv)


def attention_forward(q, k, v, seg=None):
    heads, width = 4, 256
    n, m, groups = q.shape[0], k.shape[0], q.shape[1] // 256
    masked = seg is not None
    column = lambda rows: pl.BlockSpec((rows, width), lambda p: (0, p))
    whole = lambda shape: pl.BlockSpec(shape, lambda p: (0, 0))
    extra = [seg.reshape(n, 1), seg.reshape(1, n)] if masked else []
    return pl.pallas_call(
        functools.partial(forward_kernel, heads, masked),
        grid=(groups,),
        out_shape=(jax.ShapeDtypeStruct((n, q.shape[1]), BF), jax.ShapeDtypeStruct((groups, 8, n), F32))
        + ((jax.ShapeDtypeStruct((n // 4, 4 * width), BF),) if masked else ()),
        in_specs=[column(n), column(m), column(m)] + [whole(e.shape) for e in extra],
        out_specs=(column(n), pl.BlockSpec((None, 8, n), lambda p: (p, 0, 0)))
        + ((pl.BlockSpec(memory_space=pltpu.HBM),) if masked else ()),
        scratch_shapes=[
            pltpu.VMEM((heads, n, LANES), BF),
            pltpu.VMEM((width, m), BF),
            pltpu.VMEM((width, TILE), F32),
        ]
        + (trade_semaphores(n // TILE, 1) if masked else []),
        compiler_params=attention_params(masked, 3),
        cost_estimate=pl.CostEstimate(flops=24 * n * m * q.shape[1], bytes_accessed=4 * (n + m) * q.shape[1], transcendentals=n * m * heads * groups),
        name="attention_forward",
    )(q, k, v, *extra)


def backward_kernel(heads, q_ref, k_ref, v_ref, g_ref, o_ref, lse_ref, dq_ref, dk_ref, dv_ref, qm, gm, kt, dqt, dk_acc, dv_acc, delta):
    n_query, n_key = q_ref.shape[0] // TILE, k_ref.shape[0] // TILE
    split_heads(q_ref, qm, heads)
    split_heads(g_ref, gm, heads)
    transpose_rows(k_ref, kt)
    dqt[...] = jnp.zeros_like(dqt)
    H = range(heads)
    lane = [pl.ds(h // 2 * LANES, LANES) for h in H]

    def deltas(i, carry):
        rows = pl.ds(pl.multiple_of(i * TILE, TILE), TILE)
        product = (g_ref[rows, :].astype(F32) * o_ref[rows, :].astype(F32)).T
        for h in H:
            delta[pl.ds(h, 1), rows] = jnp.sum(product[h * 64 : h * 64 + 64, :], axis=0, keepdims=True)
        return carry

    lax.fori_loop(0, n_query, deltas, 0)

    def key_tile(j, carry):
        keys = pl.ds(pl.multiple_of(j * TILE, TILE), TILE)
        dk_acc[...] = jnp.zeros_like(dk_acc)
        dv_acc[...] = jnp.zeros_like(dv_acc)

        def all_queries():
            rows = pl.ds(0, n_query * TILE)
            scores = [dot_nt(k_ref[keys, lane[h]], qm[h, rows, :]) for h in H]
            change = [dot_nt(v_ref[keys, lane[h]], gm[h, rows, :]) for h in H]
            weights = [jnp.exp(scores[h] - lse_ref[pl.ds(h, 1), rows]) for h in H]
            back = [(weights[h] * (change[h] - delta[pl.ds(h, 1), rows])).astype(BF) for h in H]
            low = [w.astype(BF) for w in weights]
            for pair in range(heads // 2):
                a, b = 2 * pair, 2 * pair + 1
                dv_acc[:, lane[a]] += dot_nn(low[a], gm[a, rows, :]) + dot_nn(low[b], gm[b, rows, :])
                dk_acc[:, lane[a]] += dot_nn(back[a], qm[a, rows, :]) + dot_nn(back[b], qm[b, rows, :])
            for h in H:
                part = pl.ds(h * 64, 64)
                dqt[part, rows] += dot_nn(kt[part, keys], back[h])

        all_queries()
        dk_ref[keys, :] = dk_acc[...].astype(BF)
        dv_ref[keys, :] = dv_acc[...].astype(BF)
        return carry

    lax.fori_loop(0, n_key, key_tile, 0)

    def finish(i, carry):
        rows = pl.ds(pl.multiple_of(i * TILE, TILE), TILE)
        dq_ref[rows, :] = dqt[:, rows].T.astype(BF)
        return carry

    lax.fori_loop(0, n_query, finish, 0)


def attention_backward(q, k, v, grad, mix, lse):
    heads, width = 4, 256
    n, m, groups = q.shape[0], k.shape[0], q.shape[1] // 256
    column = lambda rows: pl.BlockSpec((rows, width), lambda p: (0, p))
    return pl.pallas_call(
        functools.partial(backward_kernel, heads),
        grid=(groups,),
        out_shape=[jax.ShapeDtypeStruct((rows, q.shape[1]), BF) for rows in (n, m, m)],
        in_specs=[column(n), column(m), column(m), column(n), column(n), pl.BlockSpec((None, 8, n), lambda p: (p, 0, 0))],
        out_specs=[column(n), column(m), column(m)],
        scratch_shapes=[
            pltpu.VMEM((heads, n, LANES), BF),
            pltpu.VMEM((heads, n, LANES), BF),
            pltpu.VMEM((width, m), BF),
            pltpu.VMEM((width, n), F32),
            pltpu.VMEM((TILE, width), F32),
            pltpu.VMEM((TILE, width), F32),
            pltpu.VMEM((8, n), F32),
        ],
        compiler_params=pltpu.CompilerParams(vmem_limit_bytes=40 << 20),
        cost_estimate=pl.CostEstimate(flops=32 * n * m * q.shape[1], bytes_accessed=8 * (n + m) * q.shape[1], transcendentals=n * m * heads * groups),
        name="attention_backward",
    )(q, k, v, grad, mix, lse)


CH = 512
WD = 1024
SETS = ((0, 512), (512, 384), (896, 128))
RING = 4
KEEP = 6
FIRST_AT = 2
KEYS_AT = 3
GATHER_AT = 12
SOURCE_AT = 13


def backward_parts(heads, cores, q_ref, k_ref, v_ref, o_ref, lse_ref, seg_col, seg_row, projected_ref,
                   dq_ref, dk_ref, dv_ref, g_ref, qm, gm, kt, dqt, dk_acc, dv_acc, delta, load, send, recv):
    n_query, n_key = q_ref.shape[0] // TILE, k_ref.shape[0] // TILE
    prompt_tiles = n_key // 2
    H = range(heads)
    lane = [pl.ds(h // 2 * LANES, LANES) for h in H]

    def first():
        split_heads(q_ref, qm, heads)
        split_heads(g_ref, gm, heads)
        transpose_rows(k_ref, kt)
        dqt[...] = jnp.zeros_like(dqt)

        def deltas(i, carry):
            rows = pl.ds(pl.multiple_of(i * TILE, TILE), TILE)
            product = (g_ref[rows, :].astype(F32) * o_ref[rows, :].astype(F32)).T
            for h in H:
                delta[pl.ds(h, 1), rows] = jnp.sum(product[h * 64 : h * 64 + 64, :], axis=0, keepdims=True)
            return carry

        lax.fori_loop(0, n_query, deltas, 0)

    def send_rows(source, place, j):
        cores.give(source, projected_ref, j, place, load.at[place, j], send.at[place, j], recv.at[place])

    def finish_queries(i):
        rows = pl.ds(pl.multiple_of(i * TILE, TILE), TILE)
        dq_ref[rows, :] = (dqt[:, rows].T.astype(BF).astype(F32) * HEAD_SCALE).astype(BF)
        send_rows(dq_ref, 0, i)

    def key_tile(turn):
        j = lax.rem(turn + prompt_tiles, n_key)
        keys = pl.ds(pl.multiple_of(j * TILE, TILE), TILE)
        dk_acc[...] = jnp.zeros_like(dk_acc)
        dv_acc[...] = jnp.zeros_like(dv_acc)

        def tile(i, mask):
            rows = pl.ds(pl.multiple_of(i * TILE, TILE), TILE)
            scores = [dot_nt(k_ref[keys, lane[h]], qm[h, rows, :]) for h in H]
            change = [dot_nt(v_ref[keys, lane[h]], gm[h, rows, :]) for h in H]
            weights = [jnp.exp(scores[h] - lse_ref[pl.ds(h, 1), rows]) for h in H]
            if mask is not None:
                weights = [jnp.where(mask, w, 0.0) for w in weights]
            back = [(weights[h] * (change[h] - delta[pl.ds(h, 1), rows])).astype(BF) for h in H]
            low = [w.astype(BF) for w in weights]
            for pair in range(heads // 2):
                a, b = 2 * pair, 2 * pair + 1
                dv_acc[:, lane[a]] += dot_nn(low[a], gm[a, rows, :]) + dot_nn(low[b], gm[b, rows, :])
                dk_acc[:, lane[a]] += dot_nn(back[a], qm[a, rows, :]) + dot_nn(back[b], qm[b, rows, :])
            for h in H:
                part = pl.ds(h * 64, 64)
                dqt[part, rows] += dot_nn(kt[part, keys], back[h])

        def near(i, carry):
            rows = pl.ds(pl.multiple_of(i * TILE, TILE), TILE)
            tile(i, tree_mask(j, i, seg_col[keys, :], seg_row[:, rows], prompt_tiles * TILE))
            return carry

        prompt = j < prompt_tiles
        last = jnp.where(prompt, j, jnp.minimum(j + 1, n_query - 1))
        lax.fori_loop(j, last + 1, near, 0)
        lax.fori_loop(jnp.where(prompt, j + 1, n_query), n_query, lambda i, c: (tile(i, None), c)[1], 0)
        dk_ref[keys, :] = dk_acc[...].astype(BF)
        dv_ref[keys, :] = dv_acc[...].astype(BF)
        send_rows(dk_ref, 1, j)
        send_rows(dv_ref, 2, j)

        @pl.when(prompt)
        def _():
            finish_queries(j)

    def last_queries():
        lax.fori_loop(prompt_tiles, n_query, lambda i, c: (finish_queries(i), c)[1], 0)

    def end():
        for place, source in enumerate((dq_ref, dk_ref, dv_ref)):
            cores.finish(source, projected_ref, place, load.at[place], send.at[place], recv.at[place])

    return first, key_tile, last_queries, end, n_key


def finish_kernel(plan, n_sources, *refs):
    n_chunks = len(plan)
    q_ref, k_ref, v_ref, o_ref, lse_ref, seg_col, seg_row, mix_grad, block_ref, tok_ref, first_ref, gain_ref, small = refs[:13]
    sources = list(refs[13 : 13 + n_sources])
    weights_ref, memory_ref, key_terms, value_terms = (*refs[13 + n_sources : 15 + n_sources], *sources[-2:])
    out, small_out, tokens_home, block_home, source_home, projected_ref = refs[15 + n_sources : 21 + n_sources]
    (
        dq_ref, dk_ref, dv_ref, g_ref, qm, gm, kt, dqt, dk_acc, dv_acc, delta, trade_load, trade_send, trade_recv,
        tokens_out, part_ref, src_a, src_b, src_r1, src_r2, home_sem, away_send, away_recv, src_send, src_recv, grad_send, grad_recv,
        acc, snd, r0, r1, r2, r3, r4, sv, sr, xbuf, ybuf, wbuf, pbuf,
        x_sem, y_sem, w_sem, p_sem, take_sem, s0s, s0r, hs, hr, gs, gr, put_sem, svs, svr,
    ) = refs[21 + n_sources :]
    sources.append(projected_ref)
    x, y, z, c = coords()
    cores = Cores()
    sib = device_of(x, y, z, 1 - c)
    dx, dy = device_of(1 - x, y, z, c), device_of(x, 1 - y, z, c)
    dz2, dz1 = device_of(x, y, z + 2 - 4 * lax.div(z, 2), c), cores.others[0]
    far = device_of(x, y, z + 2 - 4 * lax.div(z, 2), 1 - c)
    home = lax.div(z, 2) == c
    greet((sib, dx, dy, dz2, dz1, cores.others[2], far))
    z2, z1 = lax.div(z, 2), lax.rem(z, 2)

    first, key_tile, last_queries, end_trade, n_key = backward_parts(
        4, cores, q_ref, k_ref, v_ref, o_ref, lse_ref, seg_col, seg_row, projected_ref,
        dq_ref, dk_ref, dv_ref, g_ref, qm, gm, kt, dqt, dk_acc, dv_acc, delta, trade_load, trade_send, trade_recv,
    )

    def remote(src, dst, send, recv, device):
        return pltpu.make_async_remote_copy(src_ref=src, dst_ref=dst, send_sem=send, recv_sem=recv, device_id=device, device_id_type=MESH)

    def send_home(i, src, dst, wait):
        @pl.when(home)
        def _():
            copy = pltpu.make_async_copy(src, dst, home_sem.at[i])
            copy.wait() if wait else copy.start()

        @pl.when(jnp.logical_not(home))
        def _():
            copy = remote(src, dst, away_send.at[i], away_recv.at[i], far)
            copy.wait() if wait else copy.start()

    own_block = cores.blocks[0]
    part_rows, head_cols = mix_grad.shape[0], q_ref.shape[1]
    grad_rows = g_ref.at[pl.ds(pl.multiple_of(own_block * part_rows, part_rows), part_rows), :]

    def grad_copy(k):
        cols = pl.ds(pl.multiple_of(cores.blocks[1 + k] * head_cols, head_cols), head_cols)
        return remote(mix_grad.at[:, cols], grad_rows, grad_send.at[k], grad_recv.at[k], cores.others[k])

    half_rows = part_ref.shape[0] // 2
    quarter = half_rows // 2

    def source_sib():
        return remote(part_ref.at[pl.ds(half_rows, half_rows), :], src_r1, src_send.at[0], src_recv.at[0], sib)

    def source_near():
        return remote(src_a.at[pl.ds(quarter, quarter), :], src_r2, src_send.at[1], src_recv.at[1], dz1)

    def add_blocks(target, one_ref, other_ref, rows):
        def one(k, carry):
            here = pl.ds(pl.multiple_of(k * 32, 32), 32)
            target[here, :] = (one_ref[here, :].astype(F32) + other_ref[here, :].astype(F32)).astype(BF)
            return carry

        lax.fori_loop(0, rows // 32, one, 0)

    def begin():
        for k in range(3):
            grad_copy(k).start()
        send_home(0, block_ref, block_home, False)

    def begin_keys():
        g_ref[pl.ds(pl.multiple_of(own_block * part_rows, part_rows), part_rows), :] = mix_grad[
            :, pl.ds(pl.multiple_of(own_block * head_cols, head_cols), head_cols)
        ]
        for k in range(3):
            grad_copy(k).wait()
        first()

    def memory_copy():
        return pltpu.make_async_copy(memory_ref, wbuf.at[:, pl.ds(0, 2 * WD)], w_sem.at[0])

    def source_0():
        memory_copy().wait()
        step = pbuf.shape[0]

        def one(k, carry):
            rows = pl.ds(pl.multiple_of(k * step, step), step)
            copies = [
                pltpu.make_async_copy(terms.at[rows, :], pbuf.at[:, pl.ds(p * WD, WD)], take_sem.at[p])
                for p, terms in enumerate((key_terms, value_terms))
            ]
            for copy in copies:
                copy.start()
            for copy in copies:
                copy.wait()
            part_ref[rows, :] = dot_nt(pbuf[:, : 2 * WD], wbuf[:, : 2 * WD]).astype(BF)
            return carry

        lax.fori_loop(0, part_ref.shape[0] // step, one, 0)
        source_sib().start()

    def source_1():
        source_sib().wait()
        add_blocks(src_a, part_ref, src_r1, half_rows)
        source_near().start()

    def source_2():
        source_near().wait()
        add_blocks(src_b, src_a, src_r2, quarter)
        send_home(1, src_b, source_home, False)

    def fetch(k):
        xi, kind, i, yi, column = plan[k]
        depth = sources[xi].shape[0]
        half = sources[xi].shape[1] // 2
        at = i * CH if kind == "rows" else 0
        for p, h in enumerate((c, 1 - c)):
            pltpu.make_async_copy(
                sources[xi].at[:, pl.ds(pl.multiple_of(h * half + at, CH), CH)],
                xbuf.at[k % 2, pl.ds(0, depth), pl.ds(p * CH, CH)],
                x_sem.at[k % 2, p],
            ).start()
        pltpu.make_async_copy(sources[yi].at[:, pl.ds(column * WD, WD)], ybuf.at[k % 2, pl.ds(0, depth), :], y_sem.at[k % 2]).start()

    def swap_copy(j):
        return pltpu.make_async_remote_copy(
            src_ref=snd.at[lax.rem(j, 2)], dst_ref=r0.at[lax.rem(j, RING)], send_sem=s0s.at[j], recv_sem=s0r.at[j], device_id=sib, device_id_type=MESH
        )

    def make(j, depth):
        slot, keep = lax.rem(j, 2), lax.rem(j, KEEP)
        deep = pl.ds(0, depth)
        for p in range(2):
            side = xbuf.at[slot, deep, pl.ds(p * CH, CH)]
            pltpu.make_async_copy(side, side, x_sem.at[slot, p]).wait()
        pltpu.make_async_copy(ybuf.at[slot, deep, :], ybuf.at[slot, deep, :], y_sem.at[slot]).wait()
        step = 128

        def one(k, carry):
            rows = pl.ds(pl.multiple_of(k * step, step), step)
            more = pl.ds(pl.multiple_of(CH + k * step, step), step)
            across = (((0,), (0,)), ((), ()))
            own = lax.dot_general(xbuf[slot, deep, rows], ybuf[slot, deep, :], across, preferred_element_type=F32)
            acc[keep, rows, :] = own.astype(BF)
            other = lax.dot_general(xbuf[slot, deep, more], ybuf[slot, deep, :], across, preferred_element_type=F32)
            snd[slot, rows, :] = other.astype(BF)
            return carry

        lax.fori_loop(0, CH // step, one, 0)

    rbufs = (r1, r2, r3, r4)

    def axis(jj, s, q):
        even = lax.rem(jj, 2) == 0
        along = ((("one", "two", "near", "far"), ("two", "one", "near", "far"), ("near", "one", "two", "far"))[s])[q]
        if along == "near":
            return dz1, z1
        if along == "far":
            return dz2, z2
        use_x = even if along == "one" else jnp.logical_not(even)
        return (jnp.where(use_x, dx[0], dy[0]), z, c), jnp.where(use_x, x, y)

    def start_of(jj, s, step):
        row = 0
        for q in range(step):
            row = row + axis(jj, s, q)[1] * (CH >> (q + 1))
        return row

    def halve_copy(jj, s, q):
        size = CH >> (q + 1)
        device, bit = axis(jj, s, q)
        row = start_of(jj, s, q) + (1 - bit) * size
        return pltpu.make_async_remote_copy(
            src_ref=acc.at[lax.rem(jj, KEEP), pl.ds(pl.multiple_of(row, 32), size), pl.ds(*SETS[s])],
            dst_ref=rbufs[q].at[lax.rem(jj, RING), :, pl.ds(*SETS[s])],
            send_sem=hs.at[jj, s, q],
            recv_sem=hr.at[jj, s, q],
            device_id=device,
            device_id_type=MESH,
        )

    def give_copy(jj, s, q):
        size = CH >> (q + 1)
        block = out.at[jj, pl.ds(pl.multiple_of(start_of(jj, s, q + 1), 32), size), pl.ds(*SETS[s])]
        return pltpu.make_async_remote_copy(
            src_ref=block, dst_ref=block, send_sem=gs.at[jj, s, q], recv_sem=gr.at[jj, s, q], device_id=axis(jj, s, q)[0], device_id_type=MESH
        )

    def put_copy(jj, s):
        rows = pl.ds(pl.multiple_of(start_of(jj, s, 4), 32), CH >> 4)
        return pltpu.make_async_copy(
            acc.at[lax.rem(jj, KEEP), rows, pl.ds(*SETS[s])], out.at[jj, rows, pl.ds(*SETS[s])], put_sem.at[jj, s]
        )

    def add_rows(jj, s, q):
        size = CH >> (q + 1)
        row = pl.multiple_of(start_of(jj, s, q + 1), 32)
        span = min(size, 64)
        keep, slot, cols = lax.rem(jj, KEEP), lax.rem(jj, RING), pl.ds(*SETS[s])

        def one(k, carry):
            here = pl.ds(pl.multiple_of(row + k * span, 32), span)
            there = pl.ds(pl.multiple_of(k * span, 32), span)
            acc[keep, here, cols] = (acc[keep, here, cols].astype(F32) + rbufs[q][slot, there, cols].astype(F32)).astype(BF)
            return carry

        lax.fori_loop(0, size // span, one, 0)

    def phase0(jj):
        swap_copy(jj).wait()
        keep, slot = lax.rem(jj, KEEP), lax.rem(jj, RING)

        def one(k, carry):
            here = pl.ds(pl.multiple_of(k * 32, 32), 32)
            acc[keep, here, :] = (acc[keep, here, :].astype(F32) + r0[slot, here, :].astype(F32)).astype(BF)
            return carry

        lax.fori_loop(0, CH // 32, one, 0)
        for s in range(len(SETS)):
            halve_copy(jj, s, 0).start()

    def phase_halve(jj, q):
        for s in range(len(SETS)):
            halve_copy(jj, s, q).wait()
            add_rows(jj, s, q)
            if q < 3:
                halve_copy(jj, s, q + 1).start()
            else:
                put_copy(jj, s).start()
        if q == 3:
            for s in range(len(SETS)):
                put_copy(jj, s).wait()
                give_copy(jj, s, 3).start()

    def phase_give(jj, q):
        for s in range(len(SETS)):
            give_copy(jj, s, q).wait()
            if q > 0:
                give_copy(jj, s, q - 1).start()

    partners = (sib, dx, dy, dz2, dz1)

    def small_copy(p):
        return pltpu.make_async_remote_copy(
            src_ref=sv.at[p], dst_ref=sr.at[p], send_sem=svs.at[p], recv_sem=svr.at[p], device_id=partners[p], device_id_type=MESH
        )

    def small_phase(p):
        if p > 0:
            small_copy(p - 1).wait()
            sv[p] = sv[p - 1] + sr[p - 1]
        if p < 5:
            small_copy(p).start()
        else:
            small_out[...] = sv[5]

    def w_copy():
        return pltpu.make_async_copy(weights_ref, wbuf, w_sem.at[0])

    def gather():
        end_trade()
        w_copy().wait()
        d = WD
        step = 128
        zero = jnp.zeros((1, d), F32)

        def one(k, sums):
            rows = pl.ds(pl.multiple_of(k * step, step), step)
            p_copy = pltpu.make_async_copy(projected_ref.at[rows, :], pbuf, p_sem.at[0])
            p_copy.start()
            p_copy.wait()
            projected = pbuf[...]
            e = dot_nt(projected, wbuf[...])
            values = tok_ref[rows, :].astype(F32)
            centred = values - jnp.mean(values, axis=-1, keepdims=True)
            r = lax.rsqrt(jnp.mean(centred * centred, axis=-1, keepdims=True) + EPSILON)
            xhat = centred * r
            t = e * gain_ref[...]
            change = r * (t - jnp.mean(t, axis=-1, keepdims=True) - xhat * jnp.mean(t * xhat, axis=-1, keepdims=True))
            tokens_out[rows, :] = (first_ref[rows, :] + change).astype(BF)
            wide = projected.astype(F32)
            new = (e * xhat, e, wide[:, :d], wide[:, 2 * d :])
            return tuple(s + jnp.sum(v, axis=0, keepdims=True) for s, v in zip(sums, new))

        sums = lax.fori_loop(0, tok_ref.shape[0] // step, one, (zero,) * 4)
        sv[0] = small[...]
        for row, total in enumerate(sums):
            sv[0, pl.ds(row, 1), :] = total
        send_home(2, tokens_out, tokens_home, False)
        memory_copy().start()

    late = [k for k in range(n_chunks) if plan[k][3] == n_sources]
    depth_of = [sources[entry[0]].shape[0] for entry in plan]
    fetch(0)

    def step(t, carry):
        for k in range(1, n_chunks):
            if k not in late:
                pl.when(t + 1 == k)(functools.partial(fetch, k))
        for depth in sorted(set(depth_of)):
            these = [t == k for k in range(n_chunks) if depth_of[k] == depth]
            pl.when(functools.reduce(jnp.logical_or, these))(functools.partial(make, t, depth))

        @pl.when(t < n_chunks)
        def _():
            swap_copy(t).start()

        def guarded(lag, what):
            @pl.when((t >= lag) & (t < n_chunks + lag))
            def _():
                what(t - lag)

        guarded(1, phase0)
        for q in range(4):
            guarded(q + 2, functools.partial(phase_halve, q=q))
        for q in range(3, -1, -1):
            guarded(9 - q, functools.partial(phase_give, q=q))
        pl.when(t == 0)(begin)
        pl.when(t == FIRST_AT)(begin_keys)
        pl.when((t >= KEYS_AT) & (t < KEYS_AT + n_key))(functools.partial(key_tile, t - KEYS_AT))

        @pl.when(t == KEYS_AT + n_key)
        def _():
            last_queries()
            w_copy().start()

        pl.when(t == GATHER_AT)(gather)
        pl.when(t == SOURCE_AT)(source_0)
        pl.when(t == SOURCE_AT + 1)(source_1)
        pl.when(t == SOURCE_AT + 2)(source_2)
        for p in range(6):
            pl.when(t == GATHER_AT + 1 + p)(functools.partial(small_phase, p))
        for k in late:
            pl.when(t + 1 == k)(functools.partial(fetch, k))
        return carry

    lax.fori_loop(0, n_chunks + 9, step, 0)
    for i, (src, dst) in enumerate(((block_ref, block_home), (src_b, source_home), (tokens_out, tokens_home))):
        send_home(i, src, dst, True)


def finish_backward(plan, attention, local, small, sources, weights, memory_weights):
    n_chunks = len(plan)
    q, k, v, mix, lse, seg = attention
    n, width = q.shape
    rows, d = local[0].shape
    source_rows = sources[-1].shape[0]
    hbm = pl.BlockSpec(memory_space=pltpu.HBM)
    vmem = pl.BlockSpec(memory_space=pltpu.VMEM)
    dma = pltpu.SemaphoreType.DMA
    sets = len(SETS)
    near = [q, k, v, mix, lse, seg.reshape(n, 1), seg.reshape(1, n), *local, small]
    ring = lambda rows: pltpu.VMEM((RING, rows, WD), BF)
    return pl.pallas_call(
        functools.partial(finish_kernel, plan, len(sources)),
        out_shape=(
            jax.ShapeDtypeStruct((n_chunks, CH, WD), BF),
            jax.ShapeDtypeStruct(small.shape, F32),
            jax.ShapeDtypeStruct((rows, d), BF),
            jax.ShapeDtypeStruct((rows, d), BF),
            jax.ShapeDtypeStruct((source_rows // 4, d), BF),
            jax.ShapeDtypeStruct((rows, 12 * width), BF),
        ),
        in_specs=[vmem] * len(near) + [hbm] * (len(sources) + 2),
        out_specs=(hbm, vmem, hbm, hbm, hbm, hbm),
        scratch_shapes=[pltpu.VMEM((n, width), BF)] * 4
        + [
            pltpu.VMEM((4, n, LANES), BF),
            pltpu.VMEM((4, n, LANES), BF),
            pltpu.VMEM((width, n), BF),
            pltpu.VMEM((width, n), F32),
            pltpu.VMEM((TILE, width), F32),
            pltpu.VMEM((TILE, width), F32),
            pltpu.VMEM((8, n), F32),
        ]
        + trade_semaphores(n // TILE, 3)
        + [pltpu.VMEM(shape, BF) for shape in ((rows, d), (source_rows, d), (source_rows // 2, d), (source_rows // 4, d), (source_rows // 2, d), (source_rows // 4, d))]
        + [dma((3,)), dma((3,)), dma((3,)), dma((2,)), dma((2,)), dma((3,)), dma((3,))]
        + [pltpu.VMEM((KEEP, CH, WD), BF), pltpu.VMEM((2, CH, WD), BF)]
        + [ring(CH >> q) for q in range(5)]
        + [
            pltpu.VMEM((6,) + small.shape, F32),
            pltpu.VMEM((5,) + small.shape, F32),
            pltpu.VMEM((2, source_rows, 2 * CH), BF),
            pltpu.VMEM((2, source_rows, WD), BF),
            pltpu.VMEM(weights.shape, BF),
            pltpu.VMEM((128, 12 * width), BF),
            dma((2, 2)),
            dma((2,)),
            dma((1,)),
            dma((1,)),
            dma((2,)),
            dma((n_chunks,)),
            dma((n_chunks,)),
            dma((n_chunks, sets, 4)),
            dma((n_chunks, sets, 4)),
            dma((n_chunks, sets, 4)),
            dma((n_chunks, sets, 4)),
            dma((n_chunks, sets)),
            dma((5,)),
            dma((5,)),
        ],
        compiler_params=pltpu.CompilerParams(collective_id=1, has_side_effects=True, vmem_limit_bytes=62 << 20),
        cost_estimate=pl.CostEstimate(flops=200 << 30, bytes_accessed=50 << 20, transcendentals=0),
        name="finish_backward",
    )(*near, *sources, weights, memory_weights)


def widen_kernel(ranges, *refs):
    j = pl.program_id(0)
    src, outs = refs[0], refs[1:]
    for (first, count, _), out in zip(ranges, outs):

        @pl.when((j >= first) & (j < first + count))
        def _():
            out[...] = src[0].astype(F32)


def widen(summed, pieces):
    ranges, first = [], 0
    for kind, count in pieces:
        ranges.append((first, count, kind))
        first += count

    def spec(first, count, kind):
        def index(j):
            k = jnp.clip(j - first, 0, count - 1)
            return (0, k) if kind == "cols" else (k, 0)

        return pl.BlockSpec((CH, WD), index)

    return pl.pallas_call(
        functools.partial(widen_kernel, tuple(ranges)),
        grid=(first,),
        out_shape=[
            jax.ShapeDtypeStruct((CH, WD * count) if kind == "cols" else (CH * count, WD), F32) for _, count, kind in ranges
        ],
        in_specs=[pl.BlockSpec((1, CH, WD), lambda j: (j, 0, 0))],
        out_specs=[spec(*r) for r in ranges],
        compiler_params=pltpu.CompilerParams(vmem_limit_bytes=48 << 20),
        cost_estimate=pl.CostEstimate(flops=0, bytes_accessed=6 * CH * WD * first, transcendentals=0),
        name="widen",
    )(summed)


def feed_kernel(x_ref, grad_ref, second_ref, down_bias, up_bias, up_ref, down_ref, hidden_ref, hidden_grad_ref, bias_grad_ref, block_ref, e_ref, acc):
    j = pl.program_id(0)

    @pl.when(j == 0)
    def _():
        acc[...] = jnp.zeros_like(acc)
        e_ref[...] = jnp.zeros_like(e_ref)

    step = 256
    total = jnp.zeros(bias_grad_ref.shape, F32)
    for k in range(x_ref.shape[0] // step):
        rows = pl.ds(k * step, step)
        before = dot_nn(x_ref[rows, :], up_ref[...]) + up_bias[...]
        change = dot_nt(grad_ref[rows, :], down_ref[...])
        below = 0.5 + 0.5 * lax.erf(before * math.sqrt(0.5))
        slope = below + before * jnp.exp(-0.5 * before * before) * (1.0 / math.sqrt(2.0 * math.pi))
        hidden = (before * below).astype(BF)
        hidden_grad = (change * slope).astype(BF)
        hidden_ref[rows, :] = hidden
        hidden_grad_ref[rows, :] = hidden_grad
        total = total + jnp.sum(hidden_grad.astype(F32), axis=0, keepdims=True)
        acc[rows, :] += dot_nn(hidden, down_ref[...])
        e_ref[rows, :] += dot_nt(hidden_grad, up_ref[...])
    bias_grad_ref[...] = total

    @pl.when(j == pl.num_programs(0) - 1)
    def _():
        block_ref[...] = (second_ref[...] + acc[...] + down_bias[...]).astype(BF)


def feed(x, grad, second, up, up_bias, down, down_bias):
    n, d = x.shape
    width, tile = up.shape[1], 512
    whole = lambda shape: pl.BlockSpec(shape, lambda j: (0, 0))
    column = lambda rows: pl.BlockSpec((rows, tile), lambda j: (0, j))
    return pl.pallas_call(
        feed_kernel,
        grid=(width // tile,),
        out_shape=(
            jax.ShapeDtypeStruct((n, width), BF),
            jax.ShapeDtypeStruct((n, width), BF),
            jax.ShapeDtypeStruct((1, width), F32),
            jax.ShapeDtypeStruct((n, d), BF),
            jax.ShapeDtypeStruct((n, d), F32),
        ),
        in_specs=[whole((n, d))] * 3 + [whole((1, d)), column(1), column(d), pl.BlockSpec((tile, d), lambda j: (j, 0))],
        out_specs=(column(n), column(n), column(1), whole((n, d)), whole((n, d))),
        scratch_shapes=[pltpu.VMEM((n, d), F32)],
        compiler_params=pltpu.CompilerParams(vmem_limit_bytes=48 << 20),
        cost_estimate=pl.CostEstimate(flops=16 * n * d * width, bytes_accessed=4 * d * width, transcendentals=2 * n * width),
        name="feed",
    )(x, grad, second, down_bias.reshape(1, d), up_bias.reshape(1, width), up, down)


TOKEN_PARTS = 8


def spread_kernel(n_mats, *refs):
    tok, seg = refs[:2]
    mats = refs[2 : 2 + n_mats]
    tok_all, seg_all = refs[2 + n_mats : 4 + n_mats]
    fulls = refs[4 + n_mats : 4 + 2 * n_mats]
    stage = refs[4 + 2 * n_mats : 4 + 3 * n_mats]
    tok_stage, seg_stage = refs[4 + 3 * n_mats : 6 + 3 * n_mats]
    (mat_load, mat_put, mat_send, mat_recv, own_load, own_put, far_send, far_recv, sib_send, sib_recv, near_send, near_recv, pass_send, pass_recv) = refs[6 + 3 * n_mats :]
    sib, near, diag, far, block, near_block, sib_block, diag_block, home = pair_places()
    _, _, z, c = coords()
    greet((sib, near, far))
    rows = tok.shape[0]
    part = rows // TOKEN_PARTS
    n_items = TOKEN_PARTS + 1

    def source(k):
        return seg if k == TOKEN_PARTS else tok.at[pl.ds(k * part, part), :]

    def place(k, b):
        if k == TOKEN_PARTS:
            return seg_all.at[b]
        return tok_all.at[pl.ds(pl.multiple_of(b * rows + k * part, part), part), :]

    def remote(src, dst, send, recv, device):
        return pltpu.make_async_remote_copy(src_ref=src, dst_ref=dst, send_sem=send, recv_sem=recv, device_id=device, device_id_type=MESH)

    def far_copy(k):
        return remote(source(k), place(k, z), far_send.at[k], far_recv.at[k], far)

    def staged(k):
        return seg_stage if k == TOKEN_PARTS else tok_stage.at[pl.ds(k * part, part), :]

    def own_copy(k):
        return pltpu.make_async_copy(source(k), staged(k), own_load.at[k])

    def own_out(k):
        return pltpu.make_async_copy(staged(k), place(k, block), own_put.at[k])

    def sib_copy(k):
        return remote(place(k, block), place(k, block), sib_send.at[k], sib_recv.at[k], sib)

    def near_copy(k):
        return remote(place(k, block), place(k, block), near_send.at[k], near_recv.at[k], near)

    def pass_copy(k):
        return remote(place(k, near_block), place(k, near_block), pass_send.at[k], pass_recv.at[k], sib)

    @pl.when(home)
    def _():
        for k in range(n_items):
            own_copy(k).start()

    @pl.when(jnp.logical_not(home))
    def _():
        for k in range(n_items):
            far_copy(k).start()

    def mat_target(i):
        half = mats[i].shape[0]
        return fulls[i].at[pl.ds(pl.multiple_of(c * half, 8), half), :]

    def mat_in(i):
        return pltpu.make_async_copy(mats[i], stage[i], mat_load.at[i])

    def mat_out(i):
        return pltpu.make_async_copy(stage[i], mat_target(i), mat_put.at[i])

    def mat_remote(i):
        return remote(mats[i], mat_target(i), mat_send.at[i], mat_recv.at[i], sib)

    for i in range(n_mats):
        mat_in(i).start()
        mat_remote(i).start()

    for k in range(n_items + 1):
        if k < n_items:

            @pl.when(home)
            def _():
                own_copy(k).wait()
                own_out(k).start()
                own_out(k).wait()

            @pl.when(jnp.logical_not(home))
            def _():
                far_copy(k).wait()

            sib_copy(k).start()
            near_copy(k).start()
        if k > 0:
            near_copy(k - 1).wait()
            pass_copy(k - 1).start()
    for i in range(n_mats):
        mat_in(i).wait()
        mat_out(i).start()
    for k in range(n_items):
        sib_copy(k).wait()
        pass_copy(k).wait()
    for i in range(n_mats):
        mat_out(i).wait()
        mat_remote(i).wait()


def spread(tokens, seg, mats):
    n = len(mats)
    any_spec = pl.BlockSpec(memory_space=pltpu.HBM)
    dma = pltpu.SemaphoreType.DMA
    items = TOKEN_PARTS + 1
    return pl.pallas_call(
        functools.partial(spread_kernel, n),
        out_shape=[
            jax.ShapeDtypeStruct((4 * tokens.shape[0], tokens.shape[1]), tokens.dtype),
            jax.ShapeDtypeStruct((4,) + seg.shape, seg.dtype),
        ]
        + [jax.ShapeDtypeStruct((2 * m.shape[0], m.shape[1]), m.dtype) for m in mats],
        in_specs=[any_spec] * (2 + n),
        out_specs=[any_spec] * (2 + n),
        scratch_shapes=[pltpu.VMEM(a.shape, a.dtype) for a in (*mats, tokens, seg)] + [dma((n,))] * 4 + [dma((items,))] * 10,
        compiler_params=pltpu.CompilerParams(collective_id=2, has_side_effects=True, vmem_limit_bytes=60 << 20),
        cost_estimate=pl.CostEstimate(flops=0, bytes_accessed=64 << 20, transcendentals=0),
        name="spread",
    )(tokens, seg, *mats)


def project_kernel(scale, block_ref, tok, gain, shift, wq, wk, wv, bq, bv, q_ref, k_ref, v_ref):
    del block_ref
    normed = norm_rows(tok[...].astype(F32), gain[...], shift[...]).astype(BF)
    q_ref[...] = ((product(normed, wq[...]) + bq[...]) * scale).astype(BF)
    k_ref[...] = product(normed, wk[...]).astype(BF)
    v_ref[...] = (product(normed, wv[...]) + bv[...]).astype(BF)


def project(block, tokens_all, gain, shift, weights, query_bias, value_bias, scale):
    n, d = tokens_all.shape
    width, step = d // 4, 256
    row = lambda i, b: (i, 0)
    fixed = lambda i, b: (0, 0)
    weight = lambda part: pl.BlockSpec((d, width), lambda i, b: (0, 4 * part + b[0]))
    return pl.pallas_call(
        functools.partial(project_kernel, scale),
        grid_spec=pltpu.PrefetchScalarGridSpec(
            num_scalar_prefetch=1,
            grid=(n // step,),
            in_specs=[pl.BlockSpec((step, d), row), pl.BlockSpec((1, d), fixed), pl.BlockSpec((1, d), fixed)]
            + [weight(part) for part in range(3)]
            + [pl.BlockSpec((1, width), lambda i, b: (0, b[0]))] * 2,
            out_specs=[pl.BlockSpec((step, width), row)] * 3,
        ),
        out_shape=[jax.ShapeDtypeStruct((n, width), BF)] * 3,
        compiler_params=pltpu.CompilerParams(vmem_limit_bytes=60 << 20),
        cost_estimate=pl.CostEstimate(flops=6 * n * d * width, bytes_accessed=4 * n * d, transcendentals=0),
        name="project",
    )(block.reshape(1).astype(jnp.int32), tokens_all, gain.reshape(1, d), shift.reshape(1, d), weights, weights, weights,
      query_bias.reshape(1, d), value_bias.reshape(1, d))


def owner_of(z, c):
    return (z, c) if z // 2 == c else ((z + 2) % 4, 1 - c)


def flat(z, c):
    return 2 * z + c


CORES = [(z, c) for z in range(4) for c in range(2)]
SWAP = [(flat(z, c), flat(*owner_of(z, c))) for z, c in CORES if owner_of(z, c) != (z, c)]
HOME_TO_NEAR = [(flat(z, c), flat(owner_of(z, c)[0] ^ 1, owner_of(z, c)[1])) for z, c in CORES]
SIB = [(0, 1), (1, 0)]


def is_home():
    return lax.div(lax.axis_index("ctx"), 2) == lax.axis_index("shard")


def swap(array):
    return jnp.where(is_home(), array, lax.ppermute(array, ("ctx", "shard"), SWAP))


VECTORS = (0, 1, 3, 4, 6, 7, 8, 10, 12, 14, 15, 16, 18, 20)
MATRICES = (17, 19, 13, 9, 5, 11, 2)


def pair_device(
    tokens, source, segment_ids, positions, cotangent,
    self_gain, self_shift, self_weights, query_bias, value_bias, self_output, output_bias,
    cross_gain, cross_shift, cross_query, query_offset, cross_memory, memory_offset, cross_output, return_bias,
    feed_gain, feed_shift, feed_up, up_bias, feed_down, down_bias,
):
    c, z = lax.axis_index("shard"), lax.axis_index("ctx")
    block = 2 * c + lax.rem(z, 2)
    head_scale = 1.0 / math.sqrt(HEAD_DIM)
    rows = tokens.shape[1]
    vectors = (
        self_gain, self_shift, query_bias, value_bias, output_bias, cross_gain, cross_shift, query_offset, memory_offset,
        return_bias, feed_gain, feed_shift, down_bias, up_bias,
    )
    half = D // 2
    n_packed = sum(v.shape[0] for v in vectors) // half
    packed_rows = n_packed + -n_packed % 16
    packed, at = jnp.zeros((packed_rows * half,), F32), 0
    for v in vectors:
        packed = packed + jnp.pad(v.astype(F32), (at, packed_rows * half - at - v.shape[0]))
        at += v.shape[0]
    packed = packed.astype(BF).reshape(packed_rows, half)
    mats = (self_weights, self_output, cross_memory, cross_query, cross_output, feed_up, feed_down, packed)
    spread_out = spread(tokens[0], segment_ids.reshape(4, rows // 4), mats)
    tokens_all, seg_all = spread_out[:2]
    self_weights, self_output, cross_memory, cross_query, cross_output, feed_up, feed_down, packed = spread_out[2:]
    tokens_all, source_home = lax.optimization_barrier((tokens_all, source[0]))
    own_source = swap(source_home)
    near_source = lax.ppermute(source_home, ("ctx", "shard"), HOME_TO_NEAR)
    chip_source = jnp.concatenate([own_source, near_source], axis=0)
    source_all = lax.optimization_barrier(jnp.concatenate([chip_source, lax.ppermute(chip_source, "shard", SIB)], axis=0))
    packed = packed.astype(F32).reshape(2, -1, half)
    unpacked = [packed[:, i].reshape(D) for i in range(13)]
    (
        self_gain, self_shift, query_bias, value_bias, output_bias, cross_gain, cross_shift, query_offset, memory_offset,
        return_bias, feed_gain, feed_shift, down_bias,
    ) = unpacked
    up_bias = packed[:, 13:n_packed].reshape(-1)
    seg = seg_all.reshape(-1)

    width = D // 4
    q, k, v = project(block, tokens_all, self_gain, self_shift, self_weights, query_bias, value_bias, head_scale)
    mix_heads, lse_self, mixed_self = attention_forward(q, k, v, seg)
    mixed_self, out_grad_home = lax.optimization_barrier((mixed_self, cotangent[0]))
    out_grad_far = lax.ppermute(out_grad_home, ("ctx", "shard"), SWAP)

    tok_low = lax.dynamic_slice_in_dim(tokens_all, block * rows, rows, 0)
    tok_rows = tok_low.astype(F32)
    normed_self = norm_rows(tok_rows, self_gain, self_shift).astype(BF)
    first_sum = tok_rows + product(mixed_self, self_output) + output_bias
    normed_cross = norm_rows(first_sum, cross_gain, cross_shift).astype(BF)
    cross_q = ((product(normed_cross, cross_query) + query_offset) * head_scale).astype(BF)
    memory = product(source_all, cross_memory)
    cross_keys = memory[:, :D].astype(BF)
    cross_values = (memory[:, D:] + memory_offset).astype(BF)
    mixed_cross, lse_cross = attention_forward(cross_q, cross_keys, cross_values)
    mixed_cross, out_grad_far = lax.optimization_barrier((mixed_cross, out_grad_far))
    out_grad = jnp.where(is_home(), out_grad_home, out_grad_far)
    second = first_sum + product(mixed_cross, cross_output) + return_bias
    normed_feed = norm_rows(second, feed_gain, feed_shift).astype(BF)
    hidden, hidden_grad, up_bias_grad, block_output, feed_e = feed(
        normed_feed, out_grad, second, feed_up, up_bias, feed_down, down_bias
    )
    up_bias_grad = up_bias_grad.reshape(-1)
    down_bias_grad = jnp.sum(out_grad, axis=0, dtype=F32)
    _, feed_pull = jax.vjp(norm_rows, second, feed_gain, feed_shift)
    second_part, feed_gain_grad, feed_shift_grad = feed_pull(feed_e)
    second_grad = out_grad.astype(F32) + second_part
    branch_cross = second_grad.astype(BF)
    return_bias_grad = jnp.sum(second_grad, axis=0)
    mixed_cross_grad = right_product(branch_cross, cross_output).astype(BF)
    cross_sum, key_terms, value_terms = attention_backward(
        cross_q, cross_keys, cross_values, mixed_cross_grad, mixed_cross, lse_cross
    )

    memory_offset_grad = jnp.sum(value_terms, axis=0, dtype=F32)
    cross_q_grad = cross_sum * head_scale
    query_offset_grad = jnp.sum(cross_q_grad, axis=0, dtype=F32)
    _, cross_pull = jax.vjp(norm_rows, first_sum, cross_gain, cross_shift)
    first_part, cross_gain_grad, cross_shift_grad = cross_pull(right_product(cross_q_grad, cross_query))
    first_grad = second_grad + first_part
    branch_self = first_grad.astype(BF)
    output_bias_grad = jnp.sum(first_grad, axis=0)
    mixed_self_grad = right_product(branch_self, self_output).astype(BF)
    unknown = jnp.zeros((D,), F32)
    vectors = (
        unknown, unknown, unknown, unknown, output_bias_grad, cross_gain_grad, cross_shift_grad, query_offset_grad,
        memory_offset_grad, return_bias_grad, feed_gain_grad, feed_shift_grad, up_bias_grad, down_bias_grad,
    )
    small = jnp.concatenate([v.reshape(-1, D) for v in vectors], axis=0)
    small = jnp.pad(small, ((0, -small.shape[0] % 8), (0, 0)))
    sources = (
        normed_feed, hidden_grad, hidden, out_grad, mixed_cross, branch_cross, normed_cross, cross_q_grad, mixed_self, branch_self,
        normed_self, source_all, key_terms, value_terms,
    )
    chunks = feed_up.shape[1] // D
    plan = (
        tuple((0, "cols", 0, 1, i) for i in range(chunks))
        + tuple((2, "rows", i, 3, 0) for i in range(chunks))
        + ((4, "cols", 0, 5, 0), (6, "cols", 0, 7, 0), (8, "cols", 0, 9, 0), (11, "cols", 0, 12, 0), (11, "cols", 0, 13, 0))
        + tuple((10, "cols", 0, len(sources), i) for i in range(3))
    )
    pieces = (("cols", chunks), ("rows", chunks), ("cols", 1), ("cols", 1), ("cols", 1), ("cols", 2), ("cols", 3))
    summed, small_sum, tokens_grad, block_home, source_grad, _ = finish_backward(
        plan,
        (q, k, v, mix_heads, lse_self.reshape(8, -1), seg),
        (mixed_self_grad, block_output, tok_low, first_grad, self_gain.reshape(1, D)),
        small,
        sources,
        self_weights,
        cross_memory,
    )
    results = {}
    for place, matrix in zip(MATRICES, widen(summed, pieces)):
        results[place] = matrix
    at = 0
    for place, v in zip(VECTORS, vectors):
        rows_of, size = v.shape[0] // D, v.shape[0]
        results[place] = lax.dynamic_slice_in_dim(small_sum[at : at + rows_of].reshape(size), c * (size // 2), size // 2, 0)
        at += rows_of
    return (
        block_home[None],
        tokens_grad.astype(F32)[None],
        source_grad.astype(F32)[None],
    ) + tuple(results[place] for place in sorted(results))


def per_device(
    tokens,
    source,
    segment_ids,
    positions,
    cotangent,
    self_gain,
    self_shift,
    self_weights,
    query_bias,
    value_bias,
    self_output,
    output_bias,
    cross_gain,
    cross_shift,
    cross_query,
    query_offset,
    cross_memory,
    memory_offset,
    cross_output,
    return_bias,
    feed_gain,
    feed_shift,
    feed_up,
    up_bias,
    feed_down,
    down_bias,
):
    (
        self_gain,
        self_shift,
        self_weights,
        query_bias,
        value_bias,
        self_output,
        output_bias,
        cross_gain,
        cross_shift,
        cross_query,
        query_offset,
        cross_memory,
        memory_offset,
        cross_output,
        return_bias,
        feed_gain,
        feed_shift,
        feed_up,
        up_bias,
        feed_down,
        down_bias,
    ) = (
        lax.all_gather(self_gain, "shard", axis=0, tiled=True),
        lax.all_gather(self_shift, "shard", axis=0, tiled=True),
        lax.all_gather(self_weights, "shard", axis=0, tiled=True),
        lax.all_gather(query_bias, "shard", axis=0, tiled=True),
        lax.all_gather(value_bias, "shard", axis=0, tiled=True),
        lax.all_gather(self_output, "shard", axis=0, tiled=True),
        lax.all_gather(output_bias, "shard", axis=0, tiled=True),
        lax.all_gather(cross_gain, "shard", axis=0, tiled=True),
        lax.all_gather(cross_shift, "shard", axis=0, tiled=True),
        lax.all_gather(cross_query, "shard", axis=0, tiled=True),
        lax.all_gather(query_offset, "shard", axis=0, tiled=True),
        lax.all_gather(cross_memory, "shard", axis=0, tiled=True),
        lax.all_gather(memory_offset, "shard", axis=0, tiled=True),
        lax.all_gather(cross_output, "shard", axis=0, tiled=True),
        lax.all_gather(return_bias, "shard", axis=0, tiled=True),
        lax.all_gather(feed_gain, "shard", axis=0, tiled=True),
        lax.all_gather(feed_shift, "shard", axis=0, tiled=True),
        lax.all_gather(feed_up, "shard", axis=0, tiled=True),
        lax.all_gather(up_bias, "shard", axis=0, tiled=True),
        lax.all_gather(feed_down, "shard", axis=0, tiled=True),
        lax.all_gather(down_bias, "shard", axis=0, tiled=True),
    )
    head_scale = 1.0 / math.sqrt(HEAD_DIM)
    row_count = tokens.shape[1]
    tok_rows = tokens[0].astype(jnp.float32)
    source_rows = source[0]
    tag_seg, tag_pos = (
        lax.all_gather(segment_ids, "ctx", axis=1, tiled=True),
        lax.all_gather(positions, "ctx", axis=1, tiled=True),
    )
    tag_bundle = (segment_ids[0], positions[0], tag_seg[0], tag_pos[0])
    gain_self = self_gain.astype(jnp.float32)
    shift_self = self_shift.astype(jnp.float32)
    normed_self = norm_rows(tok_rows, gain_self, shift_self).astype(jnp.bfloat16)
    projected = product(normed_self, self_weights)
    queries = ((projected[:, :D] + query_bias.astype(jnp.float32)) * head_scale).astype(
        jnp.bfloat16
    )
    keys_self = projected[:, D : 2 * D].astype(jnp.bfloat16)
    values_self = (projected[:, 2 * D :] + value_bias.astype(jnp.float32)).astype(jnp.bfloat16)
    query_heads = heads_of(queries)
    start_state = (
        jnp.full((HEADS, row_count), NEGATIVE, jnp.float32),
        jnp.zeros((HEADS, row_count), jnp.float32),
        jnp.zeros((row_count, HEADS, HEAD_DIM), jnp.float32),
    )
    folded_self = attend_piece(
        start_state,
        query_heads,
        lax.all_gather(keys_self, "ctx", axis=0, tiled=True),
        lax.all_gather(values_self, "ctx", axis=0, tiled=True),
        tag_bundle,
    )
    attended_self, total_self = finish(folded_self)
    mixed_self = attended_self.reshape(row_count, D).astype(jnp.bfloat16)
    first_sum = tok_rows + product(mixed_self, self_output) + output_bias.astype(jnp.float32)
    gain_cross = cross_gain.astype(jnp.float32)
    shift_cross = cross_shift.astype(jnp.float32)
    normed_cross = norm_rows(first_sum, gain_cross, shift_cross).astype(jnp.bfloat16)
    cross_q = (
        (product(normed_cross, cross_query) + query_offset.astype(jnp.float32)) * head_scale
    ).astype(jnp.bfloat16)
    memory = product(source_rows, cross_memory)
    memory_keys = memory[:, :D].astype(jnp.bfloat16)
    memory_values = (memory[:, D:] + memory_offset.astype(jnp.float32)).astype(jnp.bfloat16)
    cross_keys, cross_values = (
        lax.all_gather(memory_keys, "ctx", axis=0, tiled=True),
        lax.all_gather(memory_values, "ctx", axis=0, tiled=True),
    )
    cross_heads = heads_of(cross_q)
    attended_cross, total_cross = finish(
        attend_piece(start_state, cross_heads, cross_keys, cross_values, None)
    )
    mixed_cross = attended_cross.reshape(row_count, D).astype(jnp.bfloat16)
    second = first_sum + product(mixed_cross, cross_output) + return_bias.astype(jnp.float32)
    gain_feed = feed_gain.astype(jnp.float32)
    shift_feed = feed_shift.astype(jnp.float32)
    normed_feed = norm_rows(second, gain_feed, shift_feed).astype(jnp.bfloat16)
    hidden_pre = product(normed_feed, feed_up) + up_bias.astype(jnp.float32)
    hidden_act, gelu_pull = jax.vjp(exact_gelu, hidden_pre)
    hidden = hidden_act.astype(jnp.bfloat16)
    block_output = (second + product(hidden, feed_down) + down_bias.astype(jnp.float32)).astype(
        jnp.bfloat16
    )
    out_grad = cotangent[0]
    down_grad = left_product(hidden, out_grad)
    down_bias_grad = jnp.sum(out_grad, axis=0, dtype=jnp.float32)
    (hidden_grad,) = gelu_pull(right_product(out_grad, feed_down))
    hidden_grad = hidden_grad.astype(jnp.bfloat16)
    up_grad = left_product(normed_feed, hidden_grad)
    up_bias_grad = jnp.sum(hidden_grad, axis=0, dtype=jnp.float32)
    norm_value, feed_pull = jax.vjp(norm_rows, second, gain_feed, shift_feed)
    second_part, feed_gain_grad, feed_shift_grad = feed_pull(right_product(hidden_grad, feed_up))
    second_grad = out_grad.astype(jnp.float32) + second_part
    branch_cross = second_grad.astype(jnp.bfloat16)
    cross_output_grad = left_product(mixed_cross, branch_cross)
    return_bias_grad = jnp.sum(second_grad, axis=0)
    mixed_cross_grad = right_product(branch_cross, cross_output).astype(jnp.bfloat16)
    cross_grad_heads = heads_of(mixed_cross_grad)
    cross_delta = row_deltas(cross_grad_heads, attended_cross)
    cross_sum, key_terms, value_terms = attend_back(
        cross_heads, cross_keys, cross_values, cross_grad_heads, cross_delta, total_cross, None
    )
    key_part, value_part = (
        lax.psum_scatter(
            key_terms.astype(jnp.bfloat16), "ctx", scatter_dimension=0, tiled=True
        ).astype(jnp.float32),
        lax.psum_scatter(
            value_terms.astype(jnp.bfloat16), "ctx", scatter_dimension=0, tiled=True
        ).astype(jnp.float32),
    )
    memory_grad = jnp.concatenate(
        [key_part.astype(jnp.bfloat16), value_part.astype(jnp.bfloat16)], axis=1
    )
    source_grad = right_product(memory_grad, cross_memory)
    cross_memory_grad = left_product(source_rows, memory_grad)
    memory_offset_grad = jnp.sum(memory_grad[:, D:], axis=0, dtype=jnp.float32)
    cross_q_grad = cross_sum.astype(jnp.bfloat16) * head_scale
    cross_query_grad = left_product(normed_cross, cross_q_grad)
    query_offset_grad = jnp.sum(cross_q_grad, axis=0, dtype=jnp.float32)
    norm_value, cross_pull = jax.vjp(norm_rows, first_sum, gain_cross, shift_cross)
    first_part, cross_gain_grad, cross_shift_grad = cross_pull(
        right_product(cross_q_grad, cross_query)
    )
    first_grad = second_grad + first_part
    branch_self = first_grad.astype(jnp.bfloat16)
    self_output_grad = left_product(mixed_self, branch_self)
    output_bias_grad = jnp.sum(first_grad, axis=0)
    mixed_self_grad = right_product(branch_self, self_output).astype(jnp.bfloat16)
    keys_back, values_back = (
        lax.all_gather(keys_self, "ctx", axis=0, tiled=True),
        lax.all_gather(values_self, "ctx", axis=0, tiled=True),
    )
    self_grad_heads = heads_of(mixed_self_grad)
    self_delta = row_deltas(self_grad_heads, attended_self)
    query_sum, key_terms_self, value_terms_self = attend_back(
        query_heads, keys_back, values_back, self_grad_heads, self_delta, total_self, tag_bundle
    )
    key_own, value_own = (
        lax.psum_scatter(
            key_terms_self.astype(jnp.bfloat16), "ctx", scatter_dimension=0, tiled=True
        ).astype(jnp.float32),
        lax.psum_scatter(
            value_terms_self.astype(jnp.bfloat16), "ctx", scatter_dimension=0, tiled=True
        ).astype(jnp.float32),
    )
    query_grad = query_sum.astype(jnp.bfloat16) * head_scale
    value_grad = value_own.astype(jnp.bfloat16)
    projected_grad = jnp.concatenate([query_grad, key_own.astype(jnp.bfloat16), value_grad], axis=1)
    self_weights_grad = left_product(normed_self, projected_grad)
    query_bias_grad = jnp.sum(query_grad, axis=0, dtype=jnp.float32)
    value_bias_grad = jnp.sum(value_grad, axis=0, dtype=jnp.float32)
    norm_value, self_pull = jax.vjp(norm_rows, tok_rows, gain_self, shift_self)
    token_part, self_gain_grad, self_shift_grad = self_pull(
        right_product(projected_grad, self_weights)
    )
    tokens_grad = first_grad + token_part
    gradients = (
        self_gain_grad,
        self_shift_grad,
        self_weights_grad,
        query_bias_grad,
        value_bias_grad,
        self_output_grad,
        output_bias_grad,
        cross_gain_grad,
        cross_shift_grad,
        cross_query_grad,
        query_offset_grad,
        cross_memory_grad,
        memory_offset_grad,
        cross_output_grad,
        return_bias_grad,
        feed_gain_grad,
        feed_shift_grad,
        up_grad,
        up_bias_grad,
        down_grad,
        down_bias_grad,
    )
    halves = [lax.psum_scatter(g.astype(BF), "shard", scatter_dimension=0, tiled=True).astype(F32) for g in gradients]
    reduced = lax.psum(tuple(halves), ("group", "ctx"))
    return (block_output[None], tokens_grad[None], source_grad[None]) + tuple(reduced)


def solution(mesh):
    near = (mesh.shape["group"], mesh.shape["ctx"], mesh.shape["shard"]) == (4, 4, 2)
    placed = (
        P(("group", "shard"), "ctx", None),
        P(("group", "shard"), "ctx", None),
        P(("group", "shard"), "ctx"),
        P(("group", "shard"), "ctx"),
        P(("group", "shard"), "ctx", None),
        P("shard"),
        P("shard"),
        P("shard", None),
        P("shard"),
        P("shard"),
        P("shard", None),
        P("shard"),
        P("shard"),
        P("shard"),
        P("shard", None),
        P("shard"),
        P("shard", None),
        P("shard"),
        P("shard", None),
        P("shard"),
        P("shard"),
        P("shard"),
        P("shard", None),
        P("shard"),
        P("shard", None),
        P("shard"),
    )
    return jax.shard_map(
        pair_device if near else per_device,
        mesh=mesh,
        in_specs=placed,
        out_specs=(
            P(("group", "shard"), "ctx", None),
            P(("group", "shard"), "ctx", None),
            P(("group", "shard"), "ctx", None),
            P("shard"),
            P("shard"),
            P("shard", None),
            P("shard"),
            P("shard"),
            P("shard", None),
            P("shard"),
            P("shard"),
            P("shard"),
            P("shard", None),
            P("shard"),
            P("shard", None),
            P("shard"),
            P("shard", None),
            P("shard"),
            P("shard"),
            P("shard"),
            P("shard", None),
            P("shard"),
            P("shard", None),
            P("shard"),
        ),
        check_vma=False,
    )
```

```python
import functools
import math

import jax
import jax.numpy as jnp
from jax import lax
from jax.experimental import pallas as pl
from jax.experimental.pallas import tpu as pltpu
from jax.sharding import PartitionSpec as P

MESH = pl.DeviceIdType.MESH
BF = jnp.bfloat16
F32 = jnp.float32


def coords():
    g, z, c = lax.axis_index("group"), lax.axis_index("ctx"), lax.axis_index("shard")
    return lax.rem(g, 2), lax.div(g, 2), z, c


def device_of(x, y, z, c):
    return (y * 2 + x, z, c)


def greet(devices):
    barrier = pltpu.get_barrier_semaphore()
    for device in devices:
        pl.semaphore_signal(barrier, inc=1, device_id=device, device_id_type=MESH)
    pl.semaphore_wait(barrier, len(devices))


D = 1024
HEADS = 16
HEAD_DIM = 64


EPSILON = 1e-05
NEGATIVE = -1e30


def norm_rows(values, gain_vec, shift_vec):
    average = jnp.mean(values, axis=-1, keepdims=True)
    centred = values - average
    spread = jnp.mean(centred * centred, axis=-1, keepdims=True)
    return centred * lax.rsqrt(spread + EPSILON) * gain_vec + shift_vec


def exact_gelu(values):
    return jax.nn.gelu(values, approximate=False)


def product(left_side, right_side):
    return jnp.dot(left_side, right_side, preferred_element_type=jnp.float32)


def left_product(left_side, right_side):
    return lax.dot_general(
        left_side, right_side, (((0,), (0,)), ((), ())), preferred_element_type=jnp.float32
    )


def right_product(left_side, right_side):
    return lax.dot_general(
        left_side, right_side, (((1,), (1,)), ((), ())), preferred_element_type=jnp.float32
    )


def heads_of(matrix):
    return matrix.reshape(matrix.shape[0], HEADS, HEAD_DIM)


def allow_table(query_seg, query_pos, key_seg, key_pos):
    shared = (key_seg[None, :] == 0) | (key_seg[None, :] == query_seg[:, None])
    return shared & (key_pos[None, :] <= query_pos[:, None])


def fold_keys(folded, queries, key_block, value_block, allowed):
    run_max, run_sum, weighted = folded
    scores = jnp.einsum("qhd,khd->hqk", queries, key_block, preferred_element_type=jnp.float32)
    if allowed is not None:
        scores = jnp.where(allowed[None], scores, NEGATIVE)
    new_max = jnp.maximum(run_max, jnp.max(scores, axis=2))
    factor = jnp.exp(run_max - new_max)
    weighting = jnp.exp(scores - new_max[:, :, None])
    new_sum = run_sum * factor + jnp.sum(weighting, axis=2)
    update = jnp.einsum(
        "hqk,khd->qhd",
        weighting.astype(jnp.bfloat16),
        value_block,
        preferred_element_type=jnp.float32,
    )
    return (new_max, new_sum, weighted * jnp.transpose(factor)[:, :, None] + update)


def attend_piece(folded, queries, key_piece, value_piece, tag_bundle):
    count_rows = key_piece.shape[0]
    block_rows = math.gcd(count_rows, 512)

    def one_block(number, current):
        offset = number * block_rows
        key_block = heads_of(lax.dynamic_slice_in_dim(key_piece, offset, block_rows, 0))
        value_block = heads_of(lax.dynamic_slice_in_dim(value_piece, offset, block_rows, 0))
        allowed = None
        if tag_bundle is not None:
            query_seg, query_pos, seg_all, pos_all = tag_bundle
            key_seg = lax.dynamic_slice_in_dim(seg_all, offset, block_rows, 0)
            key_pos = lax.dynamic_slice_in_dim(pos_all, offset, block_rows, 0)
            allowed = allow_table(query_seg, query_pos, key_seg, key_pos)
        return fold_keys(current, queries, key_block, value_block, allowed)

    return lax.fori_loop(0, count_rows // block_rows, one_block, folded)


def finish(folded):
    run_max, run_sum, weighted = folded
    attended = weighted / jnp.transpose(run_sum)[:, :, None]
    return (attended, run_max + jnp.log(run_sum))


def row_deltas(out_grad, attended):
    return jnp.einsum("qhd,qhd->hq", out_grad, attended, preferred_element_type=jnp.float32)


def attend_back(queries, key_all, value_all, out_grad, row_delta, log_total, tag_bundle):
    total_rows = key_all.shape[0]
    row_count = queries.shape[0]
    block_rows = math.gcd(total_rows, 512)

    def one_block(query_acc, number):
        offset = number * block_rows
        key_block = heads_of(lax.dynamic_slice_in_dim(key_all, offset, block_rows, 0))
        value_block = heads_of(lax.dynamic_slice_in_dim(value_all, offset, block_rows, 0))
        scores = jnp.einsum("qhd,khd->hqk", queries, key_block, preferred_element_type=jnp.float32)
        if tag_bundle is not None:
            query_seg, query_pos, seg_all, pos_all = tag_bundle
            key_seg = lax.dynamic_slice_in_dim(seg_all, offset, block_rows, 0)
            key_pos = lax.dynamic_slice_in_dim(pos_all, offset, block_rows, 0)
            scores = jnp.where(
                allow_table(query_seg, query_pos, key_seg, key_pos)[None], scores, NEGATIVE
            )
        weighting = jnp.exp(scores - log_total[:, :, None])
        weight_grad = jnp.einsum(
            "qhd,khd->hqk", out_grad, value_block, preferred_element_type=jnp.float32
        )
        score_grad = (weighting * (weight_grad - row_delta[:, :, None])).astype(jnp.bfloat16)
        query_acc = query_acc + jnp.einsum(
            "hqk,khd->qhd", score_grad, key_block, preferred_element_type=jnp.float32
        )
        key_term = jnp.einsum(
            "hqk,qhd->khd", score_grad, queries, preferred_element_type=jnp.float32
        )
        value_term = jnp.einsum(
            "hqk,qhd->khd",
            weighting.astype(jnp.bfloat16),
            out_grad,
            preferred_element_type=jnp.float32,
        )
        return (query_acc, (key_term.reshape(block_rows, D), value_term.reshape(block_rows, D)))

    start_acc = jnp.zeros((row_count, HEADS, HEAD_DIM), jnp.float32)
    query_acc, terms = lax.scan(one_block, start_acc, jnp.arange(total_rows // block_rows))
    key_terms, value_terms = terms
    return (
        query_acc.reshape(row_count, D),
        key_terms.reshape(total_rows, D),
        value_terms.reshape(total_rows, D),
    )


def pair_places():
    x, y, z, c = coords()
    side = 1 - 2 * lax.rem(z, 2)
    sib, near, diag = device_of(x, y, z, 1 - c), device_of(x, y, z + side, c), device_of(x, y, z + side, 1 - c)
    far = device_of(x, y, z + 2 - 4 * lax.div(z, 2), 1 - c)
    block = 2 * c + lax.rem(z, 2)
    near_block = 2 * c + 1 - lax.rem(z, 2)
    sib_block = 2 * (1 - c) + lax.rem(z, 2)
    diag_block = 2 * (1 - c) + 1 - lax.rem(z, 2)
    home = lax.div(z, 2) == c
    return sib, near, diag, far, block, near_block, sib_block, diag_block, home


TILE = 256
LANES = 128
NEG = -1e30


def dot_nt(a, b):
    return lax.dot_general(a, b, (((1,), (1,)), ((), ())), preferred_element_type=F32)


def dot_nn(a, b):
    return lax.dot_general(a, b, (((1,), (0,)), ((), ())), preferred_element_type=F32)


def split_heads(source, target, heads):
    rows = source.shape[0]
    step = min(rows, 256)
    even = lax.broadcasted_iota(jnp.int32, (step, LANES), 1) < LANES // 2

    def one(k, carry):
        here = pl.ds(pl.multiple_of(k * step, step), step)
        for pair in range(heads // 2):
            block = source[here, pl.ds(pair * LANES, LANES)]
            target[2 * pair, here, :] = jnp.where(even, block, jnp.zeros_like(block))
            target[2 * pair + 1, here, :] = jnp.where(even, jnp.zeros_like(block), block)
        return carry

    lax.fori_loop(0, rows // step, one, 0)


def transpose_rows(source, target):
    rows = source.shape[0]
    step = min(rows, 256)

    def one(k, carry):
        here = pl.ds(pl.multiple_of(k * step, step), step)
        target[:, here] = source[here, :].astype(F32).T.astype(target.dtype)
        return carry

    lax.fori_loop(0, rows // step, one, 0)


def tree_mask(key_tile, query_tile, key_seg, query_seg, prompt):
    key_at = key_tile * TILE + lax.broadcasted_iota(jnp.int32, (TILE, TILE), 0)
    query_at = query_tile * TILE + lax.broadcasted_iota(jnp.int32, (TILE, TILE), 1)
    return (key_at <= query_at) & ((key_at < prompt) | (key_seg == query_seg))


HEAD_SCALE = 1.0 / math.sqrt(HEAD_DIM)


class Cores:
    def __init__(self):
        sib, near, diag, _, block, near_block, sib_block, diag_block, _ = pair_places()
        self.others = (near, sib, diag)
        self.blocks = (block, near_block, sib_block, diag_block)
        self.per_block = 2

    def tile_at(self, turn):
        b = lax.rem(self.blocks[0] + 1 + lax.div(turn, self.per_block), 4)
        return b * self.per_block + lax.rem(turn, self.per_block)

    def ends(self, source, target, tile, place):
        width = source.shape[1]
        src = source.at[pl.ds(pl.multiple_of(tile * TILE, TILE), TILE), :]
        row = pl.multiple_of(lax.rem(tile, self.per_block) * TILE, TILE)
        column = pl.multiple_of(place * 4 * width + self.blocks[0] * width, width)
        return src, target.at[pl.ds(row, TILE), pl.ds(column, width)]

    def give(self, source, target, tile, place, load, send, recv):
        src, dst = self.ends(source, target, tile, place)
        owner = lax.div(tile, self.per_block)

        @pl.when(owner == self.blocks[0])
        def _():
            pltpu.make_async_copy(src, dst, load).start()

        for device, b in zip(self.others, self.blocks[1:]):

            @pl.when(owner == b)
            def _():
                pltpu.make_async_remote_copy(
                    src_ref=src, dst_ref=dst, send_sem=send, recv_sem=recv.at[self.blocks[0], lax.rem(tile, self.per_block)],
                    device_id=device, device_id_type=MESH,
                ).start()

    def finish(self, source, target, place, load, send, recv):
        for k in range(self.per_block):
            tile = self.blocks[0] * self.per_block + k
            src, dst = self.ends(source, target, tile, place)
            pltpu.make_async_copy(src, dst, load.at[tile]).wait()
            for device, b in zip(self.others, self.blocks[1:]):
                sent = b * self.per_block + k
                src, dst = self.ends(source, target, sent, place)
                pltpu.make_async_remote_copy(
                    src_ref=src, dst_ref=dst, send_sem=send.at[sent], recv_sem=recv.at[b, k], device_id=device, device_id_type=MESH
                ).wait()


def trade_semaphores(tiles, places):
    dma = pltpu.SemaphoreType.DMA
    lead = () if places == 1 else (places,)
    return [dma(lead + (tiles,)), dma(lead + (tiles,)), dma(lead + (4, tiles // 4))]


def attention_params(masked, collective_id):
    if masked:
        return pltpu.CompilerParams(vmem_limit_bytes=60 << 20, collective_id=collective_id, has_side_effects=True)
    return pltpu.CompilerParams(vmem_limit_bytes=40 << 20)


def forward_kernel(heads, masked, *refs):
    if masked:
        q_ref, k_ref, v_ref, seg_col, seg_row, o_ref, lse_ref, mixed_ref, qm, vt, acc, load, send, recv = refs
    else:
        q_ref, k_ref, v_ref, o_ref, lse_ref, qm, vt, acc = refs
    n_query, n_key = q_ref.shape[0] // TILE, k_ref.shape[0] // TILE
    prompt_tiles = n_key // 2
    if masked:
        cores = Cores()
        greet(cores.others)
    split_heads(q_ref, qm, heads)
    transpose_rows(v_ref, vt)
    H = range(heads)

    def query_tile(turn, carry):
        i = cores.tile_at(turn) if masked else turn
        rows = pl.ds(pl.multiple_of(i * TILE, TILE), TILE)
        queries = [qm[h, rows, :] for h in H]
        acc[...] = jnp.zeros_like(acc)

        def tile(j, mask, state, span=1):
            keys = pl.ds(pl.multiple_of(j * TILE, TILE), span * TILE)
            old_m, old_l = state
            scores = [dot_nt(k_ref[keys, pl.ds(h // 2 * LANES, LANES)], queries[h]) for h in H]
            if mask is not None:
                scores = [jnp.where(mask, s, NEG) for s in scores]
            new_m = [jnp.maximum(old_m[h], jnp.max(scores[h], axis=0, keepdims=True)) for h in H]
            weights = [jnp.exp(scores[h] - new_m[h]) for h in H]
            if mask is not None:
                weights = [jnp.where(mask, w, 0.0) for w in weights]
            factor = [jnp.exp(old_m[h] - new_m[h]) for h in H]
            new_l = [old_l[h] * factor[h] + jnp.sum(weights[h], axis=0, keepdims=True) for h in H]
            low = [w.astype(BF) for w in weights]
            for h in H:
                part = pl.ds(h * 64, 64)
                acc[part, :] = acc[part, :] * factor[h] + dot_nn(vt[part, keys], low[h])
            return (new_m, new_l)

        state = ([jnp.full((1, TILE), NEG, F32)] * heads, [jnp.zeros((1, TILE), F32)] * heads)
        if masked:
            later = i >= prompt_tiles
            state = lax.fori_loop(0, jnp.where(later, 0, i), lambda j, c: tile(j, None, c), state)
            state = lax.fori_loop(0, jnp.where(later, 1, 0), lambda j, c: tile(0, None, c, prompt_tiles), state)

            def near(j, c):
                keys = pl.ds(pl.multiple_of(j * TILE, TILE), TILE)
                return tile(j, tree_mask(j, i, seg_col[keys, :], seg_row[:, rows], prompt_tiles * TILE), c)

            first = jnp.where(i > prompt_tiles, i - 1, i)
            state = lax.fori_loop(first, i + 1, near, state)
        else:
            state = tile(0, None, state, n_key)
        m, l = state
        for h in H:
            part = pl.ds(h * 64, 64)
            acc[part, :] = acc[part, :] / l[h]
            lse_ref[pl.ds(h, 1), rows] = m[h] + jnp.log(l[h])
        o_ref[rows, :] = acc[...].T.astype(BF)
        if masked:
            cores.give(o_ref, mixed_ref, i, 0, load.at[i], send.at[i], recv)
        return carry

    lax.fori_loop(0, n_query, query_tile, 0)
    if masked:
        cores.finish(o_ref, mixed_ref, 0, load, send, recv)


def attention_forward(q, k, v, seg=None):
    heads, width = 4, 256
    n, m, groups = q.shape[0], k.shape[0], q.shape[1] // 256
    masked = seg is not None
    column = lambda rows: pl.BlockSpec((rows, width), lambda p: (0, p))
    whole = lambda shape: pl.BlockSpec(shape, lambda p: (0, 0))
    extra = [seg.reshape(n, 1), seg.reshape(1, n)] if masked else []
    return pl.pallas_call(
        functools.partial(forward_kernel, heads, masked),
        grid=(groups,),
        out_shape=(jax.ShapeDtypeStruct((n, q.shape[1]), BF), jax.ShapeDtypeStruct((groups, 8, n), F32))
        + ((jax.ShapeDtypeStruct((n // 4, 4 * width), BF),) if masked else ()),
        in_specs=[column(n), column(m), column(m)] + [whole(e.shape) for e in extra],
        out_specs=(column(n), pl.BlockSpec((None, 8, n), lambda p: (p, 0, 0)))
        + ((pl.BlockSpec(memory_space=pltpu.HBM),) if masked else ()),
        scratch_shapes=[
            pltpu.VMEM((heads, n, LANES), BF),
            pltpu.VMEM((width, m), BF),
            pltpu.VMEM((width, TILE), F32),
        ]
        + (trade_semaphores(n // TILE, 1) if masked else []),
        compiler_params=attention_params(masked, 3),
        cost_estimate=pl.CostEstimate(flops=24 * n * m * q.shape[1], bytes_accessed=4 * (n + m) * q.shape[1], transcendentals=n * m * heads * groups),
        name="attention_forward",
    )(q, k, v, *extra)


CH = 512
WD = 1024
SETS = ((0, 512), (512, 512))
RING = 4
KEEP = 6
CROSS_AT = 3
DENSE_AT = 7
FIRST_AT = 8
KEYS_AT = 8
GATHER_AT = 12
SOURCE_AT = 13


def backward_parts(heads, cores, q_ref, k_ref, v_ref, o_ref, lse_ref, seg_col, seg_row, projected_ref,
                   dq_ref, dk_ref, dv_ref, g_ref, qm, gm, kt, dqt, dk_acc, dv_acc, delta, load, send, recv):
    n_query, n_key = q_ref.shape[0] // TILE, k_ref.shape[0] // TILE
    prompt_tiles = n_key // 2
    H = range(heads)
    lane = [pl.ds(h // 2 * LANES, LANES) for h in H]

    def first():
        split_heads(q_ref, qm, heads)
        split_heads(g_ref, gm, heads)
        transpose_rows(k_ref, kt)
        dqt[...] = jnp.zeros_like(dqt)

        def deltas(i, carry):
            rows = pl.ds(pl.multiple_of(i * TILE, TILE), TILE)
            product = (g_ref[rows, :].astype(F32) * o_ref[rows, :].astype(F32)).T
            for h in H:
                delta[pl.ds(h, 1), rows] = jnp.sum(product[h * 64 : h * 64 + 64, :], axis=0, keepdims=True)
            return carry

        lax.fori_loop(0, n_query, deltas, 0)

    def send_rows(source, place, j):
        cores.give(source, projected_ref, j, place, load.at[place, j], send.at[place, j], recv.at[place])

    def finish_queries(i):
        rows = pl.ds(pl.multiple_of(i * TILE, TILE), TILE)
        dq_ref[rows, :] = (dqt[:, rows].T.astype(BF).astype(F32) * HEAD_SCALE).astype(BF)
        send_rows(dq_ref, 0, i)

    def key_tile(turn):
        j = lax.rem(turn + prompt_tiles, n_key)
        keys = pl.ds(pl.multiple_of(j * TILE, TILE), TILE)
        dk_acc[...] = jnp.zeros_like(dk_acc)
        dv_acc[...] = jnp.zeros_like(dv_acc)

        def tile(i, mask):
            rows = pl.ds(pl.multiple_of(i * TILE, TILE), TILE)
            scores = [dot_nt(k_ref[keys, lane[h]], qm[h, rows, :]) for h in H]
            change = [dot_nt(v_ref[keys, lane[h]], gm[h, rows, :]) for h in H]
            weights = [jnp.exp(scores[h] - lse_ref[pl.ds(h, 1), rows]) for h in H]
            if mask is not None:
                weights = [jnp.where(mask, w, 0.0) for w in weights]
            back = [(weights[h] * (change[h] - delta[pl.ds(h, 1), rows])).astype(BF) for h in H]
            low = [w.astype(BF) for w in weights]
            for pair in range(heads // 2):
                a, b = 2 * pair, 2 * pair + 1
                dv_acc[:, lane[a]] += dot_nn(low[a], gm[a, rows, :]) + dot_nn(low[b], gm[b, rows, :])
                dk_acc[:, lane[a]] += dot_nn(back[a], qm[a, rows, :]) + dot_nn(back[b], qm[b, rows, :])
            for h in H:
                part = pl.ds(h * 64, 64)
                dqt[part, rows] += dot_nn(kt[part, keys], back[h])

        def near(i, carry):
            rows = pl.ds(pl.multiple_of(i * TILE, TILE), TILE)
            tile(i, tree_mask(j, i, seg_col[keys, :], seg_row[:, rows], prompt_tiles * TILE))
            return carry

        prompt = j < prompt_tiles
        last = jnp.where(prompt, j, jnp.minimum(j + 1, n_query - 1))
        lax.fori_loop(j, last + 1, near, 0)
        lax.fori_loop(jnp.where(prompt, j + 1, n_query), n_query, lambda i, c: (tile(i, None), c)[1], 0)
        dk_ref[keys, :] = dk_acc[...].astype(BF)
        dv_ref[keys, :] = dv_acc[...].astype(BF)
        send_rows(dk_ref, 1, j)
        send_rows(dv_ref, 2, j)

        @pl.when(prompt)
        def _():
            finish_queries(j)

    def last_queries():
        lax.fori_loop(prompt_tiles, n_query, lambda i, c: (finish_queries(i), c)[1], 0)

    def end():
        for place, source in enumerate((dq_ref, dk_ref, dv_ref)):
            cores.finish(source, projected_ref, place, load.at[place], send.at[place], recv.at[place])

    return first, key_tile, last_queries, end, n_key


def finish_kernel(plan, n_sources, *refs):
    n_chunks = len(plan)
    q_ref, k_ref, v_ref, o_ref, lse_ref, seg_col, seg_row, cross_lse, gain_ref, cross_gain, small = refs[:11]
    sources = list(refs[11 : 11 + n_sources])
    at = 11 + n_sources
    tok_hbm, block_hbm, first_hbm, second_hbm, cross_q, cross_k, cross_v, cross_o, cross_g = refs[at : at + 9]
    weights_ref, memory_ref, query_w, output_w = refs[at + 9 : at + 13]
    out, small_out, tokens_home, block_home, source_home, q_grad, branch_self, key_terms, value_terms, projected_ref = refs[at + 13 : at + 23]
    (
        dq_ref, dk_ref, dv_ref, g_ref, qm, gm, kt, dqt, dk_acc, dv_acc, delta, trade_load, trade_send, trade_recv,
        tokens_out, part_ref, src_b, src_r1, src_r2, home_sem, away_send, away_recv, src_send, src_recv, grad_send, grad_recv,
        acc, snd, r0, r1, r2, r3, r4, sv, sr, xbuf, ybuf, wbuf, pbuf,
        x_sem, y_sem, w_sem, p_sem, take_sem, s0s, s0r, hs, hr, gs, gr, put_sem, svs, svr,
        mix_grad, first_ref, fbuf, tbuf, sums_ref, in_sem, out_sem, f_sem,
    ) = refs[at + 23 :]
    sources += [q_grad, branch_self, key_terms, value_terms, projected_ref]
    x, y, z, c = coords()
    cores = Cores()
    sib = device_of(x, y, z, 1 - c)
    dx, dy = device_of(1 - x, y, z, c), device_of(x, 1 - y, z, c)
    dz2, dz1 = device_of(x, y, z + 2 - 4 * lax.div(z, 2), c), cores.others[0]
    far = device_of(x, y, z + 2 - 4 * lax.div(z, 2), 1 - c)
    home = lax.div(z, 2) == c
    greet((sib, dx, dy, dz2, dz1, cores.others[2], far))
    z2, z1 = lax.div(z, 2), lax.rem(z, 2)

    first, key_tile, last_queries, end_trade, n_key = backward_parts(
        4, cores, q_ref, k_ref, v_ref, o_ref, lse_ref, seg_col, seg_row, projected_ref,
        dq_ref, dk_ref, dv_ref, g_ref, qm, gm, kt, dqt, dk_acc, dv_acc, delta, trade_load, trade_send, trade_recv,
    )

    def remote(src, dst, send, recv, device):
        return pltpu.make_async_remote_copy(src_ref=src, dst_ref=dst, send_sem=send, recv_sem=recv, device_id=device, device_id_type=MESH)

    def send_home(i, src, dst, wait):
        @pl.when(home)
        def _():
            copy = pltpu.make_async_copy(src, dst, home_sem.at[i])
            copy.wait() if wait else copy.start()

        @pl.when(jnp.logical_not(home))
        def _():
            copy = remote(src, dst, away_send.at[i], away_recv.at[i], far)
            copy.wait() if wait else copy.start()

    own_block = cores.blocks[0]
    part_rows, head_cols = mix_grad.shape[0], q_ref.shape[1]
    grad_rows = g_ref.at[pl.ds(pl.multiple_of(own_block * part_rows, part_rows), part_rows), :]

    def grad_copy(k):
        cols = pl.ds(pl.multiple_of(cores.blocks[1 + k] * head_cols, head_cols), head_cols)
        return remote(mix_grad.at[:, cols], grad_rows, grad_send.at[k], grad_recv.at[k], cores.others[k])

    half_rows = part_ref.shape[0] // 2
    quarter = half_rows // 2
    src_a = part_ref.at[pl.ds(0, half_rows), :]

    def source_sib():
        return remote(part_ref.at[pl.ds(half_rows, half_rows), :], src_r1, src_send.at[0], src_recv.at[0], sib)

    def source_near():
        return remote(src_a.at[pl.ds(quarter, quarter), :], src_r2, src_send.at[1], src_recv.at[1], dz1)

    def add_blocks(target, one_ref, other_ref, rows):
        def one(k, carry):
            here = pl.ds(pl.multiple_of(k * 32, 32), 32)
            target[here, :] = (one_ref[here, :].astype(F32) + other_ref[here, :].astype(F32)).astype(BF)
            return carry

        lax.fori_loop(0, rows // 32, one, 0)

    def load(pairs):
        copies = [pltpu.make_async_copy(src, dst, f_sem.at[k]) for k, (src, dst) in enumerate(pairs)]
        for copy in copies:
            copy.start()
        for copy in copies:
            copy.wait()

    block_stage = part_ref.at[pl.ds(0, part_rows), :]

    def send_block():
        load([(block_hbm, block_stage)])
        send_home(0, block_stage, block_home, False)

    n_cross, m_cross = cross_q.shape[0], cross_k.shape[0]
    low, high = pl.ds(0, m_cross), pl.ds(m_cross, m_cross)
    cdq, cdk, cdv = dq_ref.at[pl.ds(0, n_cross), :], dk_ref.at[low, :], dv_ref.at[low, :]
    cq, cg, co = (dq_ref.at[pl.ds(n_cross * k, n_cross), :] for k in (1, 2, 3))
    ck, cv = dk_ref.at[high, :], dv_ref.at[high, :]

    def head_columns(group):
        return pl.ds(pl.multiple_of(group * head_cols, head_cols), head_cols)

    def cross_ins(group):
        pairs = ((cross_q, cq), (cross_g, cg), (cross_o, co), (cross_k, ck), (cross_v, cv))
        return [pltpu.make_async_copy(src.at[:, head_columns(group)], dst, in_sem.at[k]) for k, (src, dst) in enumerate(pairs)]

    def cross_outs(group):
        pairs = ((cdq, q_grad), (cdk, key_terms), (cdv, value_terms))
        return [pltpu.make_async_copy(src, dst.at[:, head_columns(group)], out_sem.at[k]) for k, (src, dst) in enumerate(pairs)]

    def cross_group(group):
        heads = head_cols // HEAD_DIM
        H = range(heads)
        lane = [pl.ds(h // 2 * LANES, LANES) for h in H]
        rows = pl.ds(0, n_cross)
        for copy in cross_ins(group):
            copy.wait()

        @pl.when(group > 0)
        def _():
            for copy in cross_outs(group - 1):
                copy.wait()

        split_heads(cq, qm, heads)
        split_heads(cg, gm, heads)
        transpose_rows(ck, kt)
        dqt[:, rows] = jnp.zeros((head_cols, n_cross), F32)
        product = (cg[...].astype(F32) * co[...].astype(F32)).T
        for h in H:
            delta[pl.ds(h, 1), rows] = jnp.sum(product[h * 64 : h * 64 + 64, :], axis=0, keepdims=True)

        def one(j, carry):
            keys = pl.ds(pl.multiple_of(j * TILE, TILE), TILE)
            scores = [dot_nt(ck[keys, lane[h]], qm[h, rows, :]) for h in H]
            change = [dot_nt(cv[keys, lane[h]], gm[h, rows, :]) for h in H]
            weights = [jnp.exp(scores[h] - cross_lse[group, pl.ds(h, 1), :]) for h in H]
            back = [(weights[h] * (change[h] - delta[pl.ds(h, 1), rows])).astype(BF) for h in H]
            kept = [w.astype(BF) for w in weights]
            for pair in range(heads // 2):
                a, b = 2 * pair, 2 * pair + 1
                cdv[keys, lane[a]] = (dot_nn(kept[a], gm[a, rows, :]) + dot_nn(kept[b], gm[b, rows, :])).astype(BF)
                cdk[keys, lane[a]] = (dot_nn(back[a], qm[a, rows, :]) + dot_nn(back[b], qm[b, rows, :])).astype(BF)
            for h in H:
                part = pl.ds(h * 64, 64)
                dqt[part, rows] += dot_nn(kt[part, keys], back[h])
            return carry

        lax.fori_loop(0, m_cross // TILE, one, 0)
        cdq[...] = (dqt[:, rows].T.astype(BF).astype(F32) * HEAD_SCALE).astype(BF)
        sums_ref[pl.ds(0, 1), head_columns(group)] = jnp.sum(cdq[...].astype(F32), axis=0, keepdims=True)
        sums_ref[pl.ds(1, 1), head_columns(group)] = jnp.sum(cdv[...].astype(F32), axis=0, keepdims=True)
        for copy in cross_outs(group):
            copy.start()

        @pl.when(group < n_groups - 1)
        def _():
            for copy in cross_ins(group + 1):
                copy.start()

    n_groups = cross_q.shape[1] // head_cols

    def norm_back(values, e, gain):
        centred = values - jnp.mean(values, axis=-1, keepdims=True)
        r = lax.rsqrt(jnp.mean(centred * centred, axis=-1, keepdims=True) + EPSILON)
        xhat = centred * r
        t = e * gain
        return r * (t - jnp.mean(t, axis=-1, keepdims=True) - xhat * jnp.mean(t * xhat, axis=-1, keepdims=True)), xhat

    def dense_weights():
        pairs = ((query_w, wbuf.at[:, pl.ds(0, WD)]), (output_w, wbuf.at[:, pl.ds(WD, WD)]))
        return [pltpu.make_async_copy(src, dst, w_sem.at[1 + k]) for k, (src, dst) in enumerate(pairs)]

    def dense():
        for copy in (*cross_outs(n_groups - 1), *dense_weights()):
            copy.wait()
        step = pbuf.shape[0]

        def one(k, sums):
            rows = pl.ds(pl.multiple_of(k * step, step), step)
            load([(q_grad.at[rows, :], pbuf.at[:, pl.ds(0, WD)]), (first_hbm.at[rows, :], fbuf.at[0]), (second_hbm.at[rows, :], fbuf.at[1])])
            e = dot_nt(pbuf[:, :WD], wbuf[:, :WD])
            change, xhat = norm_back(fbuf[0], e, cross_gain[...])
            total = fbuf[1] + change
            first_ref[rows, :] = total
            pbuf[:, WD : 2 * WD] = total.astype(BF)
            mix_grad[rows, :] = dot_nt(pbuf[:, WD : 2 * WD], wbuf[:, WD : 2 * WD]).astype(BF)
            load([(pbuf.at[:, pl.ds(WD, WD)], branch_self.at[rows, :])])
            return tuple(s + jnp.sum(v, axis=0, keepdims=True) for s, v in zip(sums, (total, e * xhat, e)))

        sums = lax.fori_loop(0, n_cross // step, one, (jnp.zeros((1, WD), F32),) * 3)
        for k, total in enumerate(sums):
            sums_ref[pl.ds(2 + k, 1), :] = total
        for k in range(3):
            grad_copy(k).start()
        w_copy().start()

    def begin_keys():
        g_ref[pl.ds(pl.multiple_of(own_block * part_rows, part_rows), part_rows), :] = mix_grad[
            :, pl.ds(pl.multiple_of(own_block * head_cols, head_cols), head_cols)
        ]
        for k in range(3):
            grad_copy(k).wait()
        first()

    def memory_copy():
        return pltpu.make_async_copy(memory_ref, wbuf.at[:, pl.ds(0, 2 * WD)], w_sem.at[0])

    def source_0(begin):
        step = pbuf.shape[0]
        blocks = part_ref.shape[0] // step // 2

        def one(k, carry):
            rows = pl.ds(pl.multiple_of(k * step, step), step)
            copies = [
                pltpu.make_async_copy(terms.at[rows, :], pbuf.at[:, pl.ds(p * WD, WD)], take_sem.at[p])
                for p, terms in enumerate((key_terms, value_terms))
            ]
            for copy in copies:
                copy.start()
            for copy in copies:
                copy.wait()
            part_ref[rows, :] = dot_nt(pbuf[:, : 2 * WD], wbuf[:, : 2 * WD]).astype(BF)
            return carry

        lax.fori_loop(begin * blocks, (begin + 1) * blocks, one, 0)

    def source_1():
        source_sib().wait()
        add_blocks(src_a, part_ref, src_r1, half_rows)
        source_near().start()

    def source_2():
        source_near().wait()
        add_blocks(src_b, src_a, src_r2, quarter)
        send_home(1, src_b, source_home, False)

    def fetch(k):
        xi, kind, i, yi, column = plan[k]
        depth = sources[xi].shape[0]
        half = sources[xi].shape[1] // 2
        at = i * CH if kind == "rows" else 0
        for p, h in enumerate((c, 1 - c)):
            pltpu.make_async_copy(
                sources[xi].at[:, pl.ds(pl.multiple_of(h * half + at, CH), CH)],
                xbuf.at[k % 2, pl.ds(0, depth), pl.ds(p * CH, CH)],
                x_sem.at[k % 2, p],
            ).start()
        pltpu.make_async_copy(sources[yi].at[:, pl.ds(column * WD, WD)], ybuf.at[k % 2, pl.ds(0, depth), :], y_sem.at[k % 2]).start()

    def swap_copy(j):
        return pltpu.make_async_remote_copy(
            src_ref=snd.at[lax.rem(j, 2)], dst_ref=r0.at[lax.rem(j, RING)], send_sem=s0s.at[j], recv_sem=s0r.at[j], device_id=sib, device_id_type=MESH
        )

    def make(j, depth):
        slot, keep = lax.rem(j, 2), lax.rem(j, KEEP)
        deep = pl.ds(0, depth)
        for p in range(2):
            side = xbuf.at[slot, deep, pl.ds(p * CH, CH)]
            pltpu.make_async_copy(side, side, x_sem.at[slot, p]).wait()
        pltpu.make_async_copy(ybuf.at[slot, deep, :], ybuf.at[slot, deep, :], y_sem.at[slot]).wait()
        step = 128

        def one(k, carry):
            rows = pl.ds(pl.multiple_of(k * step, step), step)
            more = pl.ds(pl.multiple_of(CH + k * step, step), step)
            across = (((0,), (0,)), ((), ()))
            own = lax.dot_general(xbuf[slot, deep, rows], ybuf[slot, deep, :], across, preferred_element_type=F32)
            acc[keep, rows, :] = own.astype(BF)
            other = lax.dot_general(xbuf[slot, deep, more], ybuf[slot, deep, :], across, preferred_element_type=F32)
            snd[slot, rows, :] = other.astype(BF)
            return carry

        lax.fori_loop(0, CH // step, one, 0)

    rbufs = (r1, r2, r3, r4)

    def axis(jj, s, q):
        even = lax.rem(jj, 2) == 0
        along = ((("one", "two", "near", "far"), ("two", "one", "near", "far"))[s])[q]
        if along == "near":
            return dz1, z1
        if along == "far":
            return dz2, z2
        use_x = even if along == "one" else jnp.logical_not(even)
        return (jnp.where(use_x, dx[0], dy[0]), z, c), jnp.where(use_x, x, y)

    def start_of(jj, s, step):
        row = 0
        for q in range(step):
            row = row + axis(jj, s, q)[1] * (CH >> (q + 1))
        return row

    def halve_copy(jj, s, q):
        size = CH >> (q + 1)
        device, bit = axis(jj, s, q)
        row = start_of(jj, s, q) + (1 - bit) * size
        return pltpu.make_async_remote_copy(
            src_ref=acc.at[lax.rem(jj, KEEP), pl.ds(pl.multiple_of(row, 32), size), pl.ds(*SETS[s])],
            dst_ref=rbufs[q].at[lax.rem(jj, RING), :, pl.ds(*SETS[s])],
            send_sem=hs.at[jj, s, q],
            recv_sem=hr.at[jj, s, q],
            device_id=device,
            device_id_type=MESH,
        )

    def give_copy(jj, s, q):
        size = CH >> (q + 1)
        block = out.at[jj, pl.ds(pl.multiple_of(start_of(jj, s, q + 1), 32), size), pl.ds(*SETS[s])]
        return pltpu.make_async_remote_copy(
            src_ref=block, dst_ref=block, send_sem=gs.at[jj, s, q], recv_sem=gr.at[jj, s, q], device_id=axis(jj, s, q)[0], device_id_type=MESH
        )

    def put_copy(jj, s):
        rows = pl.ds(pl.multiple_of(start_of(jj, s, 4), 32), CH >> 4)
        return pltpu.make_async_copy(
            acc.at[lax.rem(jj, KEEP), rows, pl.ds(*SETS[s])], out.at[jj, rows, pl.ds(*SETS[s])], put_sem.at[jj, s]
        )

    def add_rows(jj, s, q):
        size = CH >> (q + 1)
        row = pl.multiple_of(start_of(jj, s, q + 1), 32)
        span = min(size, 64)
        keep, slot, cols = lax.rem(jj, KEEP), lax.rem(jj, RING), pl.ds(*SETS[s])

        def one(k, carry):
            here = pl.ds(pl.multiple_of(row + k * span, 32), span)
            there = pl.ds(pl.multiple_of(k * span, 32), span)
            acc[keep, here, cols] = (acc[keep, here, cols].astype(F32) + rbufs[q][slot, there, cols].astype(F32)).astype(BF)
            return carry

        lax.fori_loop(0, size // span, one, 0)

    def phase0(jj):
        swap_copy(jj).wait()
        keep, slot = lax.rem(jj, KEEP), lax.rem(jj, RING)

        def one(k, carry):
            here = pl.ds(pl.multiple_of(k * 32, 32), 32)
            acc[keep, here, :] = (acc[keep, here, :].astype(F32) + r0[slot, here, :].astype(F32)).astype(BF)
            return carry

        lax.fori_loop(0, CH // 32, one, 0)
        for s in range(len(SETS)):
            halve_copy(jj, s, 0).start()

    def phase_halve(jj, q):
        for s in range(len(SETS)):
            halve_copy(jj, s, q).wait()
            add_rows(jj, s, q)
            if q < 3:
                halve_copy(jj, s, q + 1).start()
            else:
                put_copy(jj, s).start()
        if q == 3:
            for s in range(len(SETS)):
                put_copy(jj, s).wait()
                give_copy(jj, s, 3).start()

    def phase_give(jj, q):
        for s in range(len(SETS)):
            give_copy(jj, s, q).wait()
            if q > 0:
                give_copy(jj, s, q - 1).start()

    partners = (sib, dx, dy, dz2, dz1)

    def small_copy(p):
        return pltpu.make_async_remote_copy(
            src_ref=sv.at[p], dst_ref=sr.at[p], send_sem=svs.at[p], recv_sem=svr.at[p], device_id=partners[p], device_id_type=MESH
        )

    def small_phase(p):
        if p > 0:
            small_copy(p - 1).wait()
            sv[p] = sv[p - 1] + sr[p - 1]
        if p < 5:
            small_copy(p).start()
        else:
            small_out[...] = sv[5]

    def w_copy():
        return pltpu.make_async_copy(weights_ref, wbuf, w_sem.at[0])

    def gather():
        end_trade()
        w_copy().wait()
        d = WD
        step = 128
        zero = jnp.zeros((1, d), F32)

        def one(k, sums):
            rows = pl.ds(pl.multiple_of(k * step, step), step)
            load([(projected_ref.at[rows, :], pbuf), (tok_hbm.at[rows, :], tbuf)])
            projected = pbuf[...]
            e = dot_nt(projected, wbuf[...])
            change, xhat = norm_back(tbuf[...].astype(F32), e, gain_ref[...])
            tokens_out[rows, :] = (first_ref[rows, :] + change).astype(BF)
            wide = projected.astype(F32)
            new = (e * xhat, e, wide[:, :d], wide[:, 2 * d :])
            return tuple(s + jnp.sum(v, axis=0, keepdims=True) for s, v in zip(sums, new))

        sums = lax.fori_loop(0, n_cross // step, one, (zero,) * 4)
        sv[0] = small[...]
        for row, total in enumerate((*sums, *(sums_ref[pl.ds(k, 1), :] for k in (2, 3, 4, 0, 1)))):
            sv[0, pl.ds(row, 1), :] = total
        send_home(2, tokens_out, tokens_home, False)
        memory_copy().start()

    late = [k for k in range(n_chunks) if plan[k][3] == len(sources) - 1]
    depth_of = [sources[entry[0]].shape[0] for entry in plan]
    fetch(0)
    for copy in (*cross_ins(0), *dense_weights()):
        copy.start()

    def step(t, carry):
        for k in range(1, n_chunks):
            if k not in late:
                pl.when(t + 1 == k)(functools.partial(fetch, k))
        for depth in sorted(set(depth_of)):
            these = [t == k for k in range(n_chunks) if depth_of[k] == depth]
            pl.when(functools.reduce(jnp.logical_or, these))(functools.partial(make, t, depth))

        @pl.when(t < n_chunks)
        def _():
            swap_copy(t).start()

        def guarded(lag, what):
            @pl.when((t >= lag) & (t < n_chunks + lag))
            def _():
                what(t - lag)

        guarded(1, phase0)
        for q in range(4):
            guarded(q + 2, functools.partial(phase_halve, q=q))
        for q in range(3, -1, -1):
            guarded(9 - q, functools.partial(phase_give, q=q))
        pl.when(t == 0)(send_block)
        pl.when((t >= CROSS_AT) & (t < CROSS_AT + n_groups))(functools.partial(cross_group, t - CROSS_AT))
        pl.when(t == DENSE_AT)(dense)
        pl.when(t == FIRST_AT)(begin_keys)
        half = n_key // 2
        begin = jnp.where(t == KEYS_AT, 0, t - KEYS_AT + half - 1)
        end = jnp.where(t == KEYS_AT, half, jnp.where((t > KEYS_AT) & (t < KEYS_AT + half), begin + 1, begin))
        end = jnp.where(t == KEYS_AT + half - 1, n_key, end)
        lax.fori_loop(begin, end, lambda turn, inner: (key_tile(turn), inner)[1], 0)
        pl.when(t == KEYS_AT + half - 1)(last_queries)

        pl.when(t == GATHER_AT)(gather)
        @pl.when(t == SOURCE_AT)
        def _():
            send_home(0, block_stage, block_home, True)
            memory_copy().wait()

        @pl.when((t == SOURCE_AT) | (t == SOURCE_AT + 1))
        def _():
            source_0(t - SOURCE_AT)

        pl.when(t == SOURCE_AT + 1)(lambda: source_sib().start())
        pl.when(t == SOURCE_AT + 2)(source_1)
        pl.when(t == SOURCE_AT + 3)(source_2)
        for p in range(6):
            pl.when(t == GATHER_AT + 1 + p)(functools.partial(small_phase, p))
        for k in late:
            pl.when(t + 1 == k)(functools.partial(fetch, k))
        return carry

    lax.fori_loop(0, n_chunks + 9, step, 0)
    send_home(1, src_b, source_home, True)
    send_home(2, tokens_out, tokens_home, True)


def finish_backward(plan, attention, cross, gains, small, sources, local, weights):
    n_chunks = len(plan)
    q, k, v, mix, lse, seg = attention
    n, width = q.shape
    rows, d = local[0].shape
    source_rows = cross[1].shape[0]
    hbm = pl.BlockSpec(memory_space=pltpu.HBM)
    vmem = pl.BlockSpec(memory_space=pltpu.VMEM)
    dma = pltpu.SemaphoreType.DMA
    sets = len(SETS)
    near = [q, k, v, mix, lse, seg.reshape(n, 1), seg.reshape(1, n), cross[5], *(g.reshape(1, d) for g in gains), small]
    far = [*sources, *local, *cross[:5], *weights]
    ring = lambda rows: pltpu.VMEM((RING, rows, WD), BF)
    return pl.pallas_call(
        functools.partial(finish_kernel, plan, len(sources)),
        out_shape=(
            jax.ShapeDtypeStruct((n_chunks, CH, WD), BF),
            jax.ShapeDtypeStruct(small.shape, F32),
            jax.ShapeDtypeStruct((rows, d), BF),
            jax.ShapeDtypeStruct((rows, d), BF),
            jax.ShapeDtypeStruct((source_rows // 4, d), BF),
            jax.ShapeDtypeStruct((rows, d), BF),
            jax.ShapeDtypeStruct((rows, d), BF),
            jax.ShapeDtypeStruct((source_rows, d), BF),
            jax.ShapeDtypeStruct((source_rows, d), BF),
            jax.ShapeDtypeStruct((rows, 12 * width), BF),
        ),
        in_specs=[vmem] * len(near) + [hbm] * len(far),
        out_specs=(hbm, vmem) + (hbm,) * 8,
        scratch_shapes=[pltpu.VMEM((n, width), BF)] * 4
        + [
            pltpu.VMEM((4, n, LANES), BF),
            pltpu.VMEM((4, n, LANES), BF),
            pltpu.VMEM((width, n), BF),
            pltpu.VMEM((width, n), F32),
            pltpu.VMEM((TILE, width), F32),
            pltpu.VMEM((TILE, width), F32),
            pltpu.VMEM((8, n), F32),
        ]
        + trade_semaphores(n // TILE, 3)
        + [pltpu.VMEM(shape, BF) for shape in ((rows, d), (source_rows, d), (source_rows // 4, d), (source_rows // 2, d), (source_rows // 4, d))]
        + [dma((3,)), dma((3,)), dma((3,)), dma((2,)), dma((2,)), dma((3,)), dma((3,))]
        + [pltpu.VMEM((KEEP, CH, WD), BF), pltpu.VMEM((2, CH, WD), BF)]
        + [ring(CH >> q) for q in range(5)]
        + [
            pltpu.VMEM((6,) + small.shape, F32),
            pltpu.VMEM((5,) + small.shape, F32),
            pltpu.VMEM((2, source_rows, 2 * CH), BF),
            pltpu.VMEM((2, source_rows, WD), BF),
            pltpu.VMEM(weights[0].shape, BF),
            pltpu.VMEM((128, 12 * width), BF),
            dma((2, 2)),
            dma((2,)),
            dma((3,)),
            dma((1,)),
            dma((2,)),
            dma((n_chunks,)),
            dma((n_chunks,)),
            dma((n_chunks, sets, 4)),
            dma((n_chunks, sets, 4)),
            dma((n_chunks, sets, 4)),
            dma((n_chunks, sets, 4)),
            dma((n_chunks, sets)),
            dma((5,)),
            dma((5,)),
            pltpu.VMEM((rows, d), BF),
            pltpu.VMEM((rows, d), F32),
            pltpu.VMEM((2, 128, d), F32),
            pltpu.VMEM((128, d), BF),
            pltpu.VMEM((8, d), F32),
            dma((5,)),
            dma((3,)),
            dma((3,)),
        ],
        compiler_params=pltpu.CompilerParams(collective_id=1, has_side_effects=True, vmem_limit_bytes=62 << 20),
        cost_estimate=pl.CostEstimate(flops=200 << 30, bytes_accessed=50 << 20, transcendentals=0),
        name="finish_backward",
    )(*near, *far)


def widen_kernel(places, *refs):
    src, outs = refs[0], refs[1 : 1 + len({place for place, _, _ in places})]
    low, wide, load, put = refs[1 + len(outs) :]
    n = len(places)

    def fetch(j):
        return pltpu.make_async_copy(src.at[j], low.at[j], load.at[j])

    def store(j):
        place, row, column = places[j]
        return pltpu.make_async_copy(wide.at[j], outs[place].at[pl.ds(row, CH), pl.ds(column, WD)], put.at[j])

    for j in range(n):
        fetch(j).start()
    for j in range(n):
        fetch(j).wait()

        def one(k, carry):
            rows = pl.ds(pl.multiple_of(k * 64, 64), 64)
            wide[j, rows, :] = low[j, rows, :].astype(F32)
            return carry

        lax.fori_loop(0, CH // 64, one, 0)
        store(j).start()
    for j in range(n):
        store(j).wait()


def widen(summed, pieces):
    places = []
    for place, (kind, count) in enumerate(pieces):
        places += [(place, 0, k * WD) if kind == "cols" else (place, k * CH, 0) for k in range(count)]
    n = len(places)
    hbm = pl.BlockSpec(memory_space=pltpu.HBM)
    return pl.pallas_call(
        functools.partial(widen_kernel, tuple(places)),
        out_shape=[jax.ShapeDtypeStruct((CH, WD * count) if kind == "cols" else (CH * count, WD), F32) for kind, count in pieces],
        in_specs=[hbm],
        out_specs=[hbm] * len(pieces),
        scratch_shapes=[
            pltpu.VMEM((n, CH, WD), BF),
            pltpu.VMEM((n, CH, WD), F32),
            pltpu.SemaphoreType.DMA((n,)),
            pltpu.SemaphoreType.DMA((n,)),
        ],
        compiler_params=pltpu.CompilerParams(vmem_limit_bytes=60 << 20),
        cost_estimate=pl.CostEstimate(flops=0, bytes_accessed=6 * CH * WD * n, transcendentals=0),
        name="widen",
    )(summed)


def feed_kernel(x_ref, grad_ref, second_ref, down_bias, up_bias, up_ref, down_ref, hidden_ref, hidden_grad_ref, bias_grad_ref, block_ref, e_ref, acc):
    j = pl.program_id(0)

    @pl.when(j == 0)
    def _():
        acc[...] = jnp.zeros_like(acc)
        e_ref[...] = jnp.zeros_like(e_ref)

    step = 256
    total = jnp.zeros(bias_grad_ref.shape, F32)
    for k in range(x_ref.shape[0] // step):
        rows = pl.ds(k * step, step)
        before = dot_nn(x_ref[rows, :], up_ref[...]) + up_bias[...]
        change = dot_nt(grad_ref[rows, :], down_ref[...])
        below = 0.5 + 0.5 * lax.erf(before * math.sqrt(0.5))
        slope = below + before * jnp.exp(-0.5 * before * before) * (1.0 / math.sqrt(2.0 * math.pi))
        hidden = (before * below).astype(BF)
        hidden_grad = (change * slope).astype(BF)
        hidden_ref[rows, :] = hidden
        hidden_grad_ref[rows, :] = hidden_grad
        total = total + jnp.sum(hidden_grad.astype(F32), axis=0, keepdims=True)
        acc[rows, :] += dot_nn(hidden, down_ref[...])
        e_ref[rows, :] += dot_nt(hidden_grad, up_ref[...])
    bias_grad_ref[...] = total

    @pl.when(j == pl.num_programs(0) - 1)
    def _():
        block_ref[...] = (second_ref[...] + acc[...] + down_bias[...]).astype(BF)


def feed(x, grad, second, up, up_bias, down, down_bias):
    n, d = x.shape
    width, tile = up.shape[1], 512
    whole = lambda shape: pl.BlockSpec(shape, lambda j: (0, 0))
    column = lambda rows: pl.BlockSpec((rows, tile), lambda j: (0, j))
    return pl.pallas_call(
        feed_kernel,
        grid=(width // tile,),
        out_shape=(
            jax.ShapeDtypeStruct((n, width), BF),
            jax.ShapeDtypeStruct((n, width), BF),
            jax.ShapeDtypeStruct((1, width), F32),
            jax.ShapeDtypeStruct((n, d), BF),
            jax.ShapeDtypeStruct((n, d), F32),
        ),
        in_specs=[whole((n, d))] * 3 + [whole((1, d)), column(1), column(d), pl.BlockSpec((tile, d), lambda j: (j, 0))],
        out_specs=(column(n), column(n), column(1), whole((n, d)), whole((n, d))),
        scratch_shapes=[pltpu.VMEM((n, d), F32)],
        compiler_params=pltpu.CompilerParams(vmem_limit_bytes=48 << 20),
        cost_estimate=pl.CostEstimate(flops=16 * n * d * width, bytes_accessed=4 * d * width, transcendentals=2 * n * width),
        name="feed",
    )(x, grad, second, down_bias.reshape(1, d), up_bias.reshape(1, width), up, down)


TOKEN_PARTS = 4


def spread_kernel(n_mats, *refs):
    tok, seg = refs[:2]
    mats = refs[2 : 2 + n_mats]
    tok_all, seg_all = refs[2 + n_mats : 4 + n_mats]
    fulls = refs[4 + n_mats : 4 + 2 * n_mats]
    stage = refs[4 + 2 * n_mats : 4 + 3 * n_mats]
    tok_stage, seg_stage = refs[4 + 3 * n_mats : 6 + 3 * n_mats]
    (mat_load, mat_put, mat_send, mat_recv, own_load, own_put, far_send, far_recv, sib_send, sib_recv, near_send, near_recv, pass_send, pass_recv) = refs[6 + 3 * n_mats :]
    sib, near, diag, far, block, near_block, sib_block, diag_block, home = pair_places()
    _, _, z, c = coords()
    greet((sib, near, far))
    rows = tok.shape[0]
    part = rows // TOKEN_PARTS
    n_items = TOKEN_PARTS + 1

    def source(k):
        return seg if k == TOKEN_PARTS else tok.at[pl.ds(k * part, part), :]

    def place(k, b):
        if k == TOKEN_PARTS:
            return seg_all.at[b]
        return tok_all.at[pl.ds(pl.multiple_of(b * rows + k * part, part), part), :]

    def remote(src, dst, send, recv, device):
        return pltpu.make_async_remote_copy(src_ref=src, dst_ref=dst, send_sem=send, recv_sem=recv, device_id=device, device_id_type=MESH)

    def far_copy(k):
        return remote(source(k), place(k, z), far_send.at[k], far_recv.at[k], far)

    def staged(k):
        return seg_stage if k == TOKEN_PARTS else tok_stage.at[pl.ds(k * part, part), :]

    def own_copy(k):
        return pltpu.make_async_copy(source(k), staged(k), own_load.at[k])

    def own_out(k):
        return pltpu.make_async_copy(staged(k), place(k, block), own_put.at[k])

    def sib_copy(k):
        return remote(place(k, block), place(k, block), sib_send.at[k], sib_recv.at[k], sib)

    def near_copy(k):
        return remote(place(k, block), place(k, block), near_send.at[k], near_recv.at[k], near)

    def pass_copy(k):
        return remote(place(k, near_block), place(k, near_block), pass_send.at[k], pass_recv.at[k], sib)

    @pl.when(home)
    def _():
        for k in range(n_items):
            own_copy(k).start()

    @pl.when(jnp.logical_not(home))
    def _():
        for k in range(n_items):
            far_copy(k).start()

    def mat_target(i):
        half = mats[i].shape[0]
        return fulls[i].at[pl.ds(pl.multiple_of(c * half, 8), half), :]

    def mat_in(i):
        return pltpu.make_async_copy(mats[i], stage[i], mat_load.at[i])

    def mat_out(i):
        return pltpu.make_async_copy(stage[i], mat_target(i), mat_put.at[i])

    def mat_remote(i):
        return remote(mats[i], mat_target(i), mat_send.at[i], mat_recv.at[i], sib)

    for i in range(n_mats):
        mat_in(i).start()
        mat_remote(i).start()

    for k in range(n_items + 1):
        if k < n_items:

            @pl.when(home)
            def _():
                own_copy(k).wait()
                own_out(k).start()
                own_out(k).wait()

            @pl.when(jnp.logical_not(home))
            def _():
                far_copy(k).wait()

            sib_copy(k).start()
            near_copy(k).start()
        if k > 0:
            near_copy(k - 1).wait()
            pass_copy(k - 1).start()
    for i in range(n_mats):
        mat_in(i).wait()
        mat_out(i).start()
    for k in range(n_items):
        sib_copy(k).wait()
        pass_copy(k).wait()
    for i in range(n_mats):
        mat_out(i).wait()
        mat_remote(i).wait()


def spread(tokens, seg, mats):
    n = len(mats)
    any_spec = pl.BlockSpec(memory_space=pltpu.HBM)
    dma = pltpu.SemaphoreType.DMA
    items = TOKEN_PARTS + 1
    return pl.pallas_call(
        functools.partial(spread_kernel, n),
        out_shape=[
            jax.ShapeDtypeStruct((4 * tokens.shape[0], tokens.shape[1]), tokens.dtype),
            jax.ShapeDtypeStruct((4,) + seg.shape, seg.dtype),
        ]
        + [jax.ShapeDtypeStruct((2 * m.shape[0], m.shape[1]), m.dtype) for m in mats],
        in_specs=[any_spec] * (2 + n),
        out_specs=[any_spec] * (2 + n),
        scratch_shapes=[pltpu.VMEM(a.shape, a.dtype) for a in (*mats, tokens, seg)] + [dma((n,))] * 4 + [dma((items,))] * 10,
        compiler_params=pltpu.CompilerParams(collective_id=2, has_side_effects=True, vmem_limit_bytes=60 << 20),
        cost_estimate=pl.CostEstimate(flops=0, bytes_accessed=64 << 20, transcendentals=0),
        name="spread",
    )(tokens, seg, *mats)


def project_kernel(scale, block_ref, tok, gain, shift, wq, wk, wv, bq, bv, q_ref, k_ref, v_ref):
    del block_ref
    normed = norm_rows(tok[...].astype(F32), gain[...], shift[...]).astype(BF)
    q_ref[...] = ((product(normed, wq[...]) + bq[...]) * scale).astype(BF)
    k_ref[...] = product(normed, wk[...]).astype(BF)
    v_ref[...] = (product(normed, wv[...]) + bv[...]).astype(BF)


def project(block, tokens_all, gain, shift, weights, query_bias, value_bias, scale):
    n, d = tokens_all.shape
    width, step = d // 4, 256
    row = lambda i, b: (i, 0)
    fixed = lambda i, b: (0, 0)
    weight = lambda part: pl.BlockSpec((d, width), lambda i, b: (0, 4 * part + b[0]))
    return pl.pallas_call(
        functools.partial(project_kernel, scale),
        grid_spec=pltpu.PrefetchScalarGridSpec(
            num_scalar_prefetch=1,
            grid=(n // step,),
            in_specs=[pl.BlockSpec((step, d), row), pl.BlockSpec((1, d), fixed), pl.BlockSpec((1, d), fixed)]
            + [weight(part) for part in range(3)]
            + [pl.BlockSpec((1, width), lambda i, b: (0, b[0]))] * 2,
            out_specs=[pl.BlockSpec((step, width), row)] * 3,
        ),
        out_shape=[jax.ShapeDtypeStruct((n, width), BF)] * 3,
        compiler_params=pltpu.CompilerParams(vmem_limit_bytes=60 << 20),
        cost_estimate=pl.CostEstimate(flops=6 * n * d * width, bytes_accessed=4 * n * d, transcendentals=0),
        name="project",
    )(block.reshape(1).astype(jnp.int32), tokens_all, gain.reshape(1, d), shift.reshape(1, d), weights, weights, weights,
      query_bias.reshape(1, d), value_bias.reshape(1, d))


def owner_of(z, c):
    return (z, c) if z // 2 == c else ((z + 2) % 4, 1 - c)


def flat(z, c):
    return 2 * z + c


CORES = [(z, c) for z in range(4) for c in range(2)]
SWAP = [(flat(z, c), flat(*owner_of(z, c))) for z, c in CORES if owner_of(z, c) != (z, c)]
HOME_TO_NEAR = [(flat(z, c), flat(owner_of(z, c)[0] ^ 1, owner_of(z, c)[1])) for z, c in CORES]
SIB = [(0, 1), (1, 0)]


def is_home():
    return lax.div(lax.axis_index("ctx"), 2) == lax.axis_index("shard")


def swap(array):
    return jnp.where(is_home(), array, lax.ppermute(array, ("ctx", "shard"), SWAP))


VECTORS = (0, 1, 3, 4, 6, 7, 8, 10, 12, 14, 15, 16, 18, 20)
MATRICES = (17, 19, 13, 9, 5, 11, 2)


def pair_device(
    tokens, source, segment_ids, positions, cotangent,
    self_gain, self_shift, self_weights, query_bias, value_bias, self_output, output_bias,
    cross_gain, cross_shift, cross_query, query_offset, cross_memory, memory_offset, cross_output, return_bias,
    feed_gain, feed_shift, feed_up, up_bias, feed_down, down_bias,
):
    c, z = lax.axis_index("shard"), lax.axis_index("ctx")
    block = 2 * c + lax.rem(z, 2)
    head_scale = 1.0 / math.sqrt(HEAD_DIM)
    rows = tokens.shape[1]
    vectors = (
        self_gain, self_shift, query_bias, value_bias, output_bias, cross_gain, cross_shift, query_offset, memory_offset,
        return_bias, feed_gain, feed_shift, down_bias, up_bias,
    )
    half = D // 2
    n_packed = sum(v.shape[0] for v in vectors) // half
    packed_rows = n_packed + -n_packed % 16
    packed, at = jnp.zeros((packed_rows * half,), F32), 0
    for v in vectors:
        packed = packed + jnp.pad(v.astype(F32), (at, packed_rows * half - at - v.shape[0]))
        at += v.shape[0]
    packed = packed.astype(BF).reshape(packed_rows, half)
    mats = (self_weights, self_output, cross_memory, cross_query, cross_output, feed_up, feed_down, packed)
    spread_out = spread(tokens[0], segment_ids.reshape(4, rows // 4), mats)
    tokens_all, seg_all = spread_out[:2]
    self_weights, self_output, cross_memory, cross_query, cross_output, feed_up, feed_down, packed = spread_out[2:]
    tokens_all, source_home = lax.optimization_barrier((tokens_all, source[0]))
    own_source = swap(source_home)
    near_source = lax.ppermute(source_home, ("ctx", "shard"), HOME_TO_NEAR)
    chip_source = jnp.concatenate([own_source, near_source], axis=0)
    source_all = lax.optimization_barrier(jnp.concatenate([chip_source, lax.ppermute(chip_source, "shard", SIB)], axis=0))
    packed = packed.astype(F32).reshape(2, -1, half)
    unpacked = [packed[:, i].reshape(D) for i in range(13)]
    (
        self_gain, self_shift, query_bias, value_bias, output_bias, cross_gain, cross_shift, query_offset, memory_offset,
        return_bias, feed_gain, feed_shift, down_bias,
    ) = unpacked
    up_bias = packed[:, 13:n_packed].reshape(-1)
    seg = seg_all.reshape(-1)

    width = D // 4
    q, k, v = project(block, tokens_all, self_gain, self_shift, self_weights, query_bias, value_bias, head_scale)
    mix_heads, lse_self, mixed_self = attention_forward(q, k, v, seg)
    mixed_self, out_grad_home = lax.optimization_barrier((mixed_self, cotangent[0]))
    out_grad_far = lax.ppermute(out_grad_home, ("ctx", "shard"), SWAP)

    tok_low = lax.dynamic_slice_in_dim(tokens_all, block * rows, rows, 0)
    tok_rows = tok_low.astype(F32)
    normed_self = norm_rows(tok_rows, self_gain, self_shift).astype(BF)
    first_sum = tok_rows + product(mixed_self, self_output) + output_bias
    normed_cross = norm_rows(first_sum, cross_gain, cross_shift).astype(BF)
    cross_q = ((product(normed_cross, cross_query) + query_offset) * head_scale).astype(BF)
    memory = product(source_all, cross_memory)
    cross_keys = memory[:, :D].astype(BF)
    cross_values = (memory[:, D:] + memory_offset).astype(BF)
    mixed_cross, lse_cross = attention_forward(cross_q, cross_keys, cross_values)
    mixed_cross, out_grad_far = lax.optimization_barrier((mixed_cross, out_grad_far))
    out_grad = jnp.where(is_home(), out_grad_home, out_grad_far)
    second = first_sum + product(mixed_cross, cross_output) + return_bias
    normed_feed = norm_rows(second, feed_gain, feed_shift).astype(BF)
    hidden, hidden_grad, up_bias_grad, block_output, feed_e = feed(
        normed_feed, out_grad, second, feed_up, up_bias, feed_down, down_bias
    )
    up_bias_grad = up_bias_grad.reshape(-1)
    down_bias_grad = jnp.sum(out_grad, axis=0, dtype=F32)
    _, feed_pull = jax.vjp(norm_rows, second, feed_gain, feed_shift)
    second_part, feed_gain_grad, feed_shift_grad = feed_pull(feed_e)
    second_grad = out_grad.astype(F32) + second_part
    branch_cross = second_grad.astype(BF)
    return_bias_grad = jnp.sum(second_grad, axis=0)
    mixed_cross_grad = right_product(branch_cross, cross_output).astype(BF)
    unknown = jnp.zeros((D,), F32)
    vectors = (unknown,) * 9 + (return_bias_grad, feed_gain_grad, feed_shift_grad, up_bias_grad, down_bias_grad)
    small = jnp.concatenate([v.reshape(-1, D) for v in vectors], axis=0)
    small = jnp.pad(small, ((0, -small.shape[0] % 8), (0, 0)))
    sources = (normed_feed, hidden_grad, hidden, out_grad, mixed_cross, branch_cross, normed_cross, mixed_self, normed_self, source_all)
    made = len(sources)
    chunks = feed_up.shape[1] // D
    plan = (
        tuple((0, "cols", 0, 1, i) for i in range(chunks))
        + tuple((2, "rows", i, 3, 0) for i in range(chunks))
        + ((4, "cols", 0, 5, 0), (6, "cols", 0, made, 0), (7, "cols", 0, made + 1, 0))
        + ((9, "cols", 0, made + 2, 0), (9, "cols", 0, made + 3, 0))
        + tuple((8, "cols", 0, made + 4, i) for i in range(3))
    )
    pieces = (("cols", chunks), ("rows", chunks), ("cols", 1), ("cols", 1), ("cols", 1), ("cols", 2), ("cols", 3))
    summed, small_sum, tokens_grad, block_home, source_grad, *_ = finish_backward(
        plan,
        (q, k, v, mix_heads, lse_self.reshape(8, -1), seg),
        (cross_q, cross_keys, cross_values, mixed_cross, mixed_cross_grad, lse_cross),
        (self_gain, cross_gain),
        small,
        sources,
        (tok_low, block_output, first_sum, second_grad),
        (self_weights, cross_memory, cross_query, self_output),
    )
    results = {}
    for place, matrix in zip(MATRICES, widen(summed, pieces)):
        results[place] = matrix
    at = 0
    for place, v in zip(VECTORS, vectors):
        rows_of, size = v.shape[0] // D, v.shape[0]
        results[place] = lax.dynamic_slice_in_dim(small_sum[at : at + rows_of].reshape(size), c * (size // 2), size // 2, 0)
        at += rows_of
    return (
        block_home[None],
        tokens_grad.astype(F32)[None],
        source_grad.astype(F32)[None],
    ) + tuple(results[place] for place in sorted(results))


def per_device(
    tokens,
    source,
    segment_ids,
    positions,
    cotangent,
    self_gain,
    self_shift,
    self_weights,
    query_bias,
    value_bias,
    self_output,
    output_bias,
    cross_gain,
    cross_shift,
    cross_query,
    query_offset,
    cross_memory,
    memory_offset,
    cross_output,
    return_bias,
    feed_gain,
    feed_shift,
    feed_up,
    up_bias,
    feed_down,
    down_bias,
):
    (
        self_gain,
        self_shift,
        self_weights,
        query_bias,
        value_bias,
        self_output,
        output_bias,
        cross_gain,
        cross_shift,
        cross_query,
        query_offset,
        cross_memory,
        memory_offset,
        cross_output,
        return_bias,
        feed_gain,
        feed_shift,
        feed_up,
        up_bias,
        feed_down,
        down_bias,
    ) = (
        lax.all_gather(self_gain, "shard", axis=0, tiled=True),
        lax.all_gather(self_shift, "shard", axis=0, tiled=True),
        lax.all_gather(self_weights, "shard", axis=0, tiled=True),
        lax.all_gather(query_bias, "shard", axis=0, tiled=True),
        lax.all_gather(value_bias, "shard", axis=0, tiled=True),
        lax.all_gather(self_output, "shard", axis=0, tiled=True),
        lax.all_gather(output_bias, "shard", axis=0, tiled=True),
        lax.all_gather(cross_gain, "shard", axis=0, tiled=True),
        lax.all_gather(cross_shift, "shard", axis=0, tiled=True),
        lax.all_gather(cross_query, "shard", axis=0, tiled=True),
        lax.all_gather(query_offset, "shard", axis=0, tiled=True),
        lax.all_gather(cross_memory, "shard", axis=0, tiled=True),
        lax.all_gather(memory_offset, "shard", axis=0, tiled=True),
        lax.all_gather(cross_output, "shard", axis=0, tiled=True),
        lax.all_gather(return_bias, "shard", axis=0, tiled=True),
        lax.all_gather(feed_gain, "shard", axis=0, tiled=True),
        lax.all_gather(feed_shift, "shard", axis=0, tiled=True),
        lax.all_gather(feed_up, "shard", axis=0, tiled=True),
        lax.all_gather(up_bias, "shard", axis=0, tiled=True),
        lax.all_gather(feed_down, "shard", axis=0, tiled=True),
        lax.all_gather(down_bias, "shard", axis=0, tiled=True),
    )
    head_scale = 1.0 / math.sqrt(HEAD_DIM)
    row_count = tokens.shape[1]
    tok_rows = tokens[0].astype(jnp.float32)
    source_rows = source[0]
    tag_seg, tag_pos = (
        lax.all_gather(segment_ids, "ctx", axis=1, tiled=True),
        lax.all_gather(positions, "ctx", axis=1, tiled=True),
    )
    tag_bundle = (segment_ids[0], positions[0], tag_seg[0], tag_pos[0])
    gain_self = self_gain.astype(jnp.float32)
    shift_self = self_shift.astype(jnp.float32)
    normed_self = norm_rows(tok_rows, gain_self, shift_self).astype(jnp.bfloat16)
    projected = product(normed_self, self_weights)
    queries = ((projected[:, :D] + query_bias.astype(jnp.float32)) * head_scale).astype(
        jnp.bfloat16
    )
    keys_self = projected[:, D : 2 * D].astype(jnp.bfloat16)
    values_self = (projected[:, 2 * D :] + value_bias.astype(jnp.float32)).astype(jnp.bfloat16)
    query_heads = heads_of(queries)
    start_state = (
        jnp.full((HEADS, row_count), NEGATIVE, jnp.float32),
        jnp.zeros((HEADS, row_count), jnp.float32),
        jnp.zeros((row_count, HEADS, HEAD_DIM), jnp.float32),
    )
    folded_self = attend_piece(
        start_state,
        query_heads,
        lax.all_gather(keys_self, "ctx", axis=0, tiled=True),
        lax.all_gather(values_self, "ctx", axis=0, tiled=True),
        tag_bundle,
    )
    attended_self, total_self = finish(folded_self)
    mixed_self = attended_self.reshape(row_count, D).astype(jnp.bfloat16)
    first_sum = tok_rows + product(mixed_self, self_output) + output_bias.astype(jnp.float32)
    gain_cross = cross_gain.astype(jnp.float32)
    shift_cross = cross_shift.astype(jnp.float32)
    normed_cross = norm_rows(first_sum, gain_cross, shift_cross).astype(jnp.bfloat16)
    cross_q = (
        (product(normed_cross, cross_query) + query_offset.astype(jnp.float32)) * head_scale
    ).astype(jnp.bfloat16)
    memory = product(source_rows, cross_memory)
    memory_keys = memory[:, :D].astype(jnp.bfloat16)
    memory_values = (memory[:, D:] + memory_offset.astype(jnp.float32)).astype(jnp.bfloat16)
    cross_keys, cross_values = (
        lax.all_gather(memory_keys, "ctx", axis=0, tiled=True),
        lax.all_gather(memory_values, "ctx", axis=0, tiled=True),
    )
    cross_heads = heads_of(cross_q)
    attended_cross, total_cross = finish(
        attend_piece(start_state, cross_heads, cross_keys, cross_values, None)
    )
    mixed_cross = attended_cross.reshape(row_count, D).astype(jnp.bfloat16)
    second = first_sum + product(mixed_cross, cross_output) + return_bias.astype(jnp.float32)
    gain_feed = feed_gain.astype(jnp.float32)
    shift_feed = feed_shift.astype(jnp.float32)
    normed_feed = norm_rows(second, gain_feed, shift_feed).astype(jnp.bfloat16)
    hidden_pre = product(normed_feed, feed_up) + up_bias.astype(jnp.float32)
    hidden_act, gelu_pull = jax.vjp(exact_gelu, hidden_pre)
    hidden = hidden_act.astype(jnp.bfloat16)
    block_output = (second + product(hidden, feed_down) + down_bias.astype(jnp.float32)).astype(
        jnp.bfloat16
    )
    out_grad = cotangent[0]
    down_grad = left_product(hidden, out_grad)
    down_bias_grad = jnp.sum(out_grad, axis=0, dtype=jnp.float32)
    (hidden_grad,) = gelu_pull(right_product(out_grad, feed_down))
    hidden_grad = hidden_grad.astype(jnp.bfloat16)
    up_grad = left_product(normed_feed, hidden_grad)
    up_bias_grad = jnp.sum(hidden_grad, axis=0, dtype=jnp.float32)
    norm_value, feed_pull = jax.vjp(norm_rows, second, gain_feed, shift_feed)
    second_part, feed_gain_grad, feed_shift_grad = feed_pull(right_product(hidden_grad, feed_up))
    second_grad = out_grad.astype(jnp.float32) + second_part
    branch_cross = second_grad.astype(jnp.bfloat16)
    cross_output_grad = left_product(mixed_cross, branch_cross)
    return_bias_grad = jnp.sum(second_grad, axis=0)
    mixed_cross_grad = right_product(branch_cross, cross_output).astype(jnp.bfloat16)
    cross_grad_heads = heads_of(mixed_cross_grad)
    cross_delta = row_deltas(cross_grad_heads, attended_cross)
    cross_sum, key_terms, value_terms = attend_back(
        cross_heads, cross_keys, cross_values, cross_grad_heads, cross_delta, total_cross, None
    )
    key_part, value_part = (
        lax.psum_scatter(
            key_terms.astype(jnp.bfloat16), "ctx", scatter_dimension=0, tiled=True
        ).astype(jnp.float32),
        lax.psum_scatter(
            value_terms.astype(jnp.bfloat16), "ctx", scatter_dimension=0, tiled=True
        ).astype(jnp.float32),
    )
    memory_grad = jnp.concatenate(
        [key_part.astype(jnp.bfloat16), value_part.astype(jnp.bfloat16)], axis=1
    )
    source_grad = right_product(memory_grad, cross_memory)
    cross_memory_grad = left_product(source_rows, memory_grad)
    memory_offset_grad = jnp.sum(memory_grad[:, D:], axis=0, dtype=jnp.float32)
    cross_q_grad = cross_sum.astype(jnp.bfloat16) * head_scale
    cross_query_grad = left_product(normed_cross, cross_q_grad)
    query_offset_grad = jnp.sum(cross_q_grad, axis=0, dtype=jnp.float32)
    norm_value, cross_pull = jax.vjp(norm_rows, first_sum, gain_cross, shift_cross)
    first_part, cross_gain_grad, cross_shift_grad = cross_pull(
        right_product(cross_q_grad, cross_query)
    )
    first_grad = second_grad + first_part
    branch_self = first_grad.astype(jnp.bfloat16)
    self_output_grad = left_product(mixed_self, branch_self)
    output_bias_grad = jnp.sum(first_grad, axis=0)
    mixed_self_grad = right_product(branch_self, self_output).astype(jnp.bfloat16)
    keys_back, values_back = (
        lax.all_gather(keys_self, "ctx", axis=0, tiled=True),
        lax.all_gather(values_self, "ctx", axis=0, tiled=True),
    )
    self_grad_heads = heads_of(mixed_self_grad)
    self_delta = row_deltas(self_grad_heads, attended_self)
    query_sum, key_terms_self, value_terms_self = attend_back(
        query_heads, keys_back, values_back, self_grad_heads, self_delta, total_self, tag_bundle
    )
    key_own, value_own = (
        lax.psum_scatter(
            key_terms_self.astype(jnp.bfloat16), "ctx", scatter_dimension=0, tiled=True
        ).astype(jnp.float32),
        lax.psum_scatter(
            value_terms_self.astype(jnp.bfloat16), "ctx", scatter_dimension=0, tiled=True
        ).astype(jnp.float32),
    )
    query_grad = query_sum.astype(jnp.bfloat16) * head_scale
    value_grad = value_own.astype(jnp.bfloat16)
    projected_grad = jnp.concatenate([query_grad, key_own.astype(jnp.bfloat16), value_grad], axis=1)
    self_weights_grad = left_product(normed_self, projected_grad)
    query_bias_grad = jnp.sum(query_grad, axis=0, dtype=jnp.float32)
    value_bias_grad = jnp.sum(value_grad, axis=0, dtype=jnp.float32)
    norm_value, self_pull = jax.vjp(norm_rows, tok_rows, gain_self, shift_self)
    token_part, self_gain_grad, self_shift_grad = self_pull(
        right_product(projected_grad, self_weights)
    )
    tokens_grad = first_grad + token_part
    gradients = (
        self_gain_grad,
        self_shift_grad,
        self_weights_grad,
        query_bias_grad,
        value_bias_grad,
        self_output_grad,
        output_bias_grad,
        cross_gain_grad,
        cross_shift_grad,
        cross_query_grad,
        query_offset_grad,
        cross_memory_grad,
        memory_offset_grad,
        cross_output_grad,
        return_bias_grad,
        feed_gain_grad,
        feed_shift_grad,
        up_grad,
        up_bias_grad,
        down_grad,
        down_bias_grad,
    )
    halves = [lax.psum_scatter(g.astype(BF), "shard", scatter_dimension=0, tiled=True).astype(F32) for g in gradients]
    reduced = lax.psum(tuple(halves), ("group", "ctx"))
    return (block_output[None], tokens_grad[None], source_grad[None]) + tuple(reduced)


def solution(mesh):
    near = (mesh.shape["group"], mesh.shape["ctx"], mesh.shape["shard"]) == (4, 4, 2)
    placed = (
        P(("group", "shard"), "ctx", None),
        P(("group", "shard"), "ctx", None),
        P(("group", "shard"), "ctx"),
        P(("group", "shard"), "ctx"),
        P(("group", "shard"), "ctx", None),
        P("shard"),
        P("shard"),
        P("shard", None),
        P("shard"),
        P("shard"),
        P("shard", None),
        P("shard"),
        P("shard"),
        P("shard"),
        P("shard", None),
        P("shard"),
        P("shard", None),
        P("shard"),
        P("shard", None),
        P("shard"),
        P("shard"),
        P("shard"),
        P("shard", None),
        P("shard"),
        P("shard", None),
        P("shard"),
    )
    return jax.shard_map(
        pair_device if near else per_device,
        mesh=mesh,
        in_specs=placed,
        out_specs=(
            P(("group", "shard"), "ctx", None),
            P(("group", "shard"), "ctx", None),
            P(("group", "shard"), "ctx", None),
            P("shard"),
            P("shard"),
            P("shard", None),
            P("shard"),
            P("shard"),
            P("shard", None),
            P("shard"),
            P("shard"),
            P("shard"),
            P("shard", None),
            P("shard"),
            P("shard", None),
            P("shard"),
            P("shard", None),
            P("shard"),
            P("shard"),
            P("shard"),
            P("shard", None),
            P("shard"),
            P("shard", None),
            P("shard"),
        ),
        check_vma=False,
    )
```

```python
import functools
import math

import jax
import jax.numpy as jnp
from jax import lax
from jax.experimental import pallas as pl
from jax.experimental.pallas import tpu as pltpu
from jax.sharding import PartitionSpec as P

MESH = pl.DeviceIdType.MESH
BF = jnp.bfloat16
F32 = jnp.float32


def coords():
    g, z, c = lax.axis_index("group"), lax.axis_index("ctx"), lax.axis_index("shard")
    return lax.rem(g, 2), lax.div(g, 2), z, c


def device_of(x, y, z, c):
    return (y * 2 + x, z, c)


def greet(devices):
    barrier = pltpu.get_barrier_semaphore()
    for device in devices:
        pl.semaphore_signal(barrier, inc=1, device_id=device, device_id_type=MESH)
    pl.semaphore_wait(barrier, len(devices))


D = 1024
HEADS = 16
HEAD_DIM = 64


EPSILON = 1e-05
NEGATIVE = -1e30


def norm_rows(values, gain_vec, shift_vec):
    average = jnp.mean(values, axis=-1, keepdims=True)
    centred = values - average
    spread = jnp.mean(centred * centred, axis=-1, keepdims=True)
    return centred * lax.rsqrt(spread + EPSILON) * gain_vec + shift_vec


def exact_gelu(values):
    return jax.nn.gelu(values, approximate=False)


def product(left_side, right_side):
    return jnp.dot(left_side, right_side, preferred_element_type=jnp.float32)


def left_product(left_side, right_side):
    return lax.dot_general(
        left_side, right_side, (((0,), (0,)), ((), ())), preferred_element_type=jnp.float32
    )


def right_product(left_side, right_side):
    return lax.dot_general(
        left_side, right_side, (((1,), (1,)), ((), ())), preferred_element_type=jnp.float32
    )


def heads_of(matrix):
    return matrix.reshape(matrix.shape[0], HEADS, HEAD_DIM)


def allow_table(query_seg, query_pos, key_seg, key_pos):
    shared = (key_seg[None, :] == 0) | (key_seg[None, :] == query_seg[:, None])
    return shared & (key_pos[None, :] <= query_pos[:, None])


def fold_keys(folded, queries, key_block, value_block, allowed):
    run_max, run_sum, weighted = folded
    scores = jnp.einsum("qhd,khd->hqk", queries, key_block, preferred_element_type=jnp.float32)
    if allowed is not None:
        scores = jnp.where(allowed[None], scores, NEGATIVE)
    new_max = jnp.maximum(run_max, jnp.max(scores, axis=2))
    factor = jnp.exp(run_max - new_max)
    weighting = jnp.exp(scores - new_max[:, :, None])
    new_sum = run_sum * factor + jnp.sum(weighting, axis=2)
    update = jnp.einsum(
        "hqk,khd->qhd",
        weighting.astype(jnp.bfloat16),
        value_block,
        preferred_element_type=jnp.float32,
    )
    return (new_max, new_sum, weighted * jnp.transpose(factor)[:, :, None] + update)


def attend_piece(folded, queries, key_piece, value_piece, tag_bundle):
    count_rows = key_piece.shape[0]
    block_rows = math.gcd(count_rows, 512)

    def one_block(number, current):
        offset = number * block_rows
        key_block = heads_of(lax.dynamic_slice_in_dim(key_piece, offset, block_rows, 0))
        value_block = heads_of(lax.dynamic_slice_in_dim(value_piece, offset, block_rows, 0))
        allowed = None
        if tag_bundle is not None:
            query_seg, query_pos, seg_all, pos_all = tag_bundle
            key_seg = lax.dynamic_slice_in_dim(seg_all, offset, block_rows, 0)
            key_pos = lax.dynamic_slice_in_dim(pos_all, offset, block_rows, 0)
            allowed = allow_table(query_seg, query_pos, key_seg, key_pos)
        return fold_keys(current, queries, key_block, value_block, allowed)

    return lax.fori_loop(0, count_rows // block_rows, one_block, folded)


def finish(folded):
    run_max, run_sum, weighted = folded
    attended = weighted / jnp.transpose(run_sum)[:, :, None]
    return (attended, run_max + jnp.log(run_sum))


def row_deltas(out_grad, attended):
    return jnp.einsum("qhd,qhd->hq", out_grad, attended, preferred_element_type=jnp.float32)


def attend_back(queries, key_all, value_all, out_grad, row_delta, log_total, tag_bundle):
    total_rows = key_all.shape[0]
    row_count = queries.shape[0]
    block_rows = math.gcd(total_rows, 512)

    def one_block(query_acc, number):
        offset = number * block_rows
        key_block = heads_of(lax.dynamic_slice_in_dim(key_all, offset, block_rows, 0))
        value_block = heads_of(lax.dynamic_slice_in_dim(value_all, offset, block_rows, 0))
        scores = jnp.einsum("qhd,khd->hqk", queries, key_block, preferred_element_type=jnp.float32)
        if tag_bundle is not None:
            query_seg, query_pos, seg_all, pos_all = tag_bundle
            key_seg = lax.dynamic_slice_in_dim(seg_all, offset, block_rows, 0)
            key_pos = lax.dynamic_slice_in_dim(pos_all, offset, block_rows, 0)
            scores = jnp.where(
                allow_table(query_seg, query_pos, key_seg, key_pos)[None], scores, NEGATIVE
            )
        weighting = jnp.exp(scores - log_total[:, :, None])
        weight_grad = jnp.einsum(
            "qhd,khd->hqk", out_grad, value_block, preferred_element_type=jnp.float32
        )
        score_grad = (weighting * (weight_grad - row_delta[:, :, None])).astype(jnp.bfloat16)
        query_acc = query_acc + jnp.einsum(
            "hqk,khd->qhd", score_grad, key_block, preferred_element_type=jnp.float32
        )
        key_term = jnp.einsum(
            "hqk,qhd->khd", score_grad, queries, preferred_element_type=jnp.float32
        )
        value_term = jnp.einsum(
            "hqk,qhd->khd",
            weighting.astype(jnp.bfloat16),
            out_grad,
            preferred_element_type=jnp.float32,
        )
        return (query_acc, (key_term.reshape(block_rows, D), value_term.reshape(block_rows, D)))

    start_acc = jnp.zeros((row_count, HEADS, HEAD_DIM), jnp.float32)
    query_acc, terms = lax.scan(one_block, start_acc, jnp.arange(total_rows // block_rows))
    key_terms, value_terms = terms
    return (
        query_acc.reshape(row_count, D),
        key_terms.reshape(total_rows, D),
        value_terms.reshape(total_rows, D),
    )


def pair_places():
    x, y, z, c = coords()
    side = 1 - 2 * lax.rem(z, 2)
    sib, near, diag = device_of(x, y, z, 1 - c), device_of(x, y, z + side, c), device_of(x, y, z + side, 1 - c)
    far = device_of(x, y, z + 2 - 4 * lax.div(z, 2), 1 - c)
    block = 2 * c + lax.rem(z, 2)
    near_block = 2 * c + 1 - lax.rem(z, 2)
    sib_block = 2 * (1 - c) + lax.rem(z, 2)
    diag_block = 2 * (1 - c) + 1 - lax.rem(z, 2)
    home = lax.div(z, 2) == c
    return sib, near, diag, far, block, near_block, sib_block, diag_block, home


TILE = 256
LANES = 128
NEG = -1e30


def dot_nt(a, b):
    return lax.dot_general(a, b, (((1,), (1,)), ((), ())), preferred_element_type=F32)


def dot_nn(a, b):
    return lax.dot_general(a, b, (((1,), (0,)), ((), ())), preferred_element_type=F32)


def split_heads(source, target, heads):
    rows = source.shape[0]
    step = min(rows, 256)
    even = lax.broadcasted_iota(jnp.int32, (step, LANES), 1) < LANES // 2

    def one(k, carry):
        here = pl.ds(pl.multiple_of(k * step, step), step)
        for pair in range(heads // 2):
            block = source[here, pl.ds(pair * LANES, LANES)]
            target[2 * pair, here, :] = jnp.where(even, block, jnp.zeros_like(block))
            target[2 * pair + 1, here, :] = jnp.where(even, jnp.zeros_like(block), block)
        return carry

    lax.fori_loop(0, rows // step, one, 0)


def transpose_rows(source, target):
    rows = source.shape[0]
    step = min(rows, 256)

    def one(k, carry):
        here = pl.ds(pl.multiple_of(k * step, step), step)
        target[:, here] = source[here, :].astype(F32).T.astype(target.dtype)
        return carry

    lax.fori_loop(0, rows // step, one, 0)


def tree_mask(key_tile, query_tile, key_seg, query_seg, prompt):
    key_at = key_tile * TILE + lax.broadcasted_iota(jnp.int32, (TILE, TILE), 0)
    query_at = query_tile * TILE + lax.broadcasted_iota(jnp.int32, (TILE, TILE), 1)
    return (key_at <= query_at) & ((key_at < prompt) | (key_seg == query_seg))


HEAD_SCALE = 1.0 / math.sqrt(HEAD_DIM)


class Cores:
    def __init__(self):
        sib, near, diag, _, block, near_block, sib_block, diag_block, _ = pair_places()
        self.others = (near, sib, diag)
        self.blocks = (block, near_block, sib_block, diag_block)
        self.per_block = 2

    def tile_at(self, turn):
        b = lax.rem(self.blocks[0] + 1 + lax.div(turn, self.per_block), 4)
        return b * self.per_block + lax.rem(turn, self.per_block)

    def ends(self, source, target, tile, place):
        width = source.shape[1]
        src = source.at[pl.ds(pl.multiple_of(tile * TILE, TILE), TILE), :]
        row = pl.multiple_of(lax.rem(tile, self.per_block) * TILE, TILE)
        column = pl.multiple_of(place * 4 * width + self.blocks[0] * width, width)
        return src, target.at[pl.ds(row, TILE), pl.ds(column, width)]

    def give(self, source, target, tile, place, load, send, recv):
        src, dst = self.ends(source, target, tile, place)
        owner = lax.div(tile, self.per_block)

        @pl.when(owner == self.blocks[0])
        def _():
            pltpu.make_async_copy(src, dst, load).start()

        for device, b in zip(self.others, self.blocks[1:]):

            @pl.when(owner == b)
            def _():
                pltpu.make_async_remote_copy(
                    src_ref=src, dst_ref=dst, send_sem=send, recv_sem=recv.at[self.blocks[0], lax.rem(tile, self.per_block)],
                    device_id=device, device_id_type=MESH,
                ).start()

    def finish(self, source, target, place, load, send, recv):
        for k in range(self.per_block):
            tile = self.blocks[0] * self.per_block + k
            src, dst = self.ends(source, target, tile, place)
            pltpu.make_async_copy(src, dst, load.at[tile]).wait()
            for device, b in zip(self.others, self.blocks[1:]):
                sent = b * self.per_block + k
                src, dst = self.ends(source, target, sent, place)
                pltpu.make_async_remote_copy(
                    src_ref=src, dst_ref=dst, send_sem=send.at[sent], recv_sem=recv.at[b, k], device_id=device, device_id_type=MESH
                ).wait()


def trade_semaphores(tiles, places):
    dma = pltpu.SemaphoreType.DMA
    lead = () if places == 1 else (places,)
    return [dma(lead + (tiles,)), dma(lead + (tiles,)), dma(lead + (4, tiles // 4))]


def attention_params(masked, collective_id):
    if masked:
        return pltpu.CompilerParams(vmem_limit_bytes=60 << 20, collective_id=collective_id, has_side_effects=True)
    return pltpu.CompilerParams(vmem_limit_bytes=40 << 20)


def forward_kernel(heads, masked, *refs):
    if masked:
        q_ref, k_ref, v_ref, seg_col, seg_row, o_ref, lse_ref, mixed_ref, qm, vt, acc, load, send, recv = refs
    else:
        q_ref, k_ref, v_ref, o_ref, lse_ref, qm, vt, acc = refs
    n_query, n_key = q_ref.shape[0] // TILE, k_ref.shape[0] // TILE
    prompt_tiles = n_key // 2
    if masked:
        cores = Cores()
        greet(cores.others)
    split_heads(q_ref, qm, heads)
    transpose_rows(v_ref, vt)
    H = range(heads)

    def query_tile(turn, carry):
        i = cores.tile_at(turn) if masked else turn
        rows = pl.ds(pl.multiple_of(i * TILE, TILE), TILE)
        queries = [qm[h, rows, :] for h in H]
        acc[...] = jnp.zeros_like(acc)

        def tile(j, mask, state, span=1):
            keys = pl.ds(pl.multiple_of(j * TILE, TILE), span * TILE)
            old_m, old_l = state
            scores = [dot_nt(k_ref[keys, pl.ds(h // 2 * LANES, LANES)], queries[h]) for h in H]
            if mask is not None:
                scores = [jnp.where(mask, s, NEG) for s in scores]
            new_m = [jnp.maximum(old_m[h], jnp.max(scores[h], axis=0, keepdims=True)) for h in H]
            weights = [jnp.exp(scores[h] - new_m[h]) for h in H]
            if mask is not None:
                weights = [jnp.where(mask, w, 0.0) for w in weights]
            factor = [jnp.exp(old_m[h] - new_m[h]) for h in H]
            new_l = [old_l[h] * factor[h] + jnp.sum(weights[h], axis=0, keepdims=True) for h in H]
            low = [w.astype(BF) for w in weights]
            for h in H:
                part = pl.ds(h * 64, 64)
                acc[part, :] = acc[part, :] * factor[h] + dot_nn(vt[part, keys], low[h])
            return (new_m, new_l)

        state = ([jnp.full((1, TILE), NEG, F32)] * heads, [jnp.zeros((1, TILE), F32)] * heads)
        if masked:
            later = i >= prompt_tiles
            state = lax.fori_loop(0, jnp.where(later, 0, i), lambda j, c: tile(j, None, c), state)
            state = lax.fori_loop(0, jnp.where(later, 1, 0), lambda j, c: tile(0, None, c, prompt_tiles), state)

            def near(j, c):
                keys = pl.ds(pl.multiple_of(j * TILE, TILE), TILE)
                return tile(j, tree_mask(j, i, seg_col[keys, :], seg_row[:, rows], prompt_tiles * TILE), c)

            first = jnp.where(i > prompt_tiles, i - 1, i)
            state = lax.fori_loop(first, i + 1, near, state)
        else:
            state = tile(0, None, state, n_key)
        m, l = state
        for h in H:
            part = pl.ds(h * 64, 64)
            acc[part, :] = acc[part, :] / l[h]
            lse_ref[pl.ds(h, 1), rows] = m[h] + jnp.log(l[h])
        o_ref[rows, :] = acc[...].T.astype(BF)
        if masked:
            cores.give(o_ref, mixed_ref, i, 0, load.at[i], send.at[i], recv)
        return carry

    lax.fori_loop(0, n_query, query_tile, 0)
    if masked:
        cores.finish(o_ref, mixed_ref, 0, load, send, recv)


def attention_forward(q, k, v, seg=None):
    heads, width = 4, 256
    n, m, groups = q.shape[0], k.shape[0], q.shape[1] // 256
    masked = seg is not None
    column = lambda rows: pl.BlockSpec((rows, width), lambda p: (0, p))
    whole = lambda shape: pl.BlockSpec(shape, lambda p: (0, 0))
    extra = [seg.reshape(n, 1), seg.reshape(1, n)] if masked else []
    return pl.pallas_call(
        functools.partial(forward_kernel, heads, masked),
        grid=(groups,),
        out_shape=(jax.ShapeDtypeStruct((n, q.shape[1]), BF), jax.ShapeDtypeStruct((groups, 8, n), F32))
        + ((jax.ShapeDtypeStruct((n // 4, 4 * width), BF),) if masked else ()),
        in_specs=[column(n), column(m), column(m)] + [whole(e.shape) for e in extra],
        out_specs=(column(n), pl.BlockSpec((None, 8, n), lambda p: (p, 0, 0)))
        + ((pl.BlockSpec(memory_space=pltpu.HBM),) if masked else ()),
        scratch_shapes=[
            pltpu.VMEM((heads, n, LANES), BF),
            pltpu.VMEM((width, m), BF),
            pltpu.VMEM((width, TILE), F32),
        ]
        + (trade_semaphores(n // TILE, 1) if masked else []),
        compiler_params=attention_params(masked, 3),
        cost_estimate=pl.CostEstimate(flops=24 * n * m * q.shape[1], bytes_accessed=4 * (n + m) * q.shape[1], transcendentals=n * m * heads * groups),
        name="attention_forward",
    )(q, k, v, *extra)


CH = 512
WD = 1024
SETS = ((0, 512), (512, 512))
RING = 4
KEEP = 6
CROSS_AT = 3
DENSE_AT = 7
FIRST_AT = 8
KEYS_AT = 8
GATHER_AT = 12
SOURCE_AT = 13


def backward_parts(heads, cores, q_ref, k_ref, v_ref, o_ref, lse_ref, seg_col, seg_row, projected_ref,
                   dq_ref, dk_ref, dv_ref, g_ref, qm, gm, kt, dqt, dk_acc, dv_acc, delta, load, send, recv):
    n_query, n_key = q_ref.shape[0] // TILE, k_ref.shape[0] // TILE
    prompt_tiles = n_key // 2
    H = range(heads)
    lane = [pl.ds(h // 2 * LANES, LANES) for h in H]

    def first():
        split_heads(q_ref, qm, heads)
        split_heads(g_ref, gm, heads)
        transpose_rows(k_ref, kt)
        dqt[...] = jnp.zeros_like(dqt)

        def deltas(i, carry):
            rows = pl.ds(pl.multiple_of(i * TILE, TILE), TILE)
            product = (g_ref[rows, :].astype(F32) * o_ref[rows, :].astype(F32)).T
            for h in H:
                delta[pl.ds(h, 1), rows] = jnp.sum(product[h * 64 : h * 64 + 64, :], axis=0, keepdims=True)
            return carry

        lax.fori_loop(0, n_query, deltas, 0)

    def send_rows(source, place, j):
        cores.give(source, projected_ref, j, place, load.at[place, j], send.at[place, j], recv.at[place])

    def finish_queries(i):
        rows = pl.ds(pl.multiple_of(i * TILE, TILE), TILE)
        dq_ref[rows, :] = (dqt[:, rows].T.astype(BF).astype(F32) * HEAD_SCALE).astype(BF)
        send_rows(dq_ref, 0, i)

    def key_tile(turn):
        j = lax.rem(turn + prompt_tiles, n_key)
        keys = pl.ds(pl.multiple_of(j * TILE, TILE), TILE)
        dk_acc[...] = jnp.zeros_like(dk_acc)
        dv_acc[...] = jnp.zeros_like(dv_acc)

        def tile(i, mask):
            rows = pl.ds(pl.multiple_of(i * TILE, TILE), TILE)
            scores = [dot_nt(k_ref[keys, lane[h]], qm[h, rows, :]) for h in H]
            change = [dot_nt(v_ref[keys, lane[h]], gm[h, rows, :]) for h in H]
            weights = [jnp.exp(scores[h] - lse_ref[pl.ds(h, 1), rows]) for h in H]
            if mask is not None:
                weights = [jnp.where(mask, w, 0.0) for w in weights]
            back = [(weights[h] * (change[h] - delta[pl.ds(h, 1), rows])).astype(BF) for h in H]
            low = [w.astype(BF) for w in weights]
            for pair in range(heads // 2):
                a, b = 2 * pair, 2 * pair + 1
                dv_acc[:, lane[a]] += dot_nn(low[a], gm[a, rows, :]) + dot_nn(low[b], gm[b, rows, :])
                dk_acc[:, lane[a]] += dot_nn(back[a], qm[a, rows, :]) + dot_nn(back[b], qm[b, rows, :])
            for h in H:
                part = pl.ds(h * 64, 64)
                dqt[part, rows] += dot_nn(kt[part, keys], back[h])

        def near(i, carry):
            rows = pl.ds(pl.multiple_of(i * TILE, TILE), TILE)
            tile(i, tree_mask(j, i, seg_col[keys, :], seg_row[:, rows], prompt_tiles * TILE))
            return carry

        prompt = j < prompt_tiles
        last = jnp.where(prompt, j, jnp.minimum(j + 1, n_query - 1))
        lax.fori_loop(j, last + 1, near, 0)
        lax.fori_loop(jnp.where(prompt, j + 1, n_query), n_query, lambda i, c: (tile(i, None), c)[1], 0)
        dk_ref[keys, :] = dk_acc[...].astype(BF)
        dv_ref[keys, :] = dv_acc[...].astype(BF)
        send_rows(dk_ref, 1, j)
        send_rows(dv_ref, 2, j)

        @pl.when(prompt)
        def _():
            finish_queries(j)

    def last_queries():
        lax.fori_loop(prompt_tiles, n_query, lambda i, c: (finish_queries(i), c)[1], 0)

    def end():
        for place, source in enumerate((dq_ref, dk_ref, dv_ref)):
            cores.finish(source, projected_ref, place, load.at[place], send.at[place], recv.at[place])

    return first, key_tile, last_queries, end, n_key


def finish_kernel(plan, n_sources, *refs):
    n_chunks = len(plan)
    q_hbm, k_hbm, v_hbm, o_hbm, lse_ref, seg_col, seg_row, cross_lse, gain_ref, cross_gain, small = refs[:11]
    sources = list(refs[11 : 11 + n_sources])
    at = 11 + n_sources
    tok_hbm, block_hbm, first_hbm, second_hbm, cross_q, cross_k, cross_v, cross_o, cross_g = refs[at : at + 9]
    weights_ref, memory_ref, query_w, output_w = refs[at + 9 : at + 13]
    out, small_out, tokens_home, block_home, source_home, q_grad, branch_self, key_terms, value_terms, projected_ref = refs[at + 13 : at + 23]
    (
        dq_ref, dk_ref, dv_ref, g_ref, qm, gm, kt, dqt, dk_acc, dv_acc, delta, trade_load, trade_send, trade_recv,
        tokens_out, part_ref, src_b, src_r1, src_r2, home_sem, away_send, away_recv, src_send, src_recv, grad_send, grad_recv,
        acc, snd, r0, r1, r2, r3, r4, sv, sr, xbuf, ybuf, wbuf, pbuf,
        x_sem, y_sem, w_sem, p_sem, take_sem, s0s, s0r, hs, hr, gs, gr, put_sem, svs, svr,
        mix_grad, first_ref, fbuf, tbuf, sums_ref, in_sem, out_sem, f_sem, q_ref, k_ref, v_ref, o_ref, self_sem,
    ) = refs[at + 23 :]
    sources += [q_grad, branch_self, key_terms, value_terms, projected_ref]
    x, y, z, c = coords()
    cores = Cores()
    sib = device_of(x, y, z, 1 - c)
    dx, dy = device_of(1 - x, y, z, c), device_of(x, 1 - y, z, c)
    dz2, dz1 = device_of(x, y, z + 2 - 4 * lax.div(z, 2), c), cores.others[0]
    far = device_of(x, y, z + 2 - 4 * lax.div(z, 2), 1 - c)
    home = lax.div(z, 2) == c
    greet((sib, dx, dy, dz2, dz1, cores.others[2], far))
    z2, z1 = lax.div(z, 2), lax.rem(z, 2)

    first, key_tile, last_queries, end_trade, n_key = backward_parts(
        4, cores, q_ref, k_ref, v_ref, o_ref, lse_ref, seg_col, seg_row, projected_ref,
        dq_ref, dk_ref, dv_ref, g_ref, qm, gm, kt, dqt, dk_acc, dv_acc, delta, trade_load, trade_send, trade_recv,
    )

    def remote(src, dst, send, recv, device):
        return pltpu.make_async_remote_copy(src_ref=src, dst_ref=dst, send_sem=send, recv_sem=recv, device_id=device, device_id_type=MESH)

    def send_home(i, src, dst, wait):
        @pl.when(home)
        def _():
            copy = pltpu.make_async_copy(src, dst, home_sem.at[i])
            copy.wait() if wait else copy.start()

        @pl.when(jnp.logical_not(home))
        def _():
            copy = remote(src, dst, away_send.at[i], away_recv.at[i], far)
            copy.wait() if wait else copy.start()

    own_block = cores.blocks[0]
    part_rows, head_cols = mix_grad.shape[0], q_ref.shape[1]
    grad_rows = g_ref.at[pl.ds(pl.multiple_of(own_block * part_rows, part_rows), part_rows), :]

    def grad_copy(k):
        cols = pl.ds(pl.multiple_of(cores.blocks[1 + k] * head_cols, head_cols), head_cols)
        return remote(mix_grad.at[:, cols], grad_rows, grad_send.at[k], grad_recv.at[k], cores.others[k])

    half_rows = part_ref.shape[0] // 2
    quarter = half_rows // 2
    src_a = part_ref.at[pl.ds(0, half_rows), :]

    def source_sib():
        return remote(part_ref.at[pl.ds(half_rows, half_rows), :], src_r1, src_send.at[0], src_recv.at[0], sib)

    def source_near():
        return remote(src_a.at[pl.ds(quarter, quarter), :], src_r2, src_send.at[1], src_recv.at[1], dz1)

    def add_blocks(target, one_ref, other_ref, rows):
        def one(k, carry):
            here = pl.ds(pl.multiple_of(k * 32, 32), 32)
            target[here, :] = (one_ref[here, :].astype(F32) + other_ref[here, :].astype(F32)).astype(BF)
            return carry

        lax.fori_loop(0, rows // 32, one, 0)

    def load(pairs):
        copies = [pltpu.make_async_copy(src, dst, f_sem.at[k]) for k, (src, dst) in enumerate(pairs)]
        for copy in copies:
            copy.start()
        for copy in copies:
            copy.wait()

    block_stage = part_ref.at[pl.ds(0, part_rows), :]

    def send_block():
        load([(block_hbm, block_stage)])
        send_home(0, block_stage, block_home, False)

    n_cross, m_cross = cross_q.shape[0], cross_k.shape[0]
    low, high = pl.ds(0, m_cross), pl.ds(m_cross, m_cross)
    cdq, cdk, cdv = dq_ref.at[pl.ds(0, n_cross), :], dk_ref.at[low, :], dv_ref.at[low, :]
    cq, cg, co = (dq_ref.at[pl.ds(n_cross * k, n_cross), :] for k in (1, 2, 3))
    ck, cv = dk_ref.at[high, :], dv_ref.at[high, :]

    def head_columns(group):
        return pl.ds(pl.multiple_of(group * head_cols, head_cols), head_cols)

    def cross_ins(group):
        pairs = ((cross_q, cq), (cross_g, cg), (cross_o, co), (cross_k, ck), (cross_v, cv))
        return [pltpu.make_async_copy(src.at[:, head_columns(group)], dst, in_sem.at[k]) for k, (src, dst) in enumerate(pairs)]

    def cross_outs(group):
        pairs = ((cdq, q_grad), (cdk, key_terms), (cdv, value_terms))
        return [pltpu.make_async_copy(src, dst.at[:, head_columns(group)], out_sem.at[k]) for k, (src, dst) in enumerate(pairs)]

    def cross_group(group):
        heads = head_cols // HEAD_DIM
        H = range(heads)
        lane = [pl.ds(h // 2 * LANES, LANES) for h in H]
        rows = pl.ds(0, n_cross)
        for copy in cross_ins(group):
            copy.wait()

        @pl.when(group > 0)
        def _():
            for copy in cross_outs(group - 1):
                copy.wait()

        split_heads(cq, qm, heads)
        split_heads(cg, gm, heads)
        transpose_rows(ck, kt)
        dqt[:, rows] = jnp.zeros((head_cols, n_cross), F32)
        product = (cg[...].astype(F32) * co[...].astype(F32)).T
        for h in H:
            delta[pl.ds(h, 1), rows] = jnp.sum(product[h * 64 : h * 64 + 64, :], axis=0, keepdims=True)

        def one(j, carry):
            keys = pl.ds(pl.multiple_of(j * TILE, TILE), TILE)
            scores = [dot_nt(ck[keys, lane[h]], qm[h, rows, :]) for h in H]
            change = [dot_nt(cv[keys, lane[h]], gm[h, rows, :]) for h in H]
            weights = [jnp.exp(scores[h] - cross_lse[group, pl.ds(h, 1), :]) for h in H]
            back = [(weights[h] * (change[h] - delta[pl.ds(h, 1), rows])).astype(BF) for h in H]
            kept = [w.astype(BF) for w in weights]
            for pair in range(heads // 2):
                a, b = 2 * pair, 2 * pair + 1
                cdv[keys, lane[a]] = (dot_nn(kept[a], gm[a, rows, :]) + dot_nn(kept[b], gm[b, rows, :])).astype(BF)
                cdk[keys, lane[a]] = (dot_nn(back[a], qm[a, rows, :]) + dot_nn(back[b], qm[b, rows, :])).astype(BF)
            for h in H:
                part = pl.ds(h * 64, 64)
                dqt[part, rows] += dot_nn(kt[part, keys], back[h])
            return carry

        lax.fori_loop(0, m_cross // TILE, one, 0)
        cdq[...] = (dqt[:, rows].T.astype(BF).astype(F32) * HEAD_SCALE).astype(BF)
        sums_ref[pl.ds(0, 1), head_columns(group)] = jnp.sum(cdq[...].astype(F32), axis=0, keepdims=True)
        sums_ref[pl.ds(1, 1), head_columns(group)] = jnp.sum(cdv[...].astype(F32), axis=0, keepdims=True)
        for copy in cross_outs(group):
            copy.start()

        @pl.when(group < n_groups - 1)
        def _():
            for copy in cross_ins(group + 1):
                copy.start()

    n_groups = cross_q.shape[1] // head_cols

    def norm_back(values, e, gain):
        centred = values - jnp.mean(values, axis=-1, keepdims=True)
        r = lax.rsqrt(jnp.mean(centred * centred, axis=-1, keepdims=True) + EPSILON)
        xhat = centred * r
        t = e * gain
        return r * (t - jnp.mean(t, axis=-1, keepdims=True) - xhat * jnp.mean(t * xhat, axis=-1, keepdims=True)), xhat

    def dense_weights():
        pairs = ((query_w, wbuf.at[:, pl.ds(0, WD)]), (output_w, wbuf.at[:, pl.ds(WD, WD)]))
        return [pltpu.make_async_copy(src, dst, w_sem.at[1 + k]) for k, (src, dst) in enumerate(pairs)]

    def dense():
        for copy in (*cross_outs(n_groups - 1), *dense_weights()):
            copy.wait()
        step = pbuf.shape[0]

        def one(k, sums):
            rows = pl.ds(pl.multiple_of(k * step, step), step)
            load([(q_grad.at[rows, :], pbuf.at[:, pl.ds(0, WD)]), (first_hbm.at[rows, :], fbuf.at[0]), (second_hbm.at[rows, :], fbuf.at[1])])
            e = dot_nt(pbuf[:, :WD], wbuf[:, :WD])
            change, xhat = norm_back(fbuf[0], e, cross_gain[...])
            total = fbuf[1] + change
            first_ref[rows, :] = total
            pbuf[:, WD : 2 * WD] = total.astype(BF)
            mix_grad[rows, :] = dot_nt(pbuf[:, WD : 2 * WD], wbuf[:, WD : 2 * WD]).astype(BF)
            load([(pbuf.at[:, pl.ds(WD, WD)], branch_self.at[rows, :])])
            return tuple(s + jnp.sum(v, axis=0, keepdims=True) for s, v in zip(sums, (total, e * xhat, e)))

        sums = lax.fori_loop(0, n_cross // step, one, (jnp.zeros((1, WD), F32),) * 3)
        for k, total in enumerate(sums):
            sums_ref[pl.ds(2 + k, 1), :] = total
        for k in range(3):
            grad_copy(k).start()
        w_copy().start()

    def self_ins():
        pairs = ((q_hbm, q_ref), (k_hbm, k_ref), (v_hbm, v_ref), (o_hbm, o_ref))
        return [pltpu.make_async_copy(src, dst, self_sem.at[k]) for k, (src, dst) in enumerate(pairs)]

    def begin_keys():
        for copy in self_ins():
            copy.wait()
        g_ref[pl.ds(pl.multiple_of(own_block * part_rows, part_rows), part_rows), :] = mix_grad[
            :, pl.ds(pl.multiple_of(own_block * head_cols, head_cols), head_cols)
        ]
        for k in range(3):
            grad_copy(k).wait()
        first()

    def memory_copy():
        return pltpu.make_async_copy(memory_ref, wbuf.at[:, pl.ds(0, 2 * WD)], w_sem.at[0])

    def source_0(begin):
        step = pbuf.shape[0]
        blocks = part_ref.shape[0] // step // 2

        def one(k, carry):
            rows = pl.ds(pl.multiple_of(k * step, step), step)
            copies = [
                pltpu.make_async_copy(terms.at[rows, :], pbuf.at[:, pl.ds(p * WD, WD)], take_sem.at[p])
                for p, terms in enumerate((key_terms, value_terms))
            ]
            for copy in copies:
                copy.start()
            for copy in copies:
                copy.wait()
            part_ref[rows, :] = dot_nt(pbuf[:, : 2 * WD], wbuf[:, : 2 * WD]).astype(BF)
            return carry

        lax.fori_loop(begin * blocks, (begin + 1) * blocks, one, 0)

    def source_1():
        source_sib().wait()
        add_blocks(src_a, part_ref, src_r1, half_rows)
        source_near().start()

    def source_2():
        source_near().wait()
        add_blocks(src_b, src_a, src_r2, quarter)
        send_home(1, src_b, source_home, False)

    def fetch(k):
        xi, kind, i, yi, column = plan[k]
        depth = sources[xi].shape[0]
        half = sources[xi].shape[1] // 2
        at = i * CH if kind == "rows" else 0
        for p, h in enumerate((c, 1 - c)):
            pltpu.make_async_copy(
                sources[xi].at[:, pl.ds(pl.multiple_of(h * half + at, CH), CH)],
                xbuf.at[k % 2, pl.ds(0, depth), pl.ds(p * CH, CH)],
                x_sem.at[k % 2, p],
            ).start()
        pltpu.make_async_copy(sources[yi].at[:, pl.ds(column * WD, WD)], ybuf.at[k % 2, pl.ds(0, depth), :], y_sem.at[k % 2]).start()

    def swap_copy(j):
        return pltpu.make_async_remote_copy(
            src_ref=snd.at[lax.rem(j, 2)], dst_ref=r0.at[lax.rem(j, RING)], send_sem=s0s.at[j], recv_sem=s0r.at[j], device_id=sib, device_id_type=MESH
        )

    def make(j, depth):
        slot, keep = lax.rem(j, 2), lax.rem(j, KEEP)
        deep = pl.ds(0, depth)
        for p in range(2):
            side = xbuf.at[slot, deep, pl.ds(p * CH, CH)]
            pltpu.make_async_copy(side, side, x_sem.at[slot, p]).wait()
        pltpu.make_async_copy(ybuf.at[slot, deep, :], ybuf.at[slot, deep, :], y_sem.at[slot]).wait()
        step = 128

        def one(k, carry):
            rows = pl.ds(pl.multiple_of(k * step, step), step)
            more = pl.ds(pl.multiple_of(CH + k * step, step), step)
            across = (((0,), (0,)), ((), ()))
            own = lax.dot_general(xbuf[slot, deep, rows], ybuf[slot, deep, :], across, preferred_element_type=F32)
            acc[keep, rows, :] = own.astype(BF)
            other = lax.dot_general(xbuf[slot, deep, more], ybuf[slot, deep, :], across, preferred_element_type=F32)
            snd[slot, rows, :] = other.astype(BF)
            return carry

        lax.fori_loop(0, CH // step, one, 0)

    rbufs = (r1, r2, r3, r4)

    def axis(jj, s, q):
        even = lax.rem(jj, 2) == 0
        along = ((("one", "two", "near", "far"), ("two", "one", "near", "far"))[s])[q]
        if along == "near":
            return dz1, z1
        if along == "far":
            return dz2, z2
        use_x = even if along == "one" else jnp.logical_not(even)
        return (jnp.where(use_x, dx[0], dy[0]), z, c), jnp.where(use_x, x, y)

    def start_of(jj, s, step):
        row = 0
        for q in range(step):
            row = row + axis(jj, s, q)[1] * (CH >> (q + 1))
        return row

    def halve_copy(jj, s, q):
        size = CH >> (q + 1)
        device, bit = axis(jj, s, q)
        row = start_of(jj, s, q) + (1 - bit) * size
        return pltpu.make_async_remote_copy(
            src_ref=acc.at[lax.rem(jj, KEEP), pl.ds(pl.multiple_of(row, 32), size), pl.ds(*SETS[s])],
            dst_ref=rbufs[q].at[lax.rem(jj, RING), :, pl.ds(*SETS[s])],
            send_sem=hs.at[jj, s, q],
            recv_sem=hr.at[jj, s, q],
            device_id=device,
            device_id_type=MESH,
        )

    def give_copy(jj, s, q):
        size = CH >> (q + 1)
        block = out.at[jj, pl.ds(pl.multiple_of(start_of(jj, s, q + 1), 32), size), pl.ds(*SETS[s])]
        return pltpu.make_async_remote_copy(
            src_ref=block, dst_ref=block, send_sem=gs.at[jj, s, q], recv_sem=gr.at[jj, s, q], device_id=axis(jj, s, q)[0], device_id_type=MESH
        )

    def put_copy(jj, s):
        rows = pl.ds(pl.multiple_of(start_of(jj, s, 4), 32), CH >> 4)
        return pltpu.make_async_copy(
            acc.at[lax.rem(jj, KEEP), rows, pl.ds(*SETS[s])], out.at[jj, rows, pl.ds(*SETS[s])], put_sem.at[jj, s]
        )

    def add_rows(jj, s, q):
        size = CH >> (q + 1)
        row = pl.multiple_of(start_of(jj, s, q + 1), 32)
        span = min(size, 64)
        keep, slot, cols = lax.rem(jj, KEEP), lax.rem(jj, RING), pl.ds(*SETS[s])

        def one(k, carry):
            here = pl.ds(pl.multiple_of(row + k * span, 32), span)
            there = pl.ds(pl.multiple_of(k * span, 32), span)
            acc[keep, here, cols] = acc[keep, here, cols] + rbufs[q][slot, there, cols]
            return carry

        lax.fori_loop(0, size // span, one, 0)

    def phase0(jj):
        swap_copy(jj).wait()
        keep, slot = lax.rem(jj, KEEP), lax.rem(jj, RING)

        def one(k, carry):
            here = pl.ds(pl.multiple_of(k * 32, 32), 32)
            acc[keep, here, :] = acc[keep, here, :] + r0[slot, here, :]
            return carry

        lax.fori_loop(0, CH // 32, one, 0)
        for s in range(len(SETS)):
            halve_copy(jj, s, 0).start()

    def phase_halve(jj, q):
        for s in range(len(SETS)):
            halve_copy(jj, s, q).wait()
            add_rows(jj, s, q)
            if q < 3:
                halve_copy(jj, s, q + 1).start()
            else:
                put_copy(jj, s).start()
        if q == 3:
            for s in range(len(SETS)):
                put_copy(jj, s).wait()
                give_copy(jj, s, 3).start()

    def phase_give(jj, q):
        for s in range(len(SETS)):
            give_copy(jj, s, q).wait()
            if q > 0:
                give_copy(jj, s, q - 1).start()

    partners = (sib, dx, dy, dz2, dz1)

    def small_copy(p):
        return pltpu.make_async_remote_copy(
            src_ref=sv.at[p], dst_ref=sr.at[p], send_sem=svs.at[p], recv_sem=svr.at[p], device_id=partners[p], device_id_type=MESH
        )

    def small_phase(p):
        if p > 0:
            small_copy(p - 1).wait()
            sv[p] = sv[p - 1] + sr[p - 1]
        if p < 5:
            small_copy(p).start()
        else:
            small_out[...] = sv[5]

    def w_copy():
        return pltpu.make_async_copy(weights_ref, wbuf, w_sem.at[0])

    def gather():
        end_trade()
        w_copy().wait()
        d = WD
        step = 128
        zero = jnp.zeros((1, d), F32)

        def one(k, sums):
            rows = pl.ds(pl.multiple_of(k * step, step), step)
            load([(projected_ref.at[rows, :], pbuf), (tok_hbm.at[rows, :], tbuf)])
            projected = pbuf[...]
            e = dot_nt(projected, wbuf[...])
            change, xhat = norm_back(tbuf[...].astype(F32), e, gain_ref[...])
            tokens_out[rows, :] = (first_ref[rows, :] + change).astype(BF)
            wide = projected.astype(F32)
            new = (e * xhat, e, wide[:, :d], wide[:, 2 * d :])
            return tuple(s + jnp.sum(v, axis=0, keepdims=True) for s, v in zip(sums, new))

        sums = lax.fori_loop(0, n_cross // step, one, (zero,) * 4)
        sv[0] = small[...]
        for row, total in enumerate((*sums, *(sums_ref[pl.ds(k, 1), :] for k in (2, 3, 4, 0, 1)))):
            sv[0, pl.ds(row, 1), :] = total
        send_home(2, tokens_out, tokens_home, False)
        memory_copy().start()

    late = [k for k in range(n_chunks) if plan[k][3] == len(sources) - 1]
    depth_of = [sources[entry[0]].shape[0] for entry in plan]
    fetch(0)
    for copy in (*cross_ins(0), *dense_weights(), *self_ins()):
        copy.start()

    def step(t, carry):
        for k in range(1, n_chunks):
            if k not in late:
                pl.when(t + 1 == k)(functools.partial(fetch, k))
        for depth in sorted(set(depth_of)):
            these = [t == k for k in range(n_chunks) if depth_of[k] == depth]
            pl.when(functools.reduce(jnp.logical_or, these))(functools.partial(make, t, depth))

        @pl.when(t < n_chunks)
        def _():
            swap_copy(t).start()

        def guarded(lag, what):
            @pl.when((t >= lag) & (t < n_chunks + lag))
            def _():
                what(t - lag)

        guarded(1, phase0)
        for q in range(4):
            guarded(q + 2, functools.partial(phase_halve, q=q))
        for q in range(3, -1, -1):
            guarded(9 - q, functools.partial(phase_give, q=q))
        pl.when(t == 0)(send_block)
        pl.when((t >= CROSS_AT) & (t < CROSS_AT + n_groups))(functools.partial(cross_group, t - CROSS_AT))
        pl.when(t == DENSE_AT)(dense)
        pl.when(t == FIRST_AT)(begin_keys)
        half = n_key // 2
        begin = jnp.where(t == KEYS_AT, 0, t - KEYS_AT + half - 1)
        end = jnp.where(t == KEYS_AT, half, jnp.where((t > KEYS_AT) & (t < KEYS_AT + half), begin + 1, begin))
        end = jnp.where(t == KEYS_AT + half - 1, n_key, end)
        lax.fori_loop(begin, end, lambda turn, inner: (key_tile(turn), inner)[1], 0)
        pl.when(t == KEYS_AT + half - 1)(last_queries)

        pl.when(t == GATHER_AT)(gather)
        @pl.when(t == SOURCE_AT)
        def _():
            send_home(0, block_stage, block_home, True)
            memory_copy().wait()

        @pl.when((t == SOURCE_AT) | (t == SOURCE_AT + 1))
        def _():
            source_0(t - SOURCE_AT)

        pl.when(t == SOURCE_AT + 1)(lambda: source_sib().start())
        pl.when(t == SOURCE_AT + 2)(source_1)
        pl.when(t == SOURCE_AT + 3)(source_2)
        for p in range(6):
            pl.when(t == GATHER_AT + 1 + p)(functools.partial(small_phase, p))
        for k in late:
            pl.when(t + 1 == k)(functools.partial(fetch, k))
        return carry

    lax.fori_loop(0, n_chunks + 9, step, 0)
    send_home(1, src_b, source_home, True)
    send_home(2, tokens_out, tokens_home, True)


def finish_backward(plan, attention, cross, gains, small, sources, local, weights):
    n_chunks = len(plan)
    q, k, v, mix, lse, seg = attention
    n, width = q.shape
    rows, d = local[0].shape
    source_rows = cross[1].shape[0]
    hbm = pl.BlockSpec(memory_space=pltpu.HBM)
    vmem = pl.BlockSpec(memory_space=pltpu.VMEM)
    dma = pltpu.SemaphoreType.DMA
    sets = len(SETS)
    near = [q, k, v, mix, lse, seg.reshape(n, 1), seg.reshape(1, n), cross[5], *(g.reshape(1, d) for g in gains), small]
    far = [*sources, *local, *cross[:5], *weights]
    ring = lambda rows: pltpu.VMEM((RING, rows, WD), BF)
    return pl.pallas_call(
        functools.partial(finish_kernel, plan, len(sources)),
        out_shape=(
            jax.ShapeDtypeStruct((n_chunks, CH, WD), BF),
            jax.ShapeDtypeStruct(small.shape, F32),
            jax.ShapeDtypeStruct((rows, d), BF),
            jax.ShapeDtypeStruct((rows, d), BF),
            jax.ShapeDtypeStruct((source_rows // 4, d), BF),
            jax.ShapeDtypeStruct((rows, d), BF),
            jax.ShapeDtypeStruct((rows, d), BF),
            jax.ShapeDtypeStruct((source_rows, d), BF),
            jax.ShapeDtypeStruct((source_rows, d), BF),
            jax.ShapeDtypeStruct((rows, 12 * width), BF),
        ),
        in_specs=[hbm] * 4 + [vmem] * (len(near) - 4) + [hbm] * len(far),
        out_specs=(hbm, vmem) + (hbm,) * 8,
        scratch_shapes=[pltpu.VMEM((n, width), BF)] * 4
        + [
            pltpu.VMEM((4, n, LANES), BF),
            pltpu.VMEM((4, n, LANES), BF),
            pltpu.VMEM((width, n), BF),
            pltpu.VMEM((width, n), F32),
            pltpu.VMEM((TILE, width), F32),
            pltpu.VMEM((TILE, width), F32),
            pltpu.VMEM((8, n), F32),
        ]
        + trade_semaphores(n // TILE, 3)
        + [pltpu.VMEM(shape, BF) for shape in ((rows, d), (source_rows, d), (source_rows // 4, d), (source_rows // 2, d), (source_rows // 4, d))]
        + [dma((3,)), dma((3,)), dma((3,)), dma((2,)), dma((2,)), dma((3,)), dma((3,))]
        + [pltpu.VMEM((KEEP, CH, WD), BF), pltpu.VMEM((2, CH, WD), BF)]
        + [ring(CH >> q) for q in range(5)]
        + [
            pltpu.VMEM((6,) + small.shape, F32),
            pltpu.VMEM((5,) + small.shape, F32),
            pltpu.VMEM((2, source_rows, 2 * CH), BF),
            pltpu.VMEM((2, source_rows, WD), BF),
            pltpu.VMEM(weights[0].shape, BF),
            pltpu.VMEM((128, 12 * width), BF),
            dma((2, 2)),
            dma((2,)),
            dma((3,)),
            dma((1,)),
            dma((2,)),
            dma((n_chunks,)),
            dma((n_chunks,)),
            dma((n_chunks, sets, 4)),
            dma((n_chunks, sets, 4)),
            dma((n_chunks, sets, 4)),
            dma((n_chunks, sets, 4)),
            dma((n_chunks, sets)),
            dma((5,)),
            dma((5,)),
            pltpu.VMEM((rows, d), BF),
            pltpu.VMEM((rows, d), F32),
            pltpu.VMEM((2, 128, d), F32),
            pltpu.VMEM((128, d), BF),
            pltpu.VMEM((8, d), F32),
            dma((5,)),
            dma((3,)),
            dma((3,)),
        ]
        + [pltpu.VMEM((n, width), BF)] * 4
        + [dma((4,))],
        compiler_params=pltpu.CompilerParams(collective_id=1, has_side_effects=True, vmem_limit_bytes=62 << 20),
        cost_estimate=pl.CostEstimate(flops=200 << 30, bytes_accessed=50 << 20, transcendentals=0),
        name="finish_backward",
    )(*near, *far)


def widen_kernel(places, *refs):
    src, outs = refs[0], refs[1 : 1 + len({place for place, _, _ in places})]
    low, wide, load, put = refs[1 + len(outs) :]
    n = len(places)

    def fetch(j):
        return pltpu.make_async_copy(src.at[j], low.at[j], load.at[j])

    def store(j):
        place, row, column = places[j]
        return pltpu.make_async_copy(wide.at[j], outs[place].at[pl.ds(row, CH), pl.ds(column, WD)], put.at[j])

    for j in range(n):
        fetch(j).start()
    for j in range(n):
        fetch(j).wait()

        def one(k, carry):
            rows = pl.ds(pl.multiple_of(k * 64, 64), 64)
            wide[j, rows, :] = low[j, rows, :].astype(F32)
            return carry

        lax.fori_loop(0, CH // 64, one, 0)
        store(j).start()
    for j in range(n):
        store(j).wait()


def widen(summed, pieces):
    places = []
    for place, (kind, count) in enumerate(pieces):
        places += [(place, 0, k * WD) if kind == "cols" else (place, k * CH, 0) for k in range(count)]
    n = len(places)
    hbm = pl.BlockSpec(memory_space=pltpu.HBM)
    return pl.pallas_call(
        functools.partial(widen_kernel, tuple(places)),
        out_shape=[jax.ShapeDtypeStruct((CH, WD * count) if kind == "cols" else (CH * count, WD), F32) for kind, count in pieces],
        in_specs=[hbm],
        out_specs=[hbm] * len(pieces),
        scratch_shapes=[
            pltpu.VMEM((n, CH, WD), BF),
            pltpu.VMEM((n, CH, WD), F32),
            pltpu.SemaphoreType.DMA((n,)),
            pltpu.SemaphoreType.DMA((n,)),
        ],
        compiler_params=pltpu.CompilerParams(vmem_limit_bytes=60 << 20),
        cost_estimate=pl.CostEstimate(flops=0, bytes_accessed=6 * CH * WD * n, transcendentals=0),
        name="widen",
    )(summed)


def feed_kernel(x_ref, grad_ref, second_ref, down_bias, up_bias, up_ref, down_ref, hidden_ref, hidden_grad_ref, bias_grad_ref, block_ref, e_ref, acc):
    j = pl.program_id(0)

    @pl.when(j == 0)
    def _():
        acc[...] = jnp.zeros_like(acc)
        e_ref[...] = jnp.zeros_like(e_ref)

    step = 512
    total = jnp.zeros(bias_grad_ref.shape, F32)
    for k in range(x_ref.shape[0] // step):
        rows = pl.ds(k * step, step)
        before = dot_nn(x_ref[rows, :], up_ref[...]) + up_bias[...]
        change = dot_nt(grad_ref[rows, :], down_ref[...])
        below = 0.5 + 0.5 * lax.erf(before * math.sqrt(0.5))
        slope = below + before * jnp.exp(-0.5 * before * before) * (1.0 / math.sqrt(2.0 * math.pi))
        hidden = (before * below).astype(BF)
        hidden_grad = (change * slope).astype(BF)
        hidden_ref[rows, :] = hidden
        hidden_grad_ref[rows, :] = hidden_grad
        total = total + jnp.sum(hidden_grad.astype(F32), axis=0, keepdims=True)
        acc[rows, :] += dot_nn(hidden, down_ref[...])
        e_ref[rows, :] += dot_nt(hidden_grad, up_ref[...])
    bias_grad_ref[...] = total

    @pl.when(j == pl.num_programs(0) - 1)
    def _():
        block_ref[...] = (second_ref[...] + acc[...] + down_bias[...]).astype(BF)


def feed(x, grad, second, up, up_bias, down, down_bias):
    n, d = x.shape
    width, tile = up.shape[1], 512
    whole = lambda shape: pl.BlockSpec(shape, lambda j: (0, 0))
    column = lambda rows: pl.BlockSpec((rows, tile), lambda j: (0, j))
    return pl.pallas_call(
        feed_kernel,
        grid=(width // tile,),
        out_shape=(
            jax.ShapeDtypeStruct((n, width), BF),
            jax.ShapeDtypeStruct((n, width), BF),
            jax.ShapeDtypeStruct((1, width), F32),
            jax.ShapeDtypeStruct((n, d), BF),
            jax.ShapeDtypeStruct((n, d), F32),
        ),
        in_specs=[whole((n, d))] * 3 + [whole((1, d)), column(1), column(d), pl.BlockSpec((tile, d), lambda j: (j, 0))],
        out_specs=(column(n), column(n), column(1), whole((n, d)), whole((n, d))),
        scratch_shapes=[pltpu.VMEM((n, d), F32)],
        compiler_params=pltpu.CompilerParams(vmem_limit_bytes=48 << 20),
        cost_estimate=pl.CostEstimate(flops=16 * n * d * width, bytes_accessed=4 * d * width, transcendentals=2 * n * width),
        name="feed",
    )(x, grad, second, down_bias.reshape(1, d), up_bias.reshape(1, width), up, down)


TOKEN_PARTS = 4


def spread_kernel(n_mats, *refs):
    tok, seg = refs[:2]
    mats = refs[2 : 2 + n_mats]
    tok_all, seg_all = refs[2 + n_mats : 4 + n_mats]
    fulls = refs[4 + n_mats : 4 + 2 * n_mats]
    stage = refs[4 + 2 * n_mats : 4 + 3 * n_mats]
    tok_stage, seg_stage = refs[4 + 3 * n_mats : 6 + 3 * n_mats]
    (mat_load, mat_put, mat_send, mat_recv, own_load, own_put, far_send, far_recv, sib_send, sib_recv, near_send, near_recv, pass_send, pass_recv) = refs[6 + 3 * n_mats :]
    sib, near, diag, far, block, near_block, sib_block, diag_block, home = pair_places()
    _, _, z, c = coords()
    greet((sib, near, far))
    rows = tok.shape[0]
    part = rows // TOKEN_PARTS
    n_items = TOKEN_PARTS + 1

    def source(k):
        return seg if k == TOKEN_PARTS else tok.at[pl.ds(k * part, part), :]

    def place(k, b):
        if k == TOKEN_PARTS:
            return seg_all.at[b]
        return tok_all.at[pl.ds(pl.multiple_of(b * rows + k * part, part), part), :]

    def remote(src, dst, send, recv, device):
        return pltpu.make_async_remote_copy(src_ref=src, dst_ref=dst, send_sem=send, recv_sem=recv, device_id=device, device_id_type=MESH)

    def far_copy(k):
        return remote(source(k), place(k, z), far_send.at[k], far_recv.at[k], far)

    def staged(k):
        return seg_stage if k == TOKEN_PARTS else tok_stage.at[pl.ds(k * part, part), :]

    def own_copy(k):
        return pltpu.make_async_copy(source(k), staged(k), own_load.at[k])

    def own_out(k):
        return pltpu.make_async_copy(staged(k), place(k, block), own_put.at[k])

    def sib_copy(k):
        return remote(place(k, block), place(k, block), sib_send.at[k], sib_recv.at[k], sib)

    def near_copy(k):
        return remote(place(k, block), place(k, block), near_send.at[k], near_recv.at[k], near)

    def pass_copy(k):
        return remote(place(k, near_block), place(k, near_block), pass_send.at[k], pass_recv.at[k], sib)

    @pl.when(home)
    def _():
        for k in range(n_items):
            own_copy(k).start()

    @pl.when(jnp.logical_not(home))
    def _():
        for k in range(n_items):
            far_copy(k).start()

    def mat_target(i):
        half = mats[i].shape[0]
        return fulls[i].at[pl.ds(pl.multiple_of(c * half, 8), half), :]

    def mat_in(i):
        return pltpu.make_async_copy(mats[i], stage[i], mat_load.at[i])

    def mat_out(i):
        return pltpu.make_async_copy(stage[i], mat_target(i), mat_put.at[i])

    def mat_remote(i):
        return remote(mats[i], mat_target(i), mat_send.at[i], mat_recv.at[i], sib)

    for i in range(n_mats):
        mat_in(i).start()
        mat_remote(i).start()

    for k in range(n_items + 1):
        if k < n_items:

            @pl.when(home)
            def _():
                own_copy(k).wait()
                own_out(k).start()
                own_out(k).wait()

            @pl.when(jnp.logical_not(home))
            def _():
                far_copy(k).wait()

            sib_copy(k).start()
            near_copy(k).start()
        if k > 0:
            near_copy(k - 1).wait()
            pass_copy(k - 1).start()
    for i in range(n_mats):
        mat_in(i).wait()
        mat_out(i).start()
    for k in range(n_items):
        sib_copy(k).wait()
        pass_copy(k).wait()
    for i in range(n_mats):
        mat_out(i).wait()
        mat_remote(i).wait()


def spread(tokens, seg, mats):
    n = len(mats)
    any_spec = pl.BlockSpec(memory_space=pltpu.HBM)
    dma = pltpu.SemaphoreType.DMA
    items = TOKEN_PARTS + 1
    return pl.pallas_call(
        functools.partial(spread_kernel, n),
        out_shape=[
            jax.ShapeDtypeStruct((4 * tokens.shape[0], tokens.shape[1]), tokens.dtype),
            jax.ShapeDtypeStruct((4,) + seg.shape, seg.dtype),
        ]
        + [jax.ShapeDtypeStruct((2 * m.shape[0], m.shape[1]), m.dtype) for m in mats],
        in_specs=[any_spec] * (2 + n),
        out_specs=[any_spec] * (2 + n),
        scratch_shapes=[pltpu.VMEM(a.shape, a.dtype) for a in (*mats, tokens, seg)] + [dma((n,))] * 4 + [dma((items,))] * 10,
        compiler_params=pltpu.CompilerParams(collective_id=2, has_side_effects=True, vmem_limit_bytes=60 << 20),
        cost_estimate=pl.CostEstimate(flops=0, bytes_accessed=64 << 20, transcendentals=0),
        name="spread",
    )(tokens, seg, *mats)


def project_kernel(scale, block_ref, tok, gain, shift, wq, wk, wv, bq, bv, q_ref, k_ref, v_ref):
    del block_ref
    normed = norm_rows(tok[...].astype(F32), gain[...], shift[...]).astype(BF)
    q_ref[...] = ((product(normed, wq[...]) + bq[...]) * scale).astype(BF)
    k_ref[...] = product(normed, wk[...]).astype(BF)
    v_ref[...] = (product(normed, wv[...]) + bv[...]).astype(BF)


def project(block, tokens_all, gain, shift, weights, query_bias, value_bias, scale):
    n, d = tokens_all.shape
    width, step = d // 4, 512
    row = lambda i, b: (i, 0)
    fixed = lambda i, b: (0, 0)
    weight = lambda part: pl.BlockSpec((d, width), lambda i, b: (0, 4 * part + b[0]))
    return pl.pallas_call(
        functools.partial(project_kernel, scale),
        grid_spec=pltpu.PrefetchScalarGridSpec(
            num_scalar_prefetch=1,
            grid=(n // step,),
            in_specs=[pl.BlockSpec((step, d), row), pl.BlockSpec((1, d), fixed), pl.BlockSpec((1, d), fixed)]
            + [weight(part) for part in range(3)]
            + [pl.BlockSpec((1, width), lambda i, b: (0, b[0]))] * 2,
            out_specs=[pl.BlockSpec((step, width), row)] * 3,
        ),
        out_shape=[jax.ShapeDtypeStruct((n, width), BF)] * 3,
        compiler_params=pltpu.CompilerParams(vmem_limit_bytes=60 << 20),
        cost_estimate=pl.CostEstimate(flops=6 * n * d * width, bytes_accessed=4 * n * d, transcendentals=0),
        name="project",
    )(block.reshape(1).astype(jnp.int32), tokens_all, gain.reshape(1, d), shift.reshape(1, d), weights, weights, weights,
      query_bias.reshape(1, d), value_bias.reshape(1, d))


def owner_of(z, c):
    return (z, c) if z // 2 == c else ((z + 2) % 4, 1 - c)


def flat(z, c):
    return 2 * z + c


CORES = [(z, c) for z in range(4) for c in range(2)]
SWAP = [(flat(z, c), flat(*owner_of(z, c))) for z, c in CORES if owner_of(z, c) != (z, c)]
HOME_TO_NEAR = [(flat(z, c), flat(owner_of(z, c)[0] ^ 1, owner_of(z, c)[1])) for z, c in CORES]
SIB = [(0, 1), (1, 0)]


def is_home():
    return lax.div(lax.axis_index("ctx"), 2) == lax.axis_index("shard")


def swap(array):
    return jnp.where(is_home(), array, lax.ppermute(array, ("ctx", "shard"), SWAP))


VECTORS = (0, 1, 3, 4, 6, 7, 8, 10, 12, 14, 15, 16, 18, 20)
MATRICES = (17, 19, 13, 9, 5, 11, 2)


def pair_device(
    tokens, source, segment_ids, positions, cotangent,
    self_gain, self_shift, self_weights, query_bias, value_bias, self_output, output_bias,
    cross_gain, cross_shift, cross_query, query_offset, cross_memory, memory_offset, cross_output, return_bias,
    feed_gain, feed_shift, feed_up, up_bias, feed_down, down_bias,
):
    c, z = lax.axis_index("shard"), lax.axis_index("ctx")
    block = 2 * c + lax.rem(z, 2)
    head_scale = 1.0 / math.sqrt(HEAD_DIM)
    rows = tokens.shape[1]
    vectors = (
        self_gain, self_shift, query_bias, value_bias, output_bias, cross_gain, cross_shift, query_offset, memory_offset,
        return_bias, feed_gain, feed_shift, down_bias, up_bias,
    )
    half = D // 2
    n_packed = sum(v.shape[0] for v in vectors) // half
    packed_rows = n_packed + -n_packed % 16
    packed, at = jnp.zeros((packed_rows * half,), F32), 0
    for v in vectors:
        packed = packed + jnp.pad(v.astype(F32), (at, packed_rows * half - at - v.shape[0]))
        at += v.shape[0]
    packed = packed.astype(BF).reshape(packed_rows, half)
    mats = (self_weights, self_output, cross_memory, cross_query, cross_output, feed_up, feed_down, packed)
    spread_out = spread(tokens[0], segment_ids.reshape(4, rows // 4), mats)
    tokens_all, seg_all = spread_out[:2]
    self_weights, self_output, cross_memory, cross_query, cross_output, feed_up, feed_down, packed = spread_out[2:]
    tokens_all, source_home = lax.optimization_barrier((tokens_all, source[0]))
    own_source = swap(source_home)
    near_source = lax.ppermute(source_home, ("ctx", "shard"), HOME_TO_NEAR)
    chip_source = jnp.concatenate([own_source, near_source], axis=0)
    source_all = lax.optimization_barrier(jnp.concatenate([chip_source, lax.ppermute(chip_source, "shard", SIB)], axis=0))
    packed = packed.astype(F32).reshape(2, -1, half)
    unpacked = [packed[:, i].reshape(D) for i in range(13)]
    (
        self_gain, self_shift, query_bias, value_bias, output_bias, cross_gain, cross_shift, query_offset, memory_offset,
        return_bias, feed_gain, feed_shift, down_bias,
    ) = unpacked
    up_bias = packed[:, 13:n_packed].reshape(-1)
    seg = seg_all.reshape(-1)

    width = D // 4
    q, k, v = project(block, tokens_all, self_gain, self_shift, self_weights, query_bias, value_bias, head_scale)
    mix_heads, lse_self, mixed_self = attention_forward(q, k, v, seg)
    mixed_self, out_grad_home = lax.optimization_barrier((mixed_self, cotangent[0]))
    out_grad_far = lax.ppermute(out_grad_home, ("ctx", "shard"), SWAP)

    tok_low = lax.dynamic_slice_in_dim(tokens_all, block * rows, rows, 0)
    tok_rows = tok_low.astype(F32)
    normed_self = norm_rows(tok_rows, self_gain, self_shift).astype(BF)
    first_sum = tok_rows + product(mixed_self, self_output) + output_bias
    normed_cross = norm_rows(first_sum, cross_gain, cross_shift).astype(BF)
    cross_q = ((product(normed_cross, cross_query) + query_offset) * head_scale).astype(BF)
    memory = product(source_all, cross_memory)
    cross_keys = memory[:, :D].astype(BF)
    cross_values = (memory[:, D:] + memory_offset).astype(BF)
    mixed_cross, lse_cross = attention_forward(cross_q, cross_keys, cross_values)
    mixed_cross, out_grad_far = lax.optimization_barrier((mixed_cross, out_grad_far))
    out_grad = jnp.where(is_home(), out_grad_home, out_grad_far)
    second = first_sum + product(mixed_cross, cross_output) + return_bias
    normed_feed = norm_rows(second, feed_gain, feed_shift).astype(BF)
    hidden, hidden_grad, up_bias_grad, block_output, feed_e = feed(
        normed_feed, out_grad, second, feed_up, up_bias, feed_down, down_bias
    )
    up_bias_grad = up_bias_grad.reshape(-1)
    down_bias_grad = jnp.sum(out_grad, axis=0, dtype=F32)
    _, feed_pull = jax.vjp(norm_rows, second, feed_gain, feed_shift)
    second_part, feed_gain_grad, feed_shift_grad = feed_pull(feed_e)
    second_grad = out_grad.astype(F32) + second_part
    branch_cross = second_grad.astype(BF)
    return_bias_grad = jnp.sum(second_grad, axis=0)
    mixed_cross_grad = right_product(branch_cross, cross_output).astype(BF)
    unknown = jnp.zeros((D,), F32)
    vectors = (unknown,) * 9 + (return_bias_grad, feed_gain_grad, feed_shift_grad, up_bias_grad, down_bias_grad)
    small = jnp.concatenate([v.reshape(-1, D) for v in vectors], axis=0)
    small = jnp.pad(small, ((0, -small.shape[0] % 8), (0, 0)))
    sources = (normed_feed, hidden_grad, hidden, out_grad, mixed_cross, branch_cross, normed_cross, mixed_self, normed_self, source_all)
    made = len(sources)
    chunks = feed_up.shape[1] // D
    plan = (
        tuple((0, "cols", 0, 1, i) for i in range(chunks))
        + tuple((2, "rows", i, 3, 0) for i in range(chunks))
        + ((4, "cols", 0, 5, 0), (6, "cols", 0, made, 0), (7, "cols", 0, made + 1, 0))
        + ((9, "cols", 0, made + 2, 0), (9, "cols", 0, made + 3, 0))
        + tuple((8, "cols", 0, made + 4, i) for i in range(3))
    )
    pieces = (("cols", chunks), ("rows", chunks), ("cols", 1), ("cols", 1), ("cols", 1), ("cols", 2), ("cols", 3))
    summed, small_sum, tokens_grad, block_home, source_grad, *_ = finish_backward(
        plan,
        (q, k, v, mix_heads, lse_self.reshape(8, -1), seg),
        (cross_q, cross_keys, cross_values, mixed_cross, mixed_cross_grad, lse_cross),
        (self_gain, cross_gain),
        small,
        sources,
        (tok_low, block_output, first_sum, second_grad),
        (self_weights, cross_memory, cross_query, self_output),
    )
    results = {}
    for place, matrix in zip(MATRICES, widen(summed, pieces)):
        results[place] = matrix
    at = 0
    for place, v in zip(VECTORS, vectors):
        rows_of, size = v.shape[0] // D, v.shape[0]
        results[place] = lax.dynamic_slice_in_dim(small_sum[at : at + rows_of].reshape(size), c * (size // 2), size // 2, 0)
        at += rows_of
    return (
        block_home[None],
        tokens_grad.astype(F32)[None],
        source_grad.astype(F32)[None],
    ) + tuple(results[place] for place in sorted(results))


def per_device(
    tokens,
    source,
    segment_ids,
    positions,
    cotangent,
    self_gain,
    self_shift,
    self_weights,
    query_bias,
    value_bias,
    self_output,
    output_bias,
    cross_gain,
    cross_shift,
    cross_query,
    query_offset,
    cross_memory,
    memory_offset,
    cross_output,
    return_bias,
    feed_gain,
    feed_shift,
    feed_up,
    up_bias,
    feed_down,
    down_bias,
):
    (
        self_gain,
        self_shift,
        self_weights,
        query_bias,
        value_bias,
        self_output,
        output_bias,
        cross_gain,
        cross_shift,
        cross_query,
        query_offset,
        cross_memory,
        memory_offset,
        cross_output,
        return_bias,
        feed_gain,
        feed_shift,
        feed_up,
        up_bias,
        feed_down,
        down_bias,
    ) = (
        lax.all_gather(self_gain, "shard", axis=0, tiled=True),
        lax.all_gather(self_shift, "shard", axis=0, tiled=True),
        lax.all_gather(self_weights, "shard", axis=0, tiled=True),
        lax.all_gather(query_bias, "shard", axis=0, tiled=True),
        lax.all_gather(value_bias, "shard", axis=0, tiled=True),
        lax.all_gather(self_output, "shard", axis=0, tiled=True),
        lax.all_gather(output_bias, "shard", axis=0, tiled=True),
        lax.all_gather(cross_gain, "shard", axis=0, tiled=True),
        lax.all_gather(cross_shift, "shard", axis=0, tiled=True),
        lax.all_gather(cross_query, "shard", axis=0, tiled=True),
        lax.all_gather(query_offset, "shard", axis=0, tiled=True),
        lax.all_gather(cross_memory, "shard", axis=0, tiled=True),
        lax.all_gather(memory_offset, "shard", axis=0, tiled=True),
        lax.all_gather(cross_output, "shard", axis=0, tiled=True),
        lax.all_gather(return_bias, "shard", axis=0, tiled=True),
        lax.all_gather(feed_gain, "shard", axis=0, tiled=True),
        lax.all_gather(feed_shift, "shard", axis=0, tiled=True),
        lax.all_gather(feed_up, "shard", axis=0, tiled=True),
        lax.all_gather(up_bias, "shard", axis=0, tiled=True),
        lax.all_gather(feed_down, "shard", axis=0, tiled=True),
        lax.all_gather(down_bias, "shard", axis=0, tiled=True),
    )
    head_scale = 1.0 / math.sqrt(HEAD_DIM)
    row_count = tokens.shape[1]
    tok_rows = tokens[0].astype(jnp.float32)
    source_rows = source[0]
    tag_seg, tag_pos = (
        lax.all_gather(segment_ids, "ctx", axis=1, tiled=True),
        lax.all_gather(positions, "ctx", axis=1, tiled=True),
    )
    tag_bundle = (segment_ids[0], positions[0], tag_seg[0], tag_pos[0])
    gain_self = self_gain.astype(jnp.float32)
    shift_self = self_shift.astype(jnp.float32)
    normed_self = norm_rows(tok_rows, gain_self, shift_self).astype(jnp.bfloat16)
    projected = product(normed_self, self_weights)
    queries = ((projected[:, :D] + query_bias.astype(jnp.float32)) * head_scale).astype(
        jnp.bfloat16
    )
    keys_self = projected[:, D : 2 * D].astype(jnp.bfloat16)
    values_self = (projected[:, 2 * D :] + value_bias.astype(jnp.float32)).astype(jnp.bfloat16)
    query_heads = heads_of(queries)
    start_state = (
        jnp.full((HEADS, row_count), NEGATIVE, jnp.float32),
        jnp.zeros((HEADS, row_count), jnp.float32),
        jnp.zeros((row_count, HEADS, HEAD_DIM), jnp.float32),
    )
    folded_self = attend_piece(
        start_state,
        query_heads,
        lax.all_gather(keys_self, "ctx", axis=0, tiled=True),
        lax.all_gather(values_self, "ctx", axis=0, tiled=True),
        tag_bundle,
    )
    attended_self, total_self = finish(folded_self)
    mixed_self = attended_self.reshape(row_count, D).astype(jnp.bfloat16)
    first_sum = tok_rows + product(mixed_self, self_output) + output_bias.astype(jnp.float32)
    gain_cross = cross_gain.astype(jnp.float32)
    shift_cross = cross_shift.astype(jnp.float32)
    normed_cross = norm_rows(first_sum, gain_cross, shift_cross).astype(jnp.bfloat16)
    cross_q = (
        (product(normed_cross, cross_query) + query_offset.astype(jnp.float32)) * head_scale
    ).astype(jnp.bfloat16)
    memory = product(source_rows, cross_memory)
    memory_keys = memory[:, :D].astype(jnp.bfloat16)
    memory_values = (memory[:, D:] + memory_offset.astype(jnp.float32)).astype(jnp.bfloat16)
    cross_keys, cross_values = (
        lax.all_gather(memory_keys, "ctx", axis=0, tiled=True),
        lax.all_gather(memory_values, "ctx", axis=0, tiled=True),
    )
    cross_heads = heads_of(cross_q)
    attended_cross, total_cross = finish(
        attend_piece(start_state, cross_heads, cross_keys, cross_values, None)
    )
    mixed_cross = attended_cross.reshape(row_count, D).astype(jnp.bfloat16)
    second = first_sum + product(mixed_cross, cross_output) + return_bias.astype(jnp.float32)
    gain_feed = feed_gain.astype(jnp.float32)
    shift_feed = feed_shift.astype(jnp.float32)
    normed_feed = norm_rows(second, gain_feed, shift_feed).astype(jnp.bfloat16)
    hidden_pre = product(normed_feed, feed_up) + up_bias.astype(jnp.float32)
    hidden_act, gelu_pull = jax.vjp(exact_gelu, hidden_pre)
    hidden = hidden_act.astype(jnp.bfloat16)
    block_output = (second + product(hidden, feed_down) + down_bias.astype(jnp.float32)).astype(
        jnp.bfloat16
    )
    out_grad = cotangent[0]
    down_grad = left_product(hidden, out_grad)
    down_bias_grad = jnp.sum(out_grad, axis=0, dtype=jnp.float32)
    (hidden_grad,) = gelu_pull(right_product(out_grad, feed_down))
    hidden_grad = hidden_grad.astype(jnp.bfloat16)
    up_grad = left_product(normed_feed, hidden_grad)
    up_bias_grad = jnp.sum(hidden_grad, axis=0, dtype=jnp.float32)
    norm_value, feed_pull = jax.vjp(norm_rows, second, gain_feed, shift_feed)
    second_part, feed_gain_grad, feed_shift_grad = feed_pull(right_product(hidden_grad, feed_up))
    second_grad = out_grad.astype(jnp.float32) + second_part
    branch_cross = second_grad.astype(jnp.bfloat16)
    cross_output_grad = left_product(mixed_cross, branch_cross)
    return_bias_grad = jnp.sum(second_grad, axis=0)
    mixed_cross_grad = right_product(branch_cross, cross_output).astype(jnp.bfloat16)
    cross_grad_heads = heads_of(mixed_cross_grad)
    cross_delta = row_deltas(cross_grad_heads, attended_cross)
    cross_sum, key_terms, value_terms = attend_back(
        cross_heads, cross_keys, cross_values, cross_grad_heads, cross_delta, total_cross, None
    )
    key_part, value_part = (
        lax.psum_scatter(
            key_terms.astype(jnp.bfloat16), "ctx", scatter_dimension=0, tiled=True
        ).astype(jnp.float32),
        lax.psum_scatter(
            value_terms.astype(jnp.bfloat16), "ctx", scatter_dimension=0, tiled=True
        ).astype(jnp.float32),
    )
    memory_grad = jnp.concatenate(
        [key_part.astype(jnp.bfloat16), value_part.astype(jnp.bfloat16)], axis=1
    )
    source_grad = right_product(memory_grad, cross_memory)
    cross_memory_grad = left_product(source_rows, memory_grad)
    memory_offset_grad = jnp.sum(memory_grad[:, D:], axis=0, dtype=jnp.float32)
    cross_q_grad = cross_sum.astype(jnp.bfloat16) * head_scale
    cross_query_grad = left_product(normed_cross, cross_q_grad)
    query_offset_grad = jnp.sum(cross_q_grad, axis=0, dtype=jnp.float32)
    norm_value, cross_pull = jax.vjp(norm_rows, first_sum, gain_cross, shift_cross)
    first_part, cross_gain_grad, cross_shift_grad = cross_pull(
        right_product(cross_q_grad, cross_query)
    )
    first_grad = second_grad + first_part
    branch_self = first_grad.astype(jnp.bfloat16)
    self_output_grad = left_product(mixed_self, branch_self)
    output_bias_grad = jnp.sum(first_grad, axis=0)
    mixed_self_grad = right_product(branch_self, self_output).astype(jnp.bfloat16)
    keys_back, values_back = (
        lax.all_gather(keys_self, "ctx", axis=0, tiled=True),
        lax.all_gather(values_self, "ctx", axis=0, tiled=True),
    )
    self_grad_heads = heads_of(mixed_self_grad)
    self_delta = row_deltas(self_grad_heads, attended_self)
    query_sum, key_terms_self, value_terms_self = attend_back(
        query_heads, keys_back, values_back, self_grad_heads, self_delta, total_self, tag_bundle
    )
    key_own, value_own = (
        lax.psum_scatter(
            key_terms_self.astype(jnp.bfloat16), "ctx", scatter_dimension=0, tiled=True
        ).astype(jnp.float32),
        lax.psum_scatter(
            value_terms_self.astype(jnp.bfloat16), "ctx", scatter_dimension=0, tiled=True
        ).astype(jnp.float32),
    )
    query_grad = query_sum.astype(jnp.bfloat16) * head_scale
    value_grad = value_own.astype(jnp.bfloat16)
    projected_grad = jnp.concatenate([query_grad, key_own.astype(jnp.bfloat16), value_grad], axis=1)
    self_weights_grad = left_product(normed_self, projected_grad)
    query_bias_grad = jnp.sum(query_grad, axis=0, dtype=jnp.float32)
    value_bias_grad = jnp.sum(value_grad, axis=0, dtype=jnp.float32)
    norm_value, self_pull = jax.vjp(norm_rows, tok_rows, gain_self, shift_self)
    token_part, self_gain_grad, self_shift_grad = self_pull(
        right_product(projected_grad, self_weights)
    )
    tokens_grad = first_grad + token_part
    gradients = (
        self_gain_grad,
        self_shift_grad,
        self_weights_grad,
        query_bias_grad,
        value_bias_grad,
        self_output_grad,
        output_bias_grad,
        cross_gain_grad,
        cross_shift_grad,
        cross_query_grad,
        query_offset_grad,
        cross_memory_grad,
        memory_offset_grad,
        cross_output_grad,
        return_bias_grad,
        feed_gain_grad,
        feed_shift_grad,
        up_grad,
        up_bias_grad,
        down_grad,
        down_bias_grad,
    )
    halves = [lax.psum_scatter(g.astype(BF), "shard", scatter_dimension=0, tiled=True).astype(F32) for g in gradients]
    reduced = lax.psum(tuple(halves), ("group", "ctx"))
    return (block_output[None], tokens_grad[None], source_grad[None]) + tuple(reduced)


def solution(mesh):
    near = (mesh.shape["group"], mesh.shape["ctx"], mesh.shape["shard"]) == (4, 4, 2)
    placed = (
        P(("group", "shard"), "ctx", None),
        P(("group", "shard"), "ctx", None),
        P(("group", "shard"), "ctx"),
        P(("group", "shard"), "ctx"),
        P(("group", "shard"), "ctx", None),
        P("shard"),
        P("shard"),
        P("shard", None),
        P("shard"),
        P("shard"),
        P("shard", None),
        P("shard"),
        P("shard"),
        P("shard"),
        P("shard", None),
        P("shard"),
        P("shard", None),
        P("shard"),
        P("shard", None),
        P("shard"),
        P("shard"),
        P("shard"),
        P("shard", None),
        P("shard"),
        P("shard", None),
        P("shard"),
    )
    return jax.shard_map(
        pair_device if near else per_device,
        mesh=mesh,
        in_specs=placed,
        out_specs=(
            P(("group", "shard"), "ctx", None),
            P(("group", "shard"), "ctx", None),
            P(("group", "shard"), "ctx", None),
            P("shard"),
            P("shard"),
            P("shard", None),
            P("shard"),
            P("shard"),
            P("shard", None),
            P("shard"),
            P("shard"),
            P("shard"),
            P("shard", None),
            P("shard"),
            P("shard", None),
            P("shard"),
            P("shard", None),
            P("shard"),
            P("shard"),
            P("shard"),
            P("shard", None),
            P("shard"),
            P("shard", None),
            P("shard"),
        ),
        check_vma=False,
    )
```
